32 devices in a mesh: dp: 4 (over y, x), ctx: 2 (over core), tensor: 4 (over z).
Axes of the slice: x: 2, y: 2, z: 4, core: 2. Of those that a mesh axis runs over, the one named last changes fastest.
Arguments:
- tokens: bfloat16 [4, 4096, 1024], P('dp', ('ctx', 'tensor')), may hold values from -6 to 6
- segments: int32 [4, 4096], P('dp'), may hold values from 0 to 3, never falling along the last dimension, each value on 1 to 3072 neighbouring positions
- adapter_of: int32 [4], replicated, may hold values from 0 to 7, as said below
- cotangent: bfloat16 [4, 4096, 1024], P('dp', ('ctx', 'tensor')), may hold values from -6 to 6
- first_gain: bfloat16 [1024], replicated, may hold values from 0.099609375 to 1.8984375
- second_gain: bfloat16 [1024], replicated, may hold values from 0.099609375 to 1.8984375
- conv_taps: bfloat16 [3, 1024], P(None, 'tensor'), may hold values from -3.5 to 3.5
- entry_weight: bfloat16 [3, 1024, 1024], P(None, 'dp', 'tensor'), may hold values from -0.1875 to 0.1875
- mixer_weight: bfloat16 [1024, 1024], P('tensor', 'dp'), may hold values from -0.1875 to 0.1875
- gates_weight: bfloat16 [2, 1024, 4608], P(None, 'dp', 'tensor'), may hold values from -0.1875 to 0.1875
- outlet_weight: bfloat16 [4608, 1024], P('tensor', 'dp'), may hold values from -0.09375 to 0.09375
- entry_reduce: bfloat16 [8, 16, 1024], replicated, may hold values from -0.1875 to 0.1875
- entry_expand: bfloat16 [8, 16, 3, 1024], P(None, None, None, 'tensor'), may hold values from -0.75 to 0.75
- mixer_reduce: bfloat16 [8, 16, 1024], P(None, None, 'tensor'), may hold values from -0.1875 to 0.1875
- mixer_expand: bfloat16 [8, 16, 1024], replicated, may hold values from -0.75 to 0.75
- gates_reduce: bfloat16 [2, 8, 16, 1024], replicated, may hold values from -0.1875 to 0.1875
- gates_expand: bfloat16 [2, 8, 16, 4608], P(None, None, None, 'tensor'), may hold values from -0.75 to 0.75
- outlet_reduce: bfloat16 [8, 16, 4608], P(None, None, 'tensor'), may hold values from -0.09375 to 0.09375
- outlet_expand: bfloat16 [8, 16, 1024], replicated, may hold values from -0.75 to 0.75
Outputs:
- output: bfloat16 [4, 4096, 1024], P('dp', ('ctx', 'tensor'))
- input_grad: bfloat16 [4, 4096, 1024], P('dp', ('ctx', 'tensor'))
- grad_entry_reduce: float32 [8, 16, 1024], replicated
- grad_entry_expand: float32 [8, 16, 3, 1024], P(None, None, None, 'tensor')
- grad_mixer_reduce: float32 [8, 16, 1024], P(None, None, 'tensor')
- grad_mixer_expand: float32 [8, 16, 1024], replicated
- grad_gates_reduce: float32 [2, 8, 16, 1024], replicated
- grad_gates_expand: float32 [2, 8, 16, 4608], P(None, None, None, 'tensor')
- grad_outlet_reduce: float32 [8, 16, 4608], P(None, None, 'tensor')
- grad_outlet_expand: float32 [8, 16, 1024], replicated
The draws below stay inside these ranges and needn't reach their ends.
Inputs may be any that keep to these rules, and one draw needn't show every extreme that they name: `adapter_of`: when there are at least as many sequences as adapters, each adapter serves exactly 0 sequences; otherwise each adapter serves at most one. `segments`: within a sequence document numbers never fall; there are 4 documents of 1 to 3072 positions.
All inputs are finite; a program needn't handle non-finite values.
Results may differ from the reference program's by a relative error of at most 0.014.
Values may be sent and summed in bfloat16 or wider, within the bound.
No kernel may reach another device: no remote copies, remote signals or barrier semaphores. Data moves between devices by JAX's collectives and lax.ppermute only.
A program may use at most 192 MiB of HBM per device.

```python
import math
import jax
import jax.numpy as jnp
import numpy as np
from jax import lax

D = 1024
FF = 4608
RANK = 16
ADAPTERS = 8
DOCS = 4
SEQS = 4
SEQLEN = 4096


def draw_adapter_of(key, part):
    pool_size = max(SEQS, ADAPTERS)
    shuffled = jax.random.permutation(key, pool_size)[:SEQS]
    return (shuffled % ADAPTERS).astype(jnp.int32)


def steps_of(rng, extent, split, least, high):
    factor_of, own = 1.0, jax.random.fold_in(rng, 6)
    for dim, parts in split:
        heights = jnp.exp(jax.random.uniform(jax.random.fold_in(own, dim), (parts,), jnp.float32, least / len(split), high / len(split)))
        factor_of = factor_of * jnp.repeat(heights, extent[dim] // parts).reshape([-1 if axis == dim else 1 for axis in range(len(extent))])
    return factor_of


def split_up(amount, total, reach, skew):
    loads = [(1 << 20) // math.isqrt(grade ** skew) + 1 for grade in range(2, amount + 1)]
    spare, holding = total - reach - (amount - 1), [1] * (amount - 1)
    while spare > 0:
        movable = [i for i in range(amount - 1) if holding[i] < reach]
        whole, left = sum([loads[i] for i in movable]), spare
        for i in movable:
            addition = min(reach - holding[i], max(1, left * loads[i] // whole), spare)
            holding[i] = holding[i] + addition
            spare = spare - addition
    return np.array([reach] + holding)


def ragged_sizes(key, number_of, total, limit, slope):
    if number_of == 2:
        one = jax.random.randint(key, (), max(1, total - limit), min(limit, total - 1) + 1)
        return jnp.stack([one, total - one])
    tallies = jnp.asarray(split_up(number_of, total, limit, slope), jnp.int32)
    twos = (number_of - 1) // 2
    source_of, receiver = tallies[1:1 + 2 * twos:2], tallies[2:2 + 2 * twos:2]
    margin = jnp.minimum(source_of - 1, limit - receiver)
    passed = jax.random.randint(jax.random.fold_in(key, 1), (twos,), 0, 1 << 20) % (margin + 1)
    tallies = tallies.at[1:1 + 2 * twos:2].set(source_of - passed).at[2:2 + 2 * twos:2].set(receiver + passed)
    return tallies[jax.random.permutation(jax.random.fold_in(key, 2), number_of)]


def centred(own_key, dims, spread, limit, pieces=(), dtype=jnp.bfloat16):
    level = steps_of(own_key, dims, pieces, -0.22, 0.18) if pieces else 1.0
    drawn = jax.random.normal(own_key, dims, jnp.float32) * spread * level
    return jnp.minimum(jnp.maximum(drawn, -limit), limit).astype(dtype)


def setup_inputs(seed: int = 0) -> dict:
    keys = jax.random.split(jax.random.key(seed), 20)
    return {
        "tokens": centred(keys[0], (SEQS, SEQLEN, D), 1.0, 6.0, ((0, 4), (1, 8))),
        "segments": jax.vmap(lambda own: jnp.searchsorted(jnp.cumsum(ragged_sizes(own, DOCS, SEQLEN, 3 * SEQLEN // 4, 0)), jnp.arange(SEQLEN), side="right"))(jax.random.split(keys[1], SEQS)).reshape((SEQS, SEQLEN)).astype(jnp.int32),
        "adapter_of": draw_adapter_of(jax.random.fold_in(keys[19], 71), 0),
        "cotangent": centred(keys[3], (SEQS, SEQLEN, D), 1.0, 6.0, ((0, 4), (1, 8))),
        "first_gain": jnp.clip(1.0 + 0.18 * jax.random.normal(keys[4], (D,), jnp.float32), 0.099609375, 1.8984375).astype(jnp.bfloat16),
        "second_gain": jnp.clip(1.0 + 0.18 * jax.random.normal(keys[5], (D,), jnp.float32), 0.099609375, 1.8984375).astype(jnp.bfloat16),
        "conv_taps": centred(keys[6], (3, D), 3 ** -0.5, 3.5, ((1, 4),)),
        "entry_weight": centred(keys[7], (3, D, D), D ** -0.5, 0.1875, ((1, 4), (2, 4))),
        "mixer_weight": centred(keys[8], (D, D), D ** -0.5, 0.1875, ((0, 4), (1, 4))),
        "gates_weight": centred(keys[9], (2, D, FF), D ** -0.5, 0.1875, ((1, 4), (2, 4))),
        "outlet_weight": centred(keys[10], (FF, D), FF ** -0.5, 0.09375, ((0, 4), (1, 4))),
        "entry_reduce": centred(keys[11], (ADAPTERS, RANK, D), D ** -0.5, 0.1875),
        "entry_expand": centred(keys[12], (ADAPTERS, RANK, 3, D), (4 * RANK) ** -0.5, 0.75, ((3, 4),)),
        "mixer_reduce": centred(keys[13], (ADAPTERS, RANK, D), D ** -0.5, 0.1875, ((2, 4),)),
        "mixer_expand": centred(keys[14], (ADAPTERS, RANK, D), (4 * RANK) ** -0.5, 0.75),
        "gates_reduce": centred(keys[15], (2, ADAPTERS, RANK, D), D ** -0.5, 0.1875),
        "gates_expand": centred(keys[16], (2, ADAPTERS, RANK, FF), (4 * RANK) ** -0.5, 0.75, ((3, 4),)),
        "outlet_reduce": centred(keys[17], (ADAPTERS, RANK, FF), FF ** -0.5, 0.09375, ((2, 4),)),
        "outlet_expand": centred(keys[18], (ADAPTERS, RANK, D), (4 * RANK) ** -0.5, 0.75),
    }


EPSILON = 1e-05
HIGHEST = lax.Precision.HIGHEST

@jax.custom_vjp
def low(v):
    return lax.optimization_barrier(v.astype(jnp.bfloat16)).astype(jnp.float32)

@jax.custom_vjp
def low_back(v):
    return v

def low_keep(v):
    return (low(v), None)

def low_pass(kept, grad):
    return (grad,)

def back_keep(v):
    return (v, None)

def back_low(kept, grad):
    return (low(grad),)
low.defvjp(low_keep, low_pass)
low_back.defvjp(back_keep, back_low)

def matmul(first_op, second_op):
    return jnp.dot(first_op, second_op, precision=HIGHEST)

def normed(rows_in, gain_row):
    inverse = lax.rsqrt(lax.optimization_barrier(jnp.mean(rows_in * rows_in, axis=-1, keepdims=True)) + EPSILON)
    return rows_in * inverse * gain_row

def sequence_block(tokens, segment, adapter, params):
    first_gain, second_gain, conv_taps, entry_weight, mixer_weight, gates_weight, outlet_weight, entry_reduce, entry_expand, mixer_reduce, mixer_expand, gates_reduce, gates_expand, outlet_reduce, outlet_expand = params
    normed_in = low(normed(tokens, first_gain))
    entry_low = jnp.einsum('ld,rd->lr', normed_in, entry_reduce[adapter], precision=HIGHEST)
    projected = jnp.einsum('ld,kdc->klc', normed_in, entry_weight, precision=HIGHEST)
    projected = projected + jnp.einsum('lr,rkc->klc', entry_low, entry_expand[adapter], precision=HIGHEST)
    projected = low_back(projected)
    gate_b, gate_c, values = (projected[0], projected[1], projected[2])
    product = gate_b * values
    padded = jnp.pad(product, ((2, 0), (0, 0)))
    seg_pad = jnp.concatenate([jnp.full((2,), -1, jnp.int32), segment.astype(jnp.int32)])
    nearby = (seg_pad[1:-1] == seg_pad[2:]).astype(jnp.float32)[:, None]
    distant = (seg_pad[:-2] == seg_pad[2:]).astype(jnp.float32)[:, None]
    convolved = conv_taps[0] * product + conv_taps[1] * nearby * padded[1:-1] + conv_taps[2] * distant * padded[:-2]
    mixed_in = low(gate_c * convolved)
    mixer_low = jnp.einsum('lc,rc->lr', mixed_in, mixer_reduce[adapter], precision=HIGHEST)
    branch = low_back(matmul(mixed_in, mixer_weight) + matmul(mixer_low, mixer_expand[adapter]))
    middle = tokens + branch
    second_in = low(normed(middle, second_gain))
    gates_low = jnp.einsum('ld,krd->klr', second_in, gates_reduce[:, adapter], precision=HIGHEST)
    gate_up = jnp.einsum('ld,kdf->klf', second_in, gates_weight, precision=HIGHEST)
    gate_up = gate_up + jnp.einsum('klr,krf->klf', gates_low, gates_expand[:, adapter], precision=HIGHEST)
    gate_up = low_back(gate_up)
    hidden = low(jax.nn.silu(gate_up[0]) * gate_up[1])
    outlet_low = jnp.einsum('lf,rf->lr', hidden, outlet_reduce[adapter], precision=HIGHEST)
    feed_out = low_back(matmul(hidden, outlet_weight) + matmul(outlet_low, outlet_expand[adapter]))
    return middle + feed_out

def reference(tokens, segments, adapter_of, cotangent, first_gain, second_gain, conv_taps, entry_weight, mixer_weight, gates_weight, outlet_weight, entry_reduce, entry_expand, mixer_reduce, mixer_expand, gates_reduce, gates_expand, outlet_reduce, outlet_expand):
    params = tuple((weight.astype(jnp.float32) for weight in (first_gain, second_gain, conv_taps, entry_weight, mixer_weight, gates_weight, outlet_weight, entry_reduce, entry_expand, mixer_reduce, mixer_expand, gates_reduce, gates_expand, outlet_reduce, outlet_expand)))
    checked = jax.checkpoint(sequence_block)

    def forward(inputs, weights):

        def single(sample):
            return checked(sample[0], sample[1], sample[2], weights)
        return lax.map(single, (inputs, segments.astype(jnp.int32), adapter_of.astype(jnp.int32)))
    result, pullback = jax.vjp(forward, tokens.astype(jnp.float32), params)
    input_grad, param_grads = pullback(cotangent.astype(jnp.float32))
    return (result.astype(jnp.bfloat16), input_grad.astype(jnp.bfloat16), param_grads[7], param_grads[8], param_grads[9], param_grads[10], param_grads[11], param_grads[12], param_grads[13], param_grads[14])
```

```python
import functools

import jax
import jax.numpy as jnp
from jax import lax
from jax.experimental import pallas as pl
from jax.experimental.pallas import tpu as pltpu
from jax.sharding import PartitionSpec as P

EPSILON = 1e-05
FLOAT = jnp.float32
BRAIN = jnp.bfloat16
HALO = 16
LANES = 128
CHUNKS = 3
NN = ((1,), (0,))
NT = ((1,), (1,))
TN = ((0,), (0,))


def dot(a, b, dims=NN):
    return lax.dot_general(a, b, (dims, ((), ())), preferred_element_type=FLOAT)


def lanes(index):
    return pl.ds(pl.multiple_of(index * LANES, LANES), LANES)


def call(kernel, outs, n_any, n_smem, n_in, scratch, flops, nbytes):
    specs = [pl.BlockSpec(memory_space=pltpu.SMEM)] * n_smem
    specs += [pl.BlockSpec(memory_space=pltpu.VMEM)] * (n_in - n_smem - n_any)
    specs += [pl.BlockSpec(memory_space=pl.ANY)] * n_any
    return pl.pallas_call(
        kernel,
        out_shape=[jax.ShapeDtypeStruct(s, d) for s, d in outs],
        in_specs=specs,
        out_specs=[pl.BlockSpec(memory_space=pltpu.VMEM)] * len(outs),
        scratch_shapes=scratch,
        compiler_params=pltpu.CompilerParams(vmem_limit_bytes=52 << 20),
        cost_estimate=pl.CostEstimate(flops=flops, bytes_accessed=nbytes, transcendentals=0),
    )


def prep_kernel(tab, tok, halo, cot, gains, maps, trel, xin, crel, mrel, grel, elow, ob):
    t32 = tok[...].astype(FLOAT)
    inv = lax.rsqrt(jnp.mean(t32 * t32, axis=-1, keepdims=True) + EPSILON)
    h32 = halo[...].astype(FLOAT)
    hinv = lax.rsqrt(jnp.mean(h32 * h32, axis=-1, keepdims=True) + EPSILON)
    for r in range(tok.shape[1] // LANES):
        src = lanes(tab[r])
        dst = slice(r * LANES, (r + 1) * LANES)
        part = tok[:, src]
        gain = gains[:, src]
        trel[:, dst] = part
        xin[HALO:, dst] = (part.astype(FLOAT) * inv * gain[0:1]).astype(BRAIN)
        xin[:HALO, dst] = (halo[:, src].astype(FLOAT) * hinv * gain[0:1]).astype(BRAIN)
        crel[:, dst] = cot[:, src]
        mrel[:, dst] = maps[:, src]
        grel[:, dst] = gain
    rank = elow.shape[1]
    elow[...] = dot(xin[...], mrel[0:rank], NT).astype(BRAIN)
    ob[...] = dot(crel[...], mrel[4 * rank : 5 * rank], NT).astype(BRAIN)


def fetch(pieces, labels, w, sems, tiles, width, planes):
    sets = []
    for t in range(tiles):
        one = []
        for p, (ref, rows) in enumerate(zip(pieces, labels)):
            size = ref.shape[1]
            cols = pl.ds(t * width, width)
            one.append(
                pltpu.make_async_copy(
                    ref.at[planes, :, cols],
                    w.at[:, pl.ds(rows * LANES, size), cols],
                    sems.at[t, p],
                )
            )
        sets.append(one)
    for one in sets:
        for copy in one:
            copy.start()
    return sets


def front_kernel(labels, tiles, mask, xin, trel, mrel, grel, elow, emap, *rest):
    n = len(labels)
    pieces, rest = rest[:n], rest[n:]
    gb, gc, va, cv, mixed, mlow, middle, second, glow, w, sems = rest
    rank = elow.shape[1]
    rows = trel.shape[0]
    channels = w.shape[2]
    width = channels // tiles
    sets = fetch(pieces, labels, w, sems, tiles, width, slice(0, 4))
    near = mask[0:rows, 0:1]
    far = mask[0:rows, 1:2]
    branch = jnp.zeros((rows, w.shape[1]), FLOAT)
    low = jnp.zeros((rows, rank), FLOAT)
    for t in range(tiles):
        for copy in sets[t]:
            copy.wait()
        col = slice(t * width, (t + 1) * width)

        def project(k):
            wide = slice(k * channels + t * width, k * channels + (t + 1) * width)
            return dot(xin[...], w[k, :, col]) + dot(elow[...], emap[0:rank, wide])

        b = project(0)
        v = project(2)
        c = project(1)[HALO:]
        product = b * v
        gb[:, col] = b[HALO:].astype(BRAIN)
        va[:, col] = v[HALO:].astype(BRAIN)
        gc[:, col] = c.astype(BRAIN)
        taps = emap[rank : rank + 3, col].astype(FLOAT)
        conv = (
            taps[0:1] * product[HALO:]
            + taps[1:2] * near * pltpu.roll(product, 1, 0)[HALO:]
            + taps[2:3] * far * pltpu.roll(product, 2, 0)[HALO:]
        )
        cv[:, col] = conv.astype(BRAIN)
        mix = (c * conv).astype(BRAIN)
        mixed[:, col] = mix
        branch = branch + dot(mix, w[3, :, col], NT)
        low = low + dot(mix, emap[0:rank, 3 * channels + t * width : 3 * channels + (t + 1) * width], NT)
    low = low.astype(BRAIN)
    mlow[...] = low
    mid = trel[...].astype(FLOAT) + branch + dot(low, mrel[3 * rank : 4 * rank])
    middle[...] = mid
    inv = lax.rsqrt(jnp.mean(mid * mid, axis=-1, keepdims=True) + EPSILON)
    x2 = (mid * inv * grel[1:2]).astype(BRAIN)
    second[...] = x2
    glow[...] = dot(x2, mrel[rank : 3 * rank], NT).astype(BRAIN)


def feed_kernel(labels, tiles, first, second, crel, glow, ob, emap, *rest):
    if not first:
        out_in, grad_in, small_in = rest[:3]
        rest = rest[3:]
    n = len(labels)
    pieces, rest = rest[:n], rest[n:]
    out, grad, small, dmap, w, sems = rest
    rank = ob.shape[1]
    width = w.shape[2] // tiles
    sets = fetch(pieces, labels, w, sems, tiles, width, slice(0, 3))
    if first:
        out[...] = jnp.zeros_like(out)
        grad[...] = jnp.zeros_like(grad)
        small[...] = jnp.zeros_like(small)
    else:
        out[...] = out_in[...]
        grad[...] = grad_in[...]
        small[...] = small_in[...]
    for t in range(tiles):
        for copy in sets[t]:
            copy.wait()

    def step(t, carry):
        col = pl.ds(pl.multiple_of(t * width, LANES), width)
        eg, eu, ro = (emap[i * rank : (i + 1) * rank, col] for i in range(3))
        wg, wu, wo = (w[i, :, col] for i in range(3))
        x = second[...]
        g = dot(x, wg) + dot(glow[:, 0:rank], eg)
        u = dot(x, wu) + dot(glow[:, rank : 2 * rank], eu)
        h_grad = dot(crel[...], wo) + dot(ob[...], ro)
        sigma = 1.0 / (1.0 + jnp.exp(-g))
        act = g * sigma
        h = (act * u).astype(BRAIN)
        gg = (h_grad * u * (sigma * (1.0 + g * (1.0 - sigma)))).astype(BRAIN)
        ug = (h_grad * act).astype(BRAIN)
        out[...] += dot(h, wo, NT)
        grad[...] += dot(gg, wg, NT) + dot(ug, wu, NT)
        small[:, 0:rank] += dot(gg, eg, NT)
        small[:, rank : 2 * rank] += dot(ug, eu, NT)
        small[:, 2 * rank : 3 * rank] += dot(h, ro, NT)
        dmap[0:rank, col] = dot(glow[:, 0:rank], gg, TN)
        dmap[rank : 2 * rank, col] = dot(glow[:, rank : 2 * rank], ug, TN)
        dmap[2 * rank : 3 * rank, col] = dot(ob[...], h, TN)
        return carry

    lax.fori_loop(0, tiles, step, 0)


def pulled(v, gain, grad):
    inv = lax.rsqrt(jnp.mean(v * v, axis=-1, keepdims=True) + EPSILON)
    scaled = grad * gain
    along = jnp.mean(v * scaled, axis=-1, keepdims=True)
    return inv * scaled - v * (inv * inv * inv * along)


def middle_kernel(labels, tiles, turn, tab, out, grad, small, middle, second, crel, mrel, grel, mlow, mixed, gc, cv, emap, *rest):
    n = len(labels)
    pieces, rest = rest[:n], rest[n:]
    output, mgrad, cgrad, edge, gcg, wide_ff, wide_mix, dmix, w, sems = rest
    rank = mlow.shape[1]
    channels = w.shape[2]
    width = channels // tiles
    sets = fetch(pieces, labels, w, sems, tiles, width, slice(3, 4))
    blocks = w.shape[1] // LANES
    gback = small[:, 0 : 2 * rank].astype(BRAIN)
    olow = small[:, 2 * rank : 3 * rank].astype(BRAIN)
    mid = middle[...]
    sgrad = grad[...] + dot(gback, mrel[rank : 3 * rank])
    mg = crel[...].astype(FLOAT) + pulled(mid, grel[1:2], sgrad)
    mgrad[...] = mg
    mlo = mg.astype(BRAIN)
    back = dot(mlo, mrel[3 * rank : 4 * rank], NT).astype(BRAIN)
    for t in range(tiles):
        for copy in sets[t]:
            copy.wait()
        col = slice(t * width, (t + 1) * width)
        rm = emap[0:rank, 3 * channels + t * width : 3 * channels + (t + 1) * width]
        mx = dot(mlo, w[0, :, col]) + dot(back, rm)
        gcg[:, col] = (mx * cv[:, col].astype(FLOAT)).astype(BRAIN)
        cg = mx * gc[:, col].astype(FLOAT)
        cgrad[:, col] = cg
        for i in range(0, width, LANES):
            to = (t * width + i - turn) % channels
            edge[:, to : to + LANES] = cg[:HALO, i : i + LANES]
        dmix[:, col] = dot(back, mixed[:, col], TN)
    full = mid + out[...] + dot(olow, mrel[4 * rank : 5 * rank])
    dff = jnp.concatenate([dot(gback, second[...], TN), dot(olow, crel[...], TN)], axis=0)
    dmx = dot(mlow[...], mlo, TN)
    for r in range(blocks):
        dst = lanes(tab[r])
        src = slice(r * LANES, (r + 1) * LANES)
        output[:, dst] = full[:, src].astype(BRAIN)
        wide_ff[:, dst] = dff[:, src]
        wide_mix[:, dst] = dmx[:, src]


def back_kernel(labels, tiles, tab, mask, cgrad, edge, gcg, gb, va, mgrad, trel, xin, mrel, grel, elow, emap, *rest):
    n = len(labels)
    pieces, rest = rest[:n], rest[n:]
    igrad, wide, dent, w, sems = rest
    rank = elow.shape[1]
    rows = trel.shape[0]
    channels = w.shape[2]
    width = channels // tiles
    sets = fetch(pieces, labels, w, sems, tiles, width, slice(0, 3))
    near = mask[:, 0:1]
    far = mask[:, 1:2]
    fgrad = jnp.zeros((rows, w.shape[1]), FLOAT)
    back = jnp.zeros((rows, rank), FLOAT)
    total = rows + HALO
    for t in range(tiles):
        for copy in sets[t]:
            copy.wait()
        col = slice(t * width, (t + 1) * width)
        taps = emap[rank : rank + 3, col].astype(FLOAT)
        cg = jnp.concatenate([cgrad[:, col], edge[:, col]], axis=0)
        pg = (
            taps[0:1] * cg
            + pltpu.roll(taps[1:2] * near * cg, total - 1, 0)
            + pltpu.roll(taps[2:3] * far * cg, total - 2, 0)
        )[:rows]
        parts = (
            (pg * va[:, col].astype(FLOAT)).astype(BRAIN),
            gcg[:, col],
            (pg * gb[:, col].astype(FLOAT)).astype(BRAIN),
        )
        for k in range(3):
            fgrad = fgrad + dot(parts[k], w[k, :, col], NT)
            wide_col = slice(k * channels + t * width, k * channels + (t + 1) * width)
            back = back + dot(parts[k], emap[0:rank, wide_col], NT)
            dent[:, wide_col] = dot(elow[HALO:, :], parts[k], TN)
    back = back.astype(BRAIN)
    fgrad = fgrad + dot(back, mrel[0:rank])
    full = mgrad[...] + pulled(trel[...].astype(FLOAT), grel[0:1], fgrad)
    dred = dot(back, xin[HALO:, :], TN)
    for r in range(w.shape[1] // LANES):
        dst = lanes(tab[r])
        src = slice(r * LANES, (r + 1) * LANES)
        igrad[:, dst] = full[:, src].astype(BRAIN)
        wide[:, dst] = dred[:, src]


def flipped(block, axis, bit):
    size = lax.axis_size(axis)
    return lax.ppermute(block, axis, [(i, i ^ bit) for i in range(size)])


def shifted(block, axis, distance):
    size = lax.axis_size(axis)
    return lax.ppermute(block, axis, [(i, (i + distance) % size) for i in range(size)])


def passed_along(block, distance):
    axes = ("ctx", "tensor")
    size = lax.axis_size("ctx") * lax.axis_size("tensor")
    route = [(i, i + distance) for i in range(size) if 0 <= i + distance < size]
    return lax.ppermute(block, axes, route)


def around(block):
    size = lax.axis_size("tensor")
    return [block] + [shifted(block, "tensor", s) for s in range(1, size)]


def gathered(unit, order):
    mine = jnp.concatenate(around(unit), axis=2)
    one, two = order
    first = flipped(mine, "dp", one)
    other = flipped(mine, "dp", two)
    both = flipped(first, "dp", two)
    own = [(mine, 0), (first, one), (other, two), (both, one | two)]
    pieces, labels = [], []
    for block, e in own:
        pieces += [block, flipped(block, "ctx", 1)]
        labels += [2 * e, 2 * e + 1]
    return pieces, tuple(labels)


def spread(update, adapter, slots, axis):
    onehot = (lax.broadcasted_iota(jnp.int32, (slots,), 0) == adapter).astype(FLOAT)
    layout = [1] * (update.ndim + 1)
    layout[axis] = slots
    return jnp.expand_dims(update, axis) * onehot.reshape(layout)


def reduced(channel, wide, quick):
    here = lax.axis_index("dp")
    count = lax.axis_size("tensor")
    rows, w = channel.shape[1:]
    d = wide.shape[1]
    if not quick:
        at = lax.axis_index("tensor")
        own = lax.psum(channel, ("ctx", "tensor"))
        own = lax.dynamic_index_in_dim(own, at, 0, keepdims=False)
        all_own = lax.all_gather(own, "dp", axis=0)
        all_wide = lax.all_gather(lax.psum(wide, ("ctx", "tensor")), "dp", axis=0)
        return [(s, all_own[s], all_wide[s]) for s in range(lax.axis_size("dp"))]
    span = max(w, d)

    def padded(block):
        return jnp.pad(block, ((0, 0), (0, span - block.shape[1])))

    whole = jnp.concatenate(
        [padded(channel.reshape(count * rows, w)), padded(wide)], axis=0
    ).astype(BRAIN)
    pair = (whole.astype(FLOAT) + flipped(whole, "ctx", 1).astype(FLOAT)).astype(BRAIN)
    base = pair[count * rows :]
    parts = [jnp.concatenate([pair[s * rows : (s + 1) * rows], base], axis=0) for s in range(count)]
    terms = [parts[0]] + [shifted(parts[s], "tensor", -s) for s in range(1, count)]
    stack = jnp.stack(terms)
    at = lax.axis_index("tensor")
    total = sum(
        lax.dynamic_index_in_dim(stack, (k - at) % count, 0, keepdims=False).astype(FLOAT)
        for k in range(count)
    ).astype(BRAIN)
    result = []
    for e in range(lax.axis_size("dp")):
        got = total if e == 0 else flipped(total, "dp", e)
        result.append((here ^ e, got[:rows, :w].astype(FLOAT), got[rows:, :d].astype(FLOAT)))
    return result


def chosen(table, adapter, axis):
    return lax.dynamic_index_in_dim(table, adapter, axis, keepdims=False)


def per_device(
    tokens,
    segments,
    adapter_of,
    cotangent,
    first_gain,
    second_gain,
    conv_taps,
    entry_weight,
    mixer_weight,
    gates_weight,
    outlet_weight,
    entry_reduce,
    entry_expand,
    mixer_reduce,
    mixer_expand,
    gates_reduce,
    gates_expand,
    outlet_reduce,
    outlet_expand,
):
    slots, rank, depth = entry_reduce.shape
    seqs, cores, count = (lax.axis_size(a) for a in ("dp", "ctx", "tensor"))
    here, core, at = (lax.axis_index(a) for a in ("dp", "ctx", "tensor"))
    rows = tokens.shape[1]
    length = segments.shape[1]
    blocks = depth // LANES
    chan = mixer_weight.shape[0]
    units = outlet_weight.shape[0]
    sub = units // CHUNKS
    channels = chan * count
    quick = seqs == 4 and cores == 2 and depth == seqs * cores * LANES and sub % LANES == 0

    if quick:
        half = depth // seqs // cores
        lo = core * half
        entry_half = lax.dynamic_slice_in_dim(entry_weight, lo, half, 1)
        mixer_half = lax.dynamic_slice_in_dim(mixer_weight, lo, half, 1).T
        gates_half = lax.dynamic_slice_in_dim(gates_weight, lo, half, 1)
        outlet_half = lax.dynamic_slice_in_dim(outlet_weight, lo, half, 1).T
        front, front_at = gathered(jnp.concatenate([entry_half, mixer_half[None]], axis=0), (1, 2))
        feed = []
        for q in range(CHUNKS):
            cols = slice(q * sub, (q + 1) * sub)
            unit = jnp.concatenate([gates_half[:, :, cols], outlet_half[None, :, cols]], axis=0)
            feed.append(gathered(unit, (2, 1) if q % 2 == 0 else (1, 2)))
        tab = jnp.arange(blocks, dtype=jnp.int32) ^ (here * cores + core).astype(jnp.int32)
    else:

        def full(block, rows_axis, cols_axis):
            block = lax.all_gather(block, "dp", axis=rows_axis, tiled=True)
            return lax.all_gather(block, "tensor", axis=cols_axis, tiled=True)

        front = [
            jnp.concatenate(
                [full(entry_weight, 1, 2), full(mixer_weight, 1, 0).T[None]], axis=0
            )
        ]
        front_at = (0,)
        whole = jnp.concatenate(
            [full(gates_weight, 1, 2), full(outlet_weight, 1, 0).T[None]], axis=0
        ).reshape(3, depth, count, CHUNKS, sub)
        feed = [([whole[:, :, :, q].reshape(3, depth, count * sub)], (0,)) for q in range(CHUNKS)]
        tab = jnp.arange(blocks, dtype=jnp.int32)

    adapter = adapter_of[here]
    maps = jnp.concatenate(
        [
            chosen(entry_reduce, adapter, 0),
            chosen(gates_reduce, adapter, 1).reshape(2 * rank, depth),
            chosen(mixer_expand, adapter, 0),
            chosen(outlet_expand, adapter, 0),
        ],
        axis=0,
    )
    local = jnp.concatenate(
        [
            chosen(entry_expand, adapter, 0).reshape(rank, 3 * chan),
            chosen(mixer_reduce, adapter, 0),
            jnp.pad(conv_taps, ((0, rank - 3), (0, 0))),
            chosen(gates_expand, adapter, 1)[0],
            chosen(gates_expand, adapter, 1)[1],
            chosen(outlet_reduce, adapter, 0),
        ],
        axis=1,
    )
    if quick:
        sides = around(local)
    else:
        sides = list(lax.all_gather(local, "tensor", axis=0))

    def columns(first, size):
        return jnp.concatenate([side[:, first : first + size] for side in sides], axis=1)

    low = jnp.concatenate([columns(k * chan, chan) for k in range(4)], axis=1)
    taps = jnp.pad(columns(4 * chan, chan), ((0, 0), (0, 3 * channels)))
    front_map = jnp.concatenate([low, taps], axis=0)
    feed_maps = [
        jnp.concatenate([columns(5 * chan + k * units + q * sub, sub) for k in range(3)], axis=0)
        for q in range(CHUNKS)
    ]

    index = core * count + at
    seg = jnp.concatenate(
        [jnp.full((2,), -1, jnp.int32), segments[0], jnp.full((HALO,), -2, jnp.int32)]
    )
    seg = lax.dynamic_slice_in_dim(seg, index * rows, rows + HALO + 2)
    mask = jnp.stack([seg[1:-1] == seg[2:], seg[:-2] == seg[2:]], axis=1).astype(FLOAT)
    halo = passed_along(tokens[0, rows - HALO :], 1)
    gains = jnp.stack([first_gain, second_gain]).astype(FLOAT)

    wide = lambda dtype: ((rows, depth), dtype)
    inner = lambda dtype: ((rows, channels), dtype)
    small = lambda n: ((rows, n), BRAIN)
    dma = lambda tiles, n: pltpu.SemaphoreType.DMA((tiles, n))

    trel, xin, crel, mrel, grel, elow, ob = call(
        prep_kernel,
        [
            wide(BRAIN),
            ((rows + HALO, depth), BRAIN),
            wide(BRAIN),
            (maps.shape, BRAIN),
            (gains.shape, FLOAT),
            ((rows + HALO, rank), BRAIN),
            small(rank),
        ],
        0,
        1,
        6,
        [],
        8 * rows * depth * rank,
        10 * rows * depth,
    )(tab, tokens[0], halo, cotangent[0], gains, maps)

    tiles = 2
    gb, gc, va, cv, mixed, mlow, middle, second, glow = call(
        functools.partial(front_kernel, front_at, tiles),
        [inner(BRAIN)] * 5 + [small(rank), wide(FLOAT), wide(BRAIN), small(2 * rank)],
        len(front),
        0,
        7 + len(front),
        [pltpu.VMEM((4, depth, channels), BRAIN), dma(tiles, len(front))],
        8 * rows * depth * channels,
        8 * depth * channels + 20 * rows * depth,
    )(mask, xin, trel, mrel, grel, elow, front_map, *front)

    state, changes = (), []
    for q, (pieces, labels) in enumerate(feed):
        span = count * sub
        tiles = max(1, span // 512)
        *state, change = call(
            functools.partial(feed_kernel, labels, tiles, q == 0),
            [wide(FLOAT), wide(FLOAT), ((rows, 3 * rank), FLOAT), ((3 * rank, span), FLOAT)],
            len(pieces),
            0,
            5 + len(state) + len(pieces),
            [pltpu.VMEM((3, depth, span), BRAIN), dma(tiles, len(pieces))],
            12 * rows * depth * span,
            6 * depth * span + 20 * rows * depth,
        )(second, crel, glow, ob, feed_maps[q], *state, *pieces)
        changes.append(change.reshape(3 * rank, count, sub))

    tiles = 2
    output, mgrad, cgrad, edge, gcg, wide_feed, wide_mix, change_mix = call(
        functools.partial(middle_kernel, front_at, tiles, chan if quick else 0),
        [
            wide(BRAIN),
            wide(FLOAT),
            inner(FLOAT),
            ((HALO, channels), FLOAT),
            inner(BRAIN),
            ((3 * rank, depth), FLOAT),
            ((rank, depth), FLOAT),
            ((rank, channels), FLOAT),
        ],
        len(front),
        1,
        14 + len(front),
        [pltpu.VMEM((1, depth, channels), BRAIN), dma(tiles, len(front))],
        2 * rows * depth * channels,
        2 * depth * channels + 30 * rows * depth,
    )(tab, *state, middle, second, crel, mrel, grel, mlow, mixed, gc, cv, front_map, *front)
    edge = passed_along(edge, -1)
    in_grad, wide_entry, change_entry = call(
        functools.partial(back_kernel, front_at, tiles),
        [wide(BRAIN), ((rank, depth), FLOAT), ((rank, 3 * channels), FLOAT)],
        len(front),
        1,
        14 + len(front),
        [pltpu.VMEM((3, depth, channels), BRAIN), dma(tiles, len(front))],
        6 * rows * depth * channels,
        6 * depth * channels + 20 * rows * depth,
    )(tab, mask, cgrad, edge, gcg, gb, va, mgrad, trel, xin, mrel, grel, elow, front_map, *front)

    feed_sum = reduced(
        jnp.concatenate(changes, axis=2).transpose(1, 0, 2), wide_feed, quick
    )
    front_sum = reduced(
        jnp.concatenate(
            [
                change_entry.reshape(rank, 3, count, chan),
                change_mix.reshape(rank, 1, count, chan),
            ],
            axis=1,
        )
        .transpose(2, 0, 1, 3)
        .reshape(count, rank, 4 * chan),
        jnp.concatenate([wide_entry, wide_mix], axis=0),
        quick,
    )

    def placed(pieces, axis):
        return sum(spread(piece, adapter_of[s], slots, axis) for s, piece in pieces)

    grad_entry_reduce = placed([(s, w[:rank]) for s, _, w in front_sum], 0)
    grad_entry_expand = placed(
        [(s, c[:, : 3 * chan].reshape(rank, 3, chan)) for s, c, _ in front_sum], 0
    )
    grad_mixer_reduce = placed([(s, c[:, 3 * chan :]) for s, c, _ in front_sum], 0)
    grad_mixer_expand = placed([(s, w[rank:]) for s, _, w in front_sum], 0)
    grad_gates_reduce = placed(
        [(s, w[: 2 * rank].reshape(2, rank, depth)) for s, _, w in feed_sum], 1
    )
    grad_gates_expand = placed(
        [(s, c[: 2 * rank].reshape(2, rank, units)) for s, c, _ in feed_sum], 1
    )
    grad_outlet_reduce = placed([(s, c[2 * rank :]) for s, c, _ in feed_sum], 0)
    grad_outlet_expand = placed([(s, w[2 * rank :]) for s, _, w in feed_sum], 0)
    return (
        output[None],
        in_grad[None],
        grad_entry_reduce,
        grad_entry_expand,
        grad_mixer_reduce,
        grad_mixer_expand,
        grad_gates_reduce,
        grad_gates_expand,
        grad_outlet_reduce,
        grad_outlet_expand,
    )


def solution(mesh):
    return jax.shard_map(
        per_device,
        mesh=mesh,
        in_specs=(
            P("dp", ("ctx", "tensor"), None),
            P("dp", None),
            P(),
            P("dp", ("ctx", "tensor"), None),
            P(),
            P(),
            P(None, "tensor"),
            P(None, "dp", "tensor"),
            P("tensor", "dp"),
            P(None, "dp", "tensor"),
            P("tensor", "dp"),
            P(),
            P(None, None, None, "tensor"),
            P(None, None, "tensor"),
            P(),
            P(),
            P(None, None, None, "tensor"),
            P(None, None, "tensor"),
            P(),
        ),
        out_specs=(
            P("dp", ("ctx", "tensor"), None),
            P("dp", ("ctx", "tensor"), None),
            P(),
            P(None, None, None, "tensor"),
            P(None, None, "tensor"),
            P(),
            P(),
            P(None, None, None, "tensor"),
            P(None, None, "tensor"),
            P(),
        ),
        check_vma=False,
    )
```

```python
import functools

import jax
import jax.numpy as jnp
from jax import lax
from jax.experimental import pallas as pl
from jax.experimental.pallas import tpu as pltpu
from jax.sharding import PartitionSpec as P

EPSILON = 1e-05
FLOAT = jnp.float32
BRAIN = jnp.bfloat16
HALO = 16
LANES = 128
CHUNKS = 3
NN = ((1,), (0,))
NT = ((1,), (1,))
TN = ((0,), (0,))


def dot(a, b, dims=NN):
    return lax.dot_general(a, b, (dims, ((), ())), preferred_element_type=FLOAT)


def lanes(index):
    return pl.ds(pl.multiple_of(index * LANES, LANES), LANES)


class Held:
    def __init__(self):
        self.copies, self.gone = {}, []

    def need(self, *names):
        for name in names:
            self.copies.pop(name).wait()

    def leave(self, name, cols=None):
        at = (slice(None),) * (len(getattr(self, name).shape) - 1)
        view = lambda ref: ref if cols is None else ref.at[at + (pl.ds(*cols),)]
        copy = pltpu.make_async_copy(
            view(getattr(self, name)), view(self.targets[name]), self.out_sems.at[len(self.gone)]
        )
        copy.start()
        self.gone.append((name, copy))


def call(body, scalars, ins, raw, outs, scratch):
    forms = {n: o if isinstance(o, tuple) else (ins[o].shape, ins[o].dtype) for n, o in outs.items()}
    fresh = [n for n, o in outs.items() if isinstance(o, tuple)]
    raw_names = list(raw)

    def kernel(*refs):
        refs = list(refs)
        take = lambda count: [refs.pop(0) for _ in range(count)]
        r = Held()
        for name, ref in zip(scalars, take(len(scalars))):
            setattr(r, name, ref)
        sources = dict(zip(ins, take(len(ins))))
        for name, ref in zip(raw_names, take(len(raw_names))):
            setattr(r, name, ref)
        r.targets = dict(zip(outs, take(len(outs))))
        for name, ref in zip(ins, take(len(ins))):
            setattr(r, name, ref)
        for name, ref in zip(fresh, take(len(fresh))):
            setattr(r, name, ref)
        for name, origin in outs.items():
            if not isinstance(origin, tuple):
                setattr(r, name, getattr(r, origin))
        in_sems, r.out_sems = take(2)
        r.scratch = refs
        for k, (name, source) in enumerate(sources.items()):
            r.copies[name] = pltpu.make_async_copy(source, getattr(r, name), in_sems.at[k])
            r.copies[name].start()
        body(r)
        for name in outs:
            if name not in [n for n, _ in r.gone]:
                r.leave(name)
        for _, copy in r.gone:
            copy.wait()
        r.need(*list(r.copies))

    hbm = pl.BlockSpec(memory_space=pltpu.HBM)
    return pl.pallas_call(
        kernel,
        out_shape=[jax.ShapeDtypeStruct(*form) for form in forms.values()],
        in_specs=[pl.BlockSpec(memory_space=pltpu.SMEM)] * len(scalars)
        + [hbm] * (len(ins) + len(raw)),
        out_specs=[hbm] * len(outs),
        scratch_shapes=[pltpu.VMEM(v.shape, v.dtype) for v in ins.values()]
        + [pltpu.VMEM(*forms[n]) for n in fresh]
        + [pltpu.SemaphoreType.DMA((max(1, len(ins)),)), pltpu.SemaphoreType.DMA((32,))]
        + list(scratch),
        compiler_params=pltpu.CompilerParams(vmem_limit_bytes=54 << 20),
        cost_estimate=pl.CostEstimate(flops=1, bytes_accessed=1, transcendentals=0),
    )(*scalars.values(), *ins.values(), *raw.values())


def prep_body(r):
    rank = r.elow.shape[1]
    a = r.pick[0]
    maps, sems = r.scratch
    sources = (r.er.at[a], r.gr.at[0, a], r.gr.at[1, a], r.me.at[a], r.oe.at[a])
    copies = [
        pltpu.make_async_copy(source, maps.at[k], sems.at[k]) for k, source in enumerate(sources)
    ]
    for copy in copies:
        copy.start()
    r.need("tok", "halo")
    t32 = r.tok[...].astype(FLOAT)
    inv = lax.rsqrt(jnp.mean(t32 * t32, axis=-1, keepdims=True) + EPSILON)
    h32 = r.halo[...].astype(FLOAT)
    hinv = lax.rsqrt(jnp.mean(h32 * h32, axis=-1, keepdims=True) + EPSILON)
    r.need("cot", "gains")
    for copy in copies:
        copy.wait()
    for b in range(r.tok.shape[1] // LANES):
        src = lanes(r.tab[b])
        dst = slice(b * LANES, (b + 1) * LANES)
        part = r.tok[:, src]
        gain = r.gains[:, src]
        r.trel[:, dst] = part
        r.xin[HALO:, dst] = (part.astype(FLOAT) * inv * gain[0:1]).astype(BRAIN)
        r.xin[:HALO, dst] = (r.halo[:, src].astype(FLOAT) * hinv * gain[0:1]).astype(BRAIN)
        r.crel[:, dst] = r.cot[:, src]
        for k in range(5):
            r.mrel[k * rank : (k + 1) * rank, dst] = maps[k, :, src]
        r.grel[:, dst] = gain
    for name in ("trel", "xin", "crel"):
        r.leave(name)
    r.elow[...] = dot(r.xin[...], r.mrel[0:rank], NT).astype(BRAIN)
    r.ob[...] = dot(r.crel[...], r.mrel[4 * rank : 5 * rank], NT).astype(BRAIN)


def front_pack_body(r):
    half = r.unit.shape[1]
    rows = pl.ds(pl.multiple_of(r.core[0] * half, half), half)
    r.need("entry")
    for k in range(3):
        r.unit[k] = r.entry[k, rows, :]
    r.need("mixer")
    r.unit[3] = r.mixer[:, rows].astype(FLOAT).T.astype(BRAIN)


def feed_pack_body(count, r):
    units = [getattr(r, f"unit{q}") for q in range(count)]
    half = units[0].shape[1]
    rows = pl.ds(pl.multiple_of(r.core[0] * half, half), half)
    r.need("gates", "outlet")
    first = 0
    for q, unit in enumerate(units):
        cols = slice(first, first + unit.shape[2])
        for k in range(2):
            unit[k] = r.gates[k, rows, cols]
        unit[2] = r.outlet[cols, rows].astype(FLOAT).T.astype(BRAIN)
        r.leave(f"unit{q}")
        first += unit.shape[2]


def half_kernel(core, came, half):
    half[...] = came[...]


def local_body(r):
    whole, sems = r.scratch
    chan = r.taps.shape[1]
    units = r.orr.shape[2]
    a = r.pick[0]
    first = 5 * chan
    rank, half = r.out.shape
    copies = [
        pltpu.make_async_copy(source, whole.at[:, pl.ds(at, size)], sems.at[k])
        for k, (source, at, size) in enumerate(
            (
                (r.mr.at[a], 3 * chan, chan),
                (r.ge.at[0, a], first, units),
                (r.ge.at[1, a], first + units, units),
                (r.orr.at[a], first + 2 * units, units),
            )
        )
    ]
    for copy in copies:
        copy.start()
    r.need("ee", "taps")
    whole[:, : 3 * chan] = r.ee[...]
    whole[:, 4 * chan : 5 * chan] = jnp.zeros((rank, chan), BRAIN)
    whole[0:3, 4 * chan : 5 * chan] = r.taps[...]
    whole[:, first + 3 * units :] = jnp.zeros((rank, whole.shape[1] - first - 3 * units), BRAIN)
    for copy in copies:
        copy.wait()
    r.out[...] = whole[:, pl.ds(pl.multiple_of(r.core[0] * half, LANES), half)]


def maps_body(chan, units, subs, r):
    [side] = r.scratch
    front = r.front
    rank = front.shape[0] // 2
    half = r.mine.shape[1]
    count = r.mine.shape[0] // rank
    channels = chan * count
    r.need("mine", "theirs")
    side[:, pl.ds(pl.multiple_of(r.core[0] * half, LANES), half)] = r.mine[...]
    side[:, pl.ds(pl.multiple_of((1 - r.core[0]) * half, LANES), half)] = r.theirs[...]
    for s in range(count):
        own = slice(s * rank, (s + 1) * rank)
        z = r.pos[s]
        for k in range(4):
            at = pl.ds(pl.multiple_of(k * channels + z * chan, LANES), chan)
            front[0:rank, at] = side[own, k * chan : (k + 1) * chan]
        at = pl.ds(pl.multiple_of(z * chan, LANES), chan)
        front[rank : 2 * rank, at] = side[own, 4 * chan : 5 * chan]
        first = 5 * chan
        for q, sub in enumerate(subs):
            feed = getattr(r, f"feed{q}")
            for k in range(3):
                at = first + k * units
                to = pl.ds(pl.multiple_of(z * sub, LANES), sub)
                feed[k * rank : (k + 1) * rank, to] = side[own, at : at + sub]
            first += sub


def fetch(r, count, labels, w, sems, planes):
    pieces = [getattr(r, f"piece{p}") for p in range(len(labels))]
    width = pieces[0].shape[3]

    def copies(z):
        cols = pl.ds(pl.multiple_of(z * width, LANES), width)
        found = []
        for ref, label in zip(pieces, labels):
            for h in range(ref.shape[0] // count):
                size = ref.shape[2]
                source = ref.at[h * count + z, planes]
                target = w.at[:, pl.ds(label * LANES + h * size, size), cols]
                found.append(pltpu.make_async_copy(source, target, sems.at[z, len(found)]))
        return found

    for z in range(count):
        for copy in copies(z):
            copy.start()

    def wait(z):
        for copy in copies(z):
            copy.wait()

    def upto(t, tile):
        return range(-(-t * tile // width), -(-(t + 1) * tile // width))

    return wait, upto, width


def front_body(labels, tiles, r):
    w, sems = r.scratch
    rank = r.elow.shape[1]
    rows = r.trel.shape[0]
    channels = w.shape[2]
    width = channels // tiles
    wait, upto, _ = fetch(r, sems.shape[0], labels, w, sems, slice(0, 4))
    r.need("mask", "xin", "elow", "emap", "mrel")
    near = r.mask[0:rows, 0:1]
    far = r.mask[0:rows, 1:2]
    branch = jnp.zeros((rows, w.shape[1]), FLOAT)
    low = jnp.zeros((rows, rank), FLOAT)
    for t in range(tiles):
        for z in upto(t, width):
            wait(z)
        col = slice(t * width, (t + 1) * width)

        def project(k):
            wide = slice(k * channels + t * width, k * channels + (t + 1) * width)
            return dot(r.xin[...], w[k, :, col]) + dot(r.elow[...], r.emap[0:rank, wide])

        b = project(0)
        v = project(2)
        c = project(1)[HALO:]
        product = b * v
        r.gb[:, col] = b[HALO:].astype(BRAIN)
        r.va[:, col] = v[HALO:].astype(BRAIN)
        r.gc[:, col] = c.astype(BRAIN)
        taps = r.emap[rank : rank + 3, col].astype(FLOAT)
        conv = (
            taps[0:1] * product[HALO:]
            + taps[1:2] * near * pltpu.roll(product, 1, 0)[HALO:]
            + taps[2:3] * far * pltpu.roll(product, 2, 0)[HALO:]
        )
        r.cv[:, col] = conv.astype(BRAIN)
        mix = (c * conv).astype(BRAIN)
        r.mixed[:, col] = mix
        for name in ("gb", "gc", "va", "cv", "mixed"):
            r.leave(name, (t * width, width))
        branch = branch + dot(mix, w[3, :, col], NT)
        own = slice(3 * channels + t * width, 3 * channels + (t + 1) * width)
        low = low + dot(mix, r.emap[0:rank, own], NT)
    low = low.astype(BRAIN)
    r.mlow[...] = low
    r.need("trel", "grel")
    mid = r.trel[...].astype(FLOAT) + branch + dot(low, r.mrel[3 * rank : 4 * rank])
    r.middle[...] = mid
    r.leave("middle")
    inv = lax.rsqrt(jnp.mean(mid * mid, axis=-1, keepdims=True) + EPSILON)
    x2 = (mid * inv * r.grel[1:2]).astype(BRAIN)
    r.second[...] = x2
    r.leave("second")
    r.glow[...] = dot(x2, r.mrel[rank : 3 * rank], NT).astype(BRAIN)


def feed_body(labels, tiles, sub, first, r):
    w, sems = r.scratch
    rank = r.ob.shape[1]
    width = w.shape[2] // tiles
    wait, _, part = fetch(r, sems.shape[0], labels, w, sems, slice(0, 3))
    r.need("second", "crel", "glow", "ob", "emap")
    if first:
        r.out[...] = jnp.zeros_like(r.out)
        r.grad[...] = jnp.zeros_like(r.grad)
        r.small[...] = jnp.zeros_like(r.small)
    else:
        r.need("out_in", "grad_in", "small_in")

    def step(t, carry):
        need = lambda t: (t * width + part - 1) // part
        lax.fori_loop(need(t), need(t + 1), lambda z, c: (wait(z), c)[1], 0)
        col = pl.ds(pl.multiple_of(t * width, LANES), width)
        eg, eu, ro = (r.emap[i * rank : (i + 1) * rank, col] for i in range(3))
        wg, wu, wo = (w[i, :, col] for i in range(3))
        x = r.second[...]
        lg, lu, ob = r.glow[:, 0:rank], r.glow[:, rank : 2 * rank], r.ob[...]
        g = dot(x, wg) + dot(lg, eg)
        u = dot(x, wu) + dot(lu, eu)
        h_grad = dot(r.crel[...], wo) + dot(ob, ro)
        sigma = 1.0 / (1.0 + jnp.exp(-g))
        act = g * sigma
        h = (act * u).astype(BRAIN)
        gg = (h_grad * u * (sigma * (1.0 + g * (1.0 - sigma)))).astype(BRAIN)
        ug = (h_grad * act).astype(BRAIN)
        r.out[...] += dot(h, wo, NT)
        r.grad[...] += dot(gg, wg, NT) + dot(ug, wu, NT)
        r.small[:, 0:rank] += dot(gg, eg, NT)
        r.small[:, rank : 2 * rank] += dot(ug, eu, NT)
        r.small[:, 2 * rank : 3 * rank] += dot(h, ro, NT)
        changes = (dot(lg, gg, TN), dot(lu, ug, TN), dot(ob, h, TN))
        for j in range(0, width, LANES):
            at = t * width + j
            owner = at // sub
            for k in range(3):
                to = r.pos[owner] * (3 * sub) + k * sub + (at - owner * sub)
                to = pl.ds(pl.multiple_of(to, LANES), LANES)
                r.dmap[:, to] = changes[k][:, j : j + LANES].astype(r.dmap.dtype)
        return carry

    lax.fori_loop(0, tiles, step, 0)


def pulled(v, gain, grad):
    inv = lax.rsqrt(jnp.mean(v * v, axis=-1, keepdims=True) + EPSILON)
    scaled = grad * gain
    along = jnp.mean(v * scaled, axis=-1, keepdims=True)
    return inv * scaled - v * (inv * inv * inv * along)


def middle_body(labels, tiles, chan, r):
    w, sems = r.scratch
    rank = r.mlow.shape[1]
    channels = w.shape[2]
    width = channels // tiles
    depth = w.shape[1]
    wait, upto, _ = fetch(r, sems.shape[0], labels, w, sems, slice(3, 4))
    r.need("middle", "grad", "small", "crel", "mrel", "grel", "emap")
    gback = r.small[:, 0 : 2 * rank].astype(BRAIN)
    olow = r.small[:, 2 * rank : 3 * rank].astype(BRAIN)
    mid = r.middle[...]
    sgrad = r.grad[...] + dot(gback, r.mrel[rank : 3 * rank])
    mg = r.crel[...].astype(FLOAT) + pulled(mid, r.grel[1:2], sgrad)
    r.mgrad[...] = mg
    r.leave("mgrad")
    mlo = mg.astype(BRAIN)
    back = dot(mlo, r.mrel[3 * rank : 4 * rank], NT).astype(BRAIN)
    r.need("gc", "cv", "mixed")
    for t in range(tiles):
        for z in upto(t, width):
            wait(z)
        col = slice(t * width, (t + 1) * width)
        rm = r.emap[0:rank, 3 * channels + t * width : 3 * channels + (t + 1) * width]
        mx = dot(mlo, w[0, :, col]) + dot(back, rm)
        r.gcg[:, col] = (mx * r.cv[:, col].astype(FLOAT)).astype(BRAIN)
        cg = mx * r.gc[:, col].astype(FLOAT)
        r.cgrad[:, col] = cg
        for name in ("gcg", "cgrad"):
            r.leave(name, (t * width, width))
        r.edge[:, col] = cg[:HALO]
        change = dot(back, r.mixed[:, col], TN).astype(BRAIN)
        for j in range(0, width, LANES):
            owner, off = divmod(t * width + j, chan)
            to = pl.ds(pl.multiple_of(r.pos[owner] * chan + off, LANES), LANES)
            r.dmix[:, to] = change[:, j : j + LANES]
    r.leave("edge")
    r.need("out", "second", "mlow")
    full = mid + r.out[...] + dot(olow, r.mrel[4 * rank : 5 * rank])
    dff = jnp.concatenate([dot(gback, r.second[...], TN), dot(olow, r.crel[...], TN)], axis=0)
    dmx = dot(r.mlow[...], mlo, TN)
    for b in range(depth // LANES):
        dst = lanes(r.tab[b])
        src = slice(b * LANES, (b + 1) * LANES)
        r.output[:, dst] = full[:, src].astype(BRAIN)
        for k in range(3):
            to = pl.ds(pl.multiple_of(k * depth + r.tab[b] * LANES, LANES), LANES)
            r.wide[:, to] = dff[k * rank : (k + 1) * rank, src].astype(BRAIN)
        to = pl.ds(pl.multiple_of(3 * depth + r.tab[b] * LANES, LANES), LANES)
        r.wide[:, to] = dmx[:, src].astype(BRAIN)


def back_body(labels, tiles, chan, r):
    w, sems = r.scratch
    rank = r.elow.shape[1]
    rows = r.trel.shape[0]
    channels = w.shape[2]
    width = channels // tiles
    wait, upto, _ = fetch(r, sems.shape[0], labels, w, sems, slice(0, 3))
    r.need("mask", "edge", "cgrad", "gcg", "gb", "va", "elow", "emap", "mrel")
    near = r.mask[:, 0:1]
    far = r.mask[:, 1:2]
    fgrad = jnp.zeros((rows, w.shape[1]), FLOAT)
    back = jnp.zeros((rows, rank), FLOAT)
    total = rows + HALO
    for t in range(tiles):
        for z in upto(t, width):
            wait(z)
        col = slice(t * width, (t + 1) * width)
        taps = r.emap[rank : rank + 3, col].astype(FLOAT)
        cg = jnp.concatenate([r.cgrad[:, col], r.edge[:, col]], axis=0)
        pg = (
            taps[0:1] * cg
            + pltpu.roll(taps[1:2] * near * cg, total - 1, 0)
            + pltpu.roll(taps[2:3] * far * cg, total - 2, 0)
        )[:rows]
        parts = (
            (pg * r.va[:, col].astype(FLOAT)).astype(BRAIN),
            r.gcg[:, col],
            (pg * r.gb[:, col].astype(FLOAT)).astype(BRAIN),
        )
        for k in range(3):
            fgrad = fgrad + dot(parts[k], w[k, :, col], NT)
            wide_col = slice(k * channels + t * width, k * channels + (t + 1) * width)
            back = back + dot(parts[k], r.emap[0:rank, wide_col], NT)
            change = dot(r.elow[HALO:, :], parts[k], TN).astype(BRAIN)
            for j in range(0, width, LANES):
                owner, off = divmod(t * width + j, chan)
                to = pl.multiple_of(r.pos[owner] * 3 * chan + k * chan + off, LANES)
                r.dent[:, pl.ds(to, LANES)] = change[:, j : j + LANES]
    r.leave("dent")
    back = back.astype(BRAIN)
    fgrad = fgrad + dot(back, r.mrel[0:rank])
    r.need("mgrad", "trel", "grel", "xin")
    dred = dot(back, r.xin[HALO:, :], TN)
    full = r.mgrad[...] + pulled(r.trel[...].astype(FLOAT), r.grel[0:1], fgrad)
    for b in range(w.shape[1] // LANES):
        dst = lanes(r.tab[b])
        src = slice(b * LANES, (b + 1) * LANES)
        r.igrad[:, dst] = full[:, src].astype(BRAIN)
        r.wide[:, dst] = dred[:, src].astype(BRAIN)


def shifted(block, distance):
    size = lax.axis_size("tensor")
    return lax.ppermute(block, "tensor", [(i, (i + distance) % size) for i in range(size)])


def flipped(block, bit):
    return lax.ppermute(block, "dp", [(i, i ^ bit) for i in range(lax.axis_size("dp"))])


def swapped(block):
    return lax.ppermute(block, "ctx", [(0, 1), (1, 0)])


def turned(block, bits):
    route = [(2 * d + c, 2 * (d ^ bits[c]) + c) for d in range(lax.axis_size("dp")) for c in range(2)]
    return lax.ppermute(block, ("dp", "ctx"), route)


def passed_along(block, distance):
    axes = ("ctx", "tensor")
    size = lax.axis_size("ctx") * lax.axis_size("tensor")
    route = [(i, i + distance) for i in range(size) if 0 <= i + distance < size]
    return lax.ppermute(block, axes, route)


def after(value, *others):
    return lax.optimization_barrier((value, others))[0]


def shape_of(chip, core):
    near = jnp.where(core == 0, 1, 2)
    places = [(0, 0), (0, 1), (near, 0), (near, 1), (3 - near, 0), (3 - near, 1)]
    places += [(3, core), (3, 1 - core)]
    return jnp.stack([(chip ^ e) * 2 + h for e, h in places]).astype(jnp.int32)


class Line:
    def __init__(self):
        self.held = []
        self.values = {}

    def wait(self, *names):
        for name in names:
            self.held.append(self.values[name])
        self.held = self.held[-3:]

    def hold(self, *values):
        self.held = (self.held + list(values))[-3:]

    def ready(self, value):
        return after(value, *self.held) if self.held else value

    def start(self, name, move, value):
        self.values[name] = move(self.ready(value))

    def __getitem__(self, name):
        return self.values[name]


class Block:
    def __init__(self, line, name, unit):
        self.line, self.name, self.unit = line, name, unit

    def at(self, step):
        return self.line[self.name + step]

    def go(self, *steps):
        for step in steps:
            self.line.start(self.name + step, *self.plan(step))

    def wait(self, *steps):
        self.line.wait(*(self.name + step for step in steps))

    def plan(self, step):
        if step == "z":
            return (lambda v: lax.all_gather(v, ("ctx", "tensor"), axis=0)), self.unit
        if step == "o":
            return (lambda v: turned(v, (1, 2))), self.at("z")
        if step == "d":
            came = self.at("o")
            shape = (came.shape[0] // 2,) + came.shape[1:]
            block = (1,) + came.shape[1:]
            half = pl.pallas_call(
                half_kernel,
                grid_spec=pltpu.PrefetchScalarGridSpec(
                    num_scalar_prefetch=1,
                    grid=(shape[0],),
                    in_specs=[pl.BlockSpec(block, lambda i, c: (c[0] * shape[0] + i, 0, 0, 0))],
                    out_specs=pl.BlockSpec(block, lambda i, c: (i, 0, 0, 0)),
                ),
                out_shape=jax.ShapeDtypeStruct(shape, BRAIN),
            )(self.line.ready(lax.axis_index("ctx")[None].astype(jnp.int32)), came)
            return (lambda v: turned(v, (2, 1))), half
        return swapped, self.at(step[1:])

    def pieces(self):
        return [self.at(n) for n in ("z", "o", "co", "d", "cd")], (0, 2, 4, 6, 7)


def spread(update, adapter, slots, axis):
    onehot = (lax.broadcasted_iota(jnp.int32, (slots,), 0) == adapter).astype(FLOAT)
    layout = [1] * (update.ndim + 1)
    layout[axis] = slots
    return jnp.expand_dims(update, axis) * onehot.reshape(layout)


def rounded(value):
    return lax.reduce_precision(value, 8, 7).astype(BRAIN)


class Sum:
    def __init__(self, line, name, owned, shared):
        self.line, self.name, self.shared = line, name, shared
        self.count = lax.axis_size("tensor")
        self.owned = owned
        self.widths = [block.shape[1] // self.count for block in owned]

    def across(self):
        mine = jnp.concatenate(self.owned + self.shared, axis=1)
        self.mine = mine
        self.line.start(self.name + "across", swapped, mine)

    def down(self):
        pair = self.mine.astype(FLOAT) + self.line[self.name + "across"].astype(FLOAT)
        pair = rounded(pair)
        rest = pair[:, sum(self.widths) * self.count :]
        self.parts = []
        for s in range(self.count):
            first, part = 0, []
            for width in self.widths:
                part.append(pair[:, first + s * width : first + (s + 1) * width])
                first += width * self.count
            self.parts.append(jnp.concatenate(part + [rest] * len(self.shared), axis=1))
        for s in range(1, self.count):
            self.line.start(self.name + f"down{s}", lambda v, s=s: shifted(v, -s), self.parts[s])

    def out(self):
        terms = [self.parts[0]] + [self.line[self.name + f"down{s}"] for s in range(1, self.count)]
        stack = jnp.stack(terms)
        at = lax.axis_index("tensor")
        self.total = sum(
            lax.dynamic_index_in_dim(stack, (k - at) % self.count, 0, keepdims=False).astype(FLOAT)
            for k in range(self.count)
        )
        self.total = rounded(self.total)
        for e in range(1, lax.axis_size("dp")):
            self.line.start(self.name + f"out{e}", lambda v, e=e: flipped(v, e), self.total)

    def result(self):
        here = lax.axis_index("dp")
        rows = [(here, self.total)]
        for e in range(1, lax.axis_size("dp")):
            rows.append((here ^ e, self.line[self.name + f"out{e}"]))
        return [(s, row.astype(FLOAT)) for s, row in rows]


def plain_sum(owned, shared):
    count = lax.axis_size("tensor")
    at = lax.axis_index("tensor")
    parts = []
    for block in owned:
        block = lax.psum(block.astype(FLOAT), ("ctx", "tensor"))
        width = block.shape[1] // count
        parts.append(lax.dynamic_slice_in_dim(block, at * width, width, 1))
    parts.append(lax.psum(shared.astype(FLOAT), ("ctx", "tensor")))
    rows = lax.all_gather(jnp.concatenate(parts, axis=1), "dp", axis=0)
    return [(s, rows[s]) for s in range(lax.axis_size("dp"))]


def chosen(table, adapter, axis):
    return lax.dynamic_index_in_dim(table, adapter, axis, keepdims=False)


def chunk_widths(units):
    if units == 1152:
        return (384, 384, 384)
    return (units // 3,) * 3


def per_device(
    tokens,
    segments,
    adapter_of,
    cotangent,
    first_gain,
    second_gain,
    conv_taps,
    entry_weight,
    mixer_weight,
    gates_weight,
    outlet_weight,
    entry_reduce,
    entry_expand,
    mixer_reduce,
    mixer_expand,
    gates_reduce,
    gates_expand,
    outlet_reduce,
    outlet_expand,
):
    slots, rank, depth = entry_reduce.shape
    seqs, cores, count = (lax.axis_size(a) for a in ("dp", "ctx", "tensor"))
    here, core, at = (lax.axis_index(a) for a in ("dp", "ctx", "tensor"))
    rows = tokens.shape[1]
    blocks = depth // LANES
    chan = mixer_weight.shape[0]
    units = outlet_weight.shape[0]
    channels = chan * count
    subs = chunk_widths(units)
    firsts = [sum(subs[:q]) for q in range(len(subs))]
    quick = (
        seqs == 4
        and cores == 2
        and count == 4
        and depth == seqs * cores * LANES
        and all(sub % LANES == 0 for sub in subs)
    )
    line = Line()

    adapter = adapter_of[here]
    pick = adapter[None].astype(jnp.int32)
    own = core[None].astype(jnp.int32)
    expand = chosen(entry_expand, adapter, 0).reshape(rank, 3 * chan)

    if quick:
        half = depth // seqs // cores
        [front_unit] = call(
            front_pack_body,
            dict(core=own),
            dict(entry=entry_weight, mixer=mixer_weight),
            {},
            dict(unit=((4, half, chan), BRAIN)),
            [],
        )
        line.start("halo", lambda v: passed_along(v, 1), tokens[0, rows - HALO :])
        halo = line["halo"]
        e = Block(line, "e", front_unit)
        e.go("z")
        span = 5 * chan + 3 * units
        span = (span + 2 * LANES - 1) // (2 * LANES) * LANES
        [local] = call(
            local_body,
            dict(pick=pick, core=after(own, front_unit)),
            dict(ee=expand, taps=conv_taps),
            dict(mr=mixer_reduce, ge=gates_expand, orr=outlet_reduce),
            dict(out=((rank, span), BRAIN)),
            [pltpu.VMEM((rank, 2 * span), BRAIN), pltpu.SemaphoreType.DMA((4,))],
        )
        feed_units = call(
            functools.partial(feed_pack_body, len(subs)),
            dict(core=after(own, front_unit)),
            dict(gates=gates_weight, outlet=outlet_weight),
            {},
            {f"unit{q}": ((3, half, sub), BRAIN) for q, sub in enumerate(subs)},
            [],
        )
        tab = shape_of(here, core)
        pos = ((at - jnp.arange(count)) % count).astype(jnp.int32)
    else:
        halo = passed_along(tokens[0, rows - HALO :], 1)
        local = jnp.concatenate(
            [
                expand,
                chosen(mixer_reduce, adapter, 0),
                jnp.pad(conv_taps, ((0, rank - 3), (0, 0))),
                chosen(gates_expand, adapter, 1)[0],
                chosen(gates_expand, adapter, 1)[1],
                chosen(outlet_reduce, adapter, 0),
            ],
            axis=1,
        )

        def full(block, rows_axis, cols_axis):
            block = lax.all_gather(block, "dp", axis=rows_axis, tiled=True)
            return lax.all_gather(block, "tensor", axis=cols_axis, tiled=True)

        front = [
            jnp.concatenate(
                [full(entry_weight, 1, 2), full(mixer_weight, 1, 0).T[None]], axis=0
            )
        ]
        front = [front[0][None]]
        front_at = (0,)
        pos = jnp.arange(count, dtype=jnp.int32)
        whole = jnp.concatenate(
            [full(gates_weight, 1, 2), full(outlet_weight, 1, 0).T[None]], axis=0
        ).reshape(3, depth, count, units)
        feed = [
            ([whole[:, :, :, first : first + sub].reshape(1, 3, depth, count * sub)], (0,))
            for first, sub in zip(firsts, subs)
        ]
        tab = jnp.arange(blocks, dtype=jnp.int32)
        side = list(lax.all_gather(local, "tensor", axis=0))

        def columns(first, size):
            return jnp.concatenate([part[:, first : first + size] for part in side], axis=1)

        low = jnp.concatenate([columns(k * chan, chan) for k in range(4)], axis=1)
        taps = jnp.pad(columns(4 * chan, chan), ((0, 0), (0, 3 * channels)))
        front_map = jnp.concatenate([low, taps], axis=0)
        feed_maps = [
            jnp.concatenate([columns(5 * chan + k * units + first, sub) for k in range(3)], axis=0)
            for first, sub in zip(firsts, subs)
        ]

    index = core * count + at
    seg = jnp.concatenate(
        [jnp.full((2,), -1, jnp.int32), segments[0], jnp.full((HALO,), -2, jnp.int32)]
    )
    seg = lax.dynamic_slice_in_dim(seg, index * rows, rows + HALO + 2)
    mask = jnp.stack([seg[1:-1] == seg[2:], seg[:-2] == seg[2:]], axis=1).astype(FLOAT)
    gains = jnp.stack([first_gain, second_gain]).astype(FLOAT)

    wide = lambda dtype: ((rows, depth), dtype)
    inner = lambda dtype: ((rows, channels), dtype)
    small = lambda n: ((rows, n), BRAIN)
    dma = pltpu.SemaphoreType.DMA((count if quick else 1, blocks))
    numbered = lambda pieces: {f"piece{p}": piece for p, piece in enumerate(pieces)}

    def run_prep():
        return call(
            prep_body,
            dict(pick=pick, tab=tab),
            dict(tok=tokens[0], halo=halo, cot=cotangent[0], gains=gains),
            dict(er=entry_reduce, gr=gates_reduce, me=mixer_expand, oe=outlet_expand),
            dict(
                trel=wide(BRAIN),
                xin=((rows + HALO, depth), BRAIN),
                crel=wide(BRAIN),
                mrel=((5 * rank, depth), BRAIN),
                grel=(gains.shape, FLOAT),
                elow=((rows + HALO, rank), BRAIN),
                ob=small(rank),
            ),
            [pltpu.VMEM((5, rank, depth), BRAIN), pltpu.SemaphoreType.DMA((5,))],
        )

    def run_front(pieces, labels, mask):
        return call(
            functools.partial(front_body, labels, 2),
            {},
            dict(
                mask=mask, xin=xin, elow=elow, emap=front_map, mrel=mrel, trel=trel, grel=grel
            ),
            numbered(pieces),
            dict(
                gb=inner(BRAIN),
                gc=inner(BRAIN),
                va=inner(BRAIN),
                cv=inner(BRAIN),
                mixed=inner(BRAIN),
                mlow=small(rank),
                middle=wide(FLOAT),
                second=wide(BRAIN),
                glow=small(2 * rank),
            ),
            [pltpu.VMEM((4, depth, channels), BRAIN), dma],
        )

    def run_feed(q, pieces, labels, state, feed_map):
        width = count * subs[q]
        ins = dict(second=second, crel=crel, glow=glow, ob=ob, emap=feed_map)
        if state:
            ins.update(out_in=state[0], grad_in=state[1], small_in=state[2])
            outs = dict(out="out_in", grad="grad_in", small="small_in")
        else:
            outs = dict(out=wide(FLOAT), grad=wide(FLOAT), small=((rows, 3 * rank), FLOAT))
        *state, change = call(
            functools.partial(
                feed_body, labels, max(1, width // 512), subs[q] if quick else width, not state
            ),
            dict(pos=pos),
            ins,
            numbered(pieces),
            dict(outs, dmap=((rank, 3 * width), BRAIN)),
            [pltpu.VMEM((3, depth, width), BRAIN), dma],
        )
        return state, change

    state, changes = (), []
    if quick:
        f = [Block(line, f"f{q}", unit) for q, unit in enumerate(feed_units)]
        trel, xin, crel, mrel, grel, elow, ob = run_prep()
        line.hold(local, ob, feed_units[0])
        f[0].go("z")
        for k in range(1, count):
            line.start(f"local{k}", lambda v, k=k: shifted(v, k), local)
        e.wait("z")
        e.go("o")
        f[1].go("z")
        line.wait("local1", "local2", "local3")
        mine = jnp.concatenate([local] + [line[f"local{k}"] for k in range(1, count)], axis=0)
        line.start("locals", swapped, mine)
        line.wait("locals")
        front_map, *feed_maps = call(
            functools.partial(maps_body, chan, units, subs),
            dict(core=own, pos=pos),
            dict(mine=mine, theirs=line["locals"]),
            {},
            dict(
                {"front": ((2 * rank, 4 * channels), BRAIN)},
                **{f"feed{q}": ((3 * rank, count * sub), BRAIN) for q, sub in enumerate(subs)},
            ),
            [pltpu.VMEM((count * rank, 2 * span), BRAIN)],
        )
        line.hold(front_map)
        e.wait("o")
        e.go("d", "co")
        e.wait("d")
        e.go("cd")
        f[0].wait("z")
        f[0].go("o")
        f[2].go("z")
        e.wait("co", "cd")
        front, front_at = e.pieces()
        gb, gc, va, cv, mixed, mlow, middle, second, glow = run_front(
            front, front_at, line.ready(mask)
        )
        line.hold(glow)
        f[0].wait("o")
        f[0].go("d", "co")
        f[0].wait("d")
        f[0].go("cd")
        f[1].wait("z")
        f[1].go("o")
        f[0].wait("cd", "co")
        state, change = run_feed(0, *f[0].pieces(), state, line.ready(feed_maps[0]))
        changes.append(change)
        line.hold(change)
        f[1].wait("o")
        f[1].go("d", "co")
        f[1].wait("d")
        f[1].go("cd")
        f[2].wait("z")
        f[2].go("o")
        f[1].wait("cd", "co")
        state, change = run_feed(1, *f[1].pieces(), state, line.ready(feed_maps[1]))
        changes.append(change)
        line.hold(change)
        f[2].wait("o")
        f[2].go("d", "co")
        f[2].wait("d")
        f[2].go("cd")
        f[2].wait("cd", "co")
        early = Sum(line, "early", changes[:2], [])
        early.across()
        state, change = run_feed(2, *f[2].pieces(), state, feed_maps[2])
        changes.append(change)
        line.hold(change)
        line.wait("earlyacross")
        early.down()
    else:
        trel, xin, crel, mrel, grel, elow, ob = run_prep()
        gb, gc, va, cv, mixed, mlow, middle, second, glow = run_front(front, front_at, mask)
        for q, (pieces, labels) in enumerate(feed):
            state, change = run_feed(q, pieces, labels, state, feed_maps[q])
            change = change.reshape(rank, 3, count, subs[q]).swapaxes(1, 2)
            changes.append(change.reshape(rank, -1))

    output, mgrad, cgrad, edge, gcg, wide_feed, change_mix = call(
        functools.partial(middle_body, front_at, 2, chan),
        dict(tab=tab, pos=pos),
        dict(
            middle=middle,
            grad=state[1],
            small=state[2],
            crel=crel,
            mrel=mrel,
            grel=grel,
            emap=front_map,
            gc=gc,
            cv=cv,
            mixed=mixed,
            out=state[0],
            second=second,
            mlow=mlow,
        ),
        numbered(front),
        dict(
            output=wide(BRAIN),
            mgrad=wide(FLOAT),
            cgrad=inner(FLOAT),
            edge=((HALO, channels), FLOAT),
            gcg=inner(BRAIN),
            wide=((rank, 4 * depth), BRAIN),
            dmix=((rank, channels), BRAIN),
        ),
        [pltpu.VMEM((1, depth, channels), BRAIN), dma],
    )

    def run_back(mask, edge):
        return call(
            functools.partial(back_body, front_at, 2, chan),
            dict(tab=tab, pos=pos),
            dict(
                mask=mask,
                edge=edge,
                cgrad=cgrad,
                gcg=gcg,
                gb=gb,
                va=va,
                elow=elow,
                emap=front_map,
                mrel=mrel,
                mgrad=mgrad,
                trel=trel,
                grel=grel,
                xin=xin,
            ),
            numbered(front),
            dict(
                igrad=wide(BRAIN), wide=((rank, depth), BRAIN), dent=((rank, 3 * channels), BRAIN)
            ),
            [pltpu.VMEM((3, depth, channels), BRAIN), dma],
        )

    if quick:
        line.start("edge", lambda v: passed_along(v, -1), edge)
        most = Sum(line, "most", [*changes[2:], change_mix], [wide_feed])
        most.across()
        line.wait("edge", "mostacross")
        most.down()
        in_grad, wide_entry, change_entry = run_back(mask, line["edge"])
        line.hold(wide_entry)
        last = Sum(line, "last", [change_entry], [wide_entry])
        last.across()
        line.wait("earlydown1", "earlydown2", "earlydown3")
        early.out()
        line.wait("lastacross")
        last.down()
        line.wait("mostdown1", "mostdown2", "mostdown3")
        most.out()
        line.wait("lastdown1", "lastdown2", "lastdown3")
        last.out()
        most_rows = [
            (s, jnp.concatenate([a, b], axis=1))
            for (s, a), (_, b) in zip(early.result(), most.result())
        ]
        last_rows = last.result()
    else:
        in_grad, wide_entry, change_entry = run_back(mask, passed_along(edge, -1))
        most_rows = plain_sum([*changes, change_mix], wide_feed)
        last_rows = plain_sum([change_entry], wide_entry)

    def placed(pick, found, axis):
        return sum(spread(pick(row), adapter_of[s], slots, axis) for s, row in found)

    def feed_part(row, k):
        return jnp.concatenate(
            [row[:, 3 * first + k * sub : 3 * first + (k + 1) * sub] for first, sub in zip(firsts, subs)],
            axis=1,
        )

    base = 3 * units + chan

    def wide_part(row, k):
        return row[:, base + k * depth : base + (k + 1) * depth]

    return (
        output[None],
        in_grad[None],
        placed(lambda row: row[:, 3 * chan :], last_rows, 0),
        placed(lambda row: row[:, : 3 * chan].reshape(rank, 3, chan), last_rows, 0),
        placed(lambda row: row[:, 3 * units : base], most_rows, 0),
        placed(lambda row: wide_part(row, 3), most_rows, 0),
        placed(lambda row: jnp.stack([wide_part(row, 0), wide_part(row, 1)]), most_rows, 1),
        placed(lambda row: jnp.stack([feed_part(row, 0), feed_part(row, 1)]), most_rows, 1),
        placed(lambda row: feed_part(row, 2), most_rows, 0),
        placed(lambda row: wide_part(row, 2), most_rows, 0),
    )


def solution(mesh):
    return jax.shard_map(
        per_device,
        mesh=mesh,
        in_specs=(
            P("dp", ("ctx", "tensor"), None),
            P("dp", None),
            P(),
            P("dp", ("ctx", "tensor"), None),
            P(),
            P(),
            P(None, "tensor"),
            P(None, "dp", "tensor"),
            P("tensor", "dp"),
            P(None, "dp", "tensor"),
            P("tensor", "dp"),
            P(),
            P(None, None, None, "tensor"),
            P(None, None, "tensor"),
            P(),
            P(),
            P(None, None, None, "tensor"),
            P(None, None, "tensor"),
            P(),
        ),
        out_specs=(
            P("dp", ("ctx", "tensor"), None),
            P("dp", ("ctx", "tensor"), None),
            P(),
            P(None, None, None, "tensor"),
            P(None, None, "tensor"),
            P(),
            P(),
            P(None, None, None, "tensor"),
            P(None, None, "tensor"),
            P(),
        ),
        check_vma=False,
    )
```

```python
import functools

import jax
import jax.numpy as jnp
from jax import lax
from jax.experimental import pallas as pl
from jax.experimental.pallas import tpu as pltpu
from jax.sharding import PartitionSpec as P

EPSILON = 1e-05
FLOAT = jnp.float32
BRAIN = jnp.bfloat16
HALO = 16
LANES = 128
CHUNKS = 3
NN = ((1,), (0,))
NT = ((1,), (1,))
TN = ((0,), (0,))


def dot(a, b, dims=NN):
    return lax.dot_general(a, b, (dims, ((), ())), preferred_element_type=FLOAT)


def lanes(index):
    return pl.ds(pl.multiple_of(index * LANES, LANES), LANES)


class Held:
    def __init__(self):
        self.copies, self.gone = {}, []

    def begin(self, *names):
        for name in names:
            self.copies[name].start()

    def need(self, *names):
        for name in names:
            self.copies.pop(name).wait()

    def leave(self, name):
        copy = pltpu.make_async_copy(
            getattr(self, name), self.targets[name], self.out_sems.at[len(self.gone)]
        )
        copy.start()
        self.gone.append((name, copy.wait))

    def leave_tile(self, name, tile, tiles):
        ref, target, first = getattr(self, name), self.targets[name], len(self.gone)
        width = ref.shape[1] // tiles

        def copy(t):
            cols = pl.ds(t * width, width)
            if not isinstance(t, int):
                cols = pl.ds(pl.multiple_of(t * width, LANES), width)
            return pltpu.make_async_copy(
                ref.at[:, cols], target.at[:, cols], self.out_sems.at[first + t]
            )

        copy(tile).start()
        self.gone += [(name, lambda t=t: copy(t).wait()) for t in range(tiles)]


def call(body, scalars, ins, raw, outs, scratch, late=(), inner={}):
    forms = {n: o if isinstance(o, tuple) else (ins[o].shape, ins[o].dtype) for n, o in outs.items()}
    fresh = [n for n, o in outs.items() if isinstance(o, tuple)]
    raw_names = list(raw)

    def kernel(*refs):
        refs = list(refs)
        take = lambda count: [refs.pop(0) for _ in range(count)]
        r = Held()
        for name, ref in zip(scalars, take(len(scalars))):
            setattr(r, name, ref)
        sources = dict(zip(ins, take(len(ins))))
        for name, ref in zip(raw_names, take(len(raw_names))):
            setattr(r, name, ref)
        r.targets = dict(zip(outs, take(len(outs))))
        for name, ref in zip(ins, take(len(ins))):
            setattr(r, name, ref)
        for name, ref in zip(fresh + list(inner), take(len(fresh) + len(inner))):
            setattr(r, name, ref)
        for name, origin in outs.items():
            if not isinstance(origin, tuple):
                setattr(r, name, getattr(r, origin))
        in_sems, r.out_sems = take(2)
        r.scratch = refs
        for k, (name, source) in enumerate(sources.items()):
            r.copies[name] = pltpu.make_async_copy(source, getattr(r, name), in_sems.at[k])
            if name not in late:
                r.copies[name].start()
        body(r)
        for name in outs:
            if name not in [n for n, _ in r.gone]:
                r.leave(name)
        for _, wait in r.gone:
            wait()
        r.need(*list(r.copies))

    hbm = pl.BlockSpec(memory_space=pltpu.HBM)
    return pl.pallas_call(
        kernel,
        out_shape=[jax.ShapeDtypeStruct(*form) for form in forms.values()],
        in_specs=[pl.BlockSpec(memory_space=pltpu.SMEM)] * len(scalars)
        + [hbm] * (len(ins) + len(raw)),
        out_specs=[hbm] * len(outs),
        scratch_shapes=[pltpu.VMEM(v.shape, v.dtype) for v in ins.values()]
        + [pltpu.VMEM(*forms[n]) for n in fresh]
        + [pltpu.VMEM(*form) for form in inner.values()]
        + [pltpu.SemaphoreType.DMA((max(1, len(ins)),)), pltpu.SemaphoreType.DMA((32,))]
        + list(scratch),
        compiler_params=pltpu.CompilerParams(vmem_limit_bytes=54 << 20),
        cost_estimate=pl.CostEstimate(flops=1, bytes_accessed=1, transcendentals=0),
    )(*scalars.values(), *ins.values(), *raw.values())


def prep_body(r):
    rank = r.elow.shape[1]
    a = r.pick[0]
    maps, sems = r.scratch
    sources = (r.er.at[a], r.gr.at[0, a], r.gr.at[1, a], r.me.at[a], r.oe.at[a])
    copies = [
        pltpu.make_async_copy(source, maps.at[k], sems.at[k]) for k, source in enumerate(sources)
    ]
    for copy in copies:
        copy.start()
    r.need("tok", "halo")
    t32 = r.tok[...].astype(FLOAT)
    inv = lax.rsqrt(jnp.mean(t32 * t32, axis=-1, keepdims=True) + EPSILON)
    h32 = r.halo[...].astype(FLOAT)
    hinv = lax.rsqrt(jnp.mean(h32 * h32, axis=-1, keepdims=True) + EPSILON)
    r.need("cot", "gains")
    for copy in copies:
        copy.wait()
    for b in range(r.tok.shape[1] // LANES):
        src = lanes(r.tab[b])
        dst = slice(b * LANES, (b + 1) * LANES)
        part = r.tok[:, src]
        gain = r.gains[:, src]
        r.trel[:, dst] = part
        r.xin[HALO:, dst] = (part.astype(FLOAT) * inv * gain[0:1]).astype(BRAIN)
        r.xin[:HALO, dst] = (r.halo[:, src].astype(FLOAT) * hinv * gain[0:1]).astype(BRAIN)
        r.crel[:, dst] = r.cot[:, src]
        for k in range(5):
            r.mrel[k * rank : (k + 1) * rank, dst] = maps[k, :, src]
        r.grel[:, dst] = gain
    for name in ("trel", "xin", "crel"):
        r.leave(name)
    r.elow[...] = dot(r.xin[...], r.mrel[0:rank], NT).astype(BRAIN)
    r.ob[...] = dot(r.crel[...], r.mrel[4 * rank : 5 * rank], NT).astype(BRAIN)


def front_pack_body(r):
    half = r.unit.shape[1]
    rows = pl.ds(pl.multiple_of(r.core[0] * half, half), half)
    r.need("entry")
    for k in range(3):
        r.unit[k] = r.entry[k, rows, :]
    r.need("mixer")
    r.unit[3] = r.mixer[:, rows].astype(FLOAT).T.astype(BRAIN)


def feed_pack_body(count, r):
    units = [getattr(r, f"unit{q}") for q in range(count)]
    half = units[0].shape[1]
    rows = pl.ds(pl.multiple_of(r.core[0] * half, half), half)
    r.need("gates", "outlet")
    first = 0
    for q, unit in enumerate(units):
        cols = slice(first, first + unit.shape[2])
        for k in range(2):
            unit[k] = r.gates[k, rows, cols]
        unit[2] = r.outlet[cols, rows].astype(FLOAT).T.astype(BRAIN)
        r.leave(f"unit{q}")
        first += unit.shape[2]


def half_kernel(core, came, half, held, sems):
    count = half.shape[0]
    first = core[0] * count
    ins = [pltpu.make_async_copy(came.at[first + z], held.at[z], sems.at[0, z]) for z in range(count)]
    outs = [pltpu.make_async_copy(held.at[z], half.at[z], sems.at[1, z]) for z in range(count)]
    for copy in ins:
        copy.start()
    for z in range(count):
        ins[z].wait()
        outs[z].start()
    for copy in outs:
        copy.wait()


def local_body(r):
    whole, sems = r.scratch
    chan = r.taps.shape[1]
    units = r.orr.shape[2]
    a = r.pick[0]
    first = 5 * chan
    rank, half = r.out.shape
    copies = [
        pltpu.make_async_copy(source, whole.at[:, pl.ds(at, size)], sems.at[k])
        for k, (source, at, size) in enumerate(
            (
                (r.mr.at[a], 3 * chan, chan),
                (r.ge.at[0, a], first, units),
                (r.ge.at[1, a], first + units, units),
                (r.orr.at[a], first + 2 * units, units),
            )
        )
    ]
    for copy in copies:
        copy.start()
    r.need("ee", "taps")
    whole[:, : 3 * chan] = r.ee[...]
    whole[:, 4 * chan : 5 * chan] = jnp.zeros((rank, chan), BRAIN)
    whole[0:3, 4 * chan : 5 * chan] = r.taps[...]
    whole[:, first + 3 * units :] = jnp.zeros((rank, whole.shape[1] - first - 3 * units), BRAIN)
    for copy in copies:
        copy.wait()
    r.out[...] = whole[:, pl.ds(pl.multiple_of(r.core[0] * half, LANES), half)]


def maps_body(chan, units, subs, r):
    [side] = r.scratch
    front = r.front
    rank = front.shape[0] // 2
    half = r.mine.shape[1]
    count = r.mine.shape[0] // rank
    channels = chan * count
    r.need("mine", "theirs")
    side[:, pl.ds(pl.multiple_of(r.core[0] * half, LANES), half)] = r.mine[...]
    side[:, pl.ds(pl.multiple_of((1 - r.core[0]) * half, LANES), half)] = r.theirs[...]
    for s in range(count):
        own = slice(s * rank, (s + 1) * rank)
        z = r.pos[s]
        for k in range(4):
            at = pl.ds(pl.multiple_of(k * channels + z * chan, LANES), chan)
            front[0:rank, at] = side[own, k * chan : (k + 1) * chan]
        at = pl.ds(pl.multiple_of(z * chan, LANES), chan)
        front[rank : 2 * rank, at] = side[own, 4 * chan : 5 * chan]
        first = 5 * chan
        for q, sub in enumerate(subs):
            feed = getattr(r, f"feed{q}")
            for k in range(3):
                at = first + k * units
                to = pl.ds(pl.multiple_of(z * sub, LANES), sub)
                feed[k * rank : (k + 1) * rank, to] = side[own, at : at + sub]
            first += sub


def fetch(r, count, labels, w, sems, planes):
    pieces = [getattr(r, f"piece{p}") for p in range(len(labels))]
    width = pieces[0].shape[3]

    def copies(z):
        cols = pl.ds(pl.multiple_of(z * width, LANES), width)
        found = []
        for ref, label in zip(pieces, labels):
            for h in range(ref.shape[0] // count):
                size = ref.shape[2]
                place = label if isinstance(label, tuple) else (label + h * (size // LANES),)
                size //= len(place)
                for k, slot in enumerate(place):
                    if not isinstance(slot, int):
                        slot = slot(r.core[0])
                    source = ref.at[h * count + z, planes, pl.ds(k * size, size)]
                    target = pl.ds(pl.multiple_of(slot * LANES, LANES), size)
                    target = w.at[:, target, cols]
                    found.append(pltpu.make_async_copy(source, target, sems.at[z, len(found)]))
        return found

    for z in range(count):
        for copy in copies(z):
            copy.start()

    def wait(z):
        for copy in copies(z):
            copy.wait()

    def arrive(t, tile):
        need = lambda t: (t * tile + width - 1) // width
        lax.fori_loop(need(t), need(t + 1), lambda z, c: (wait(z), c)[1], 0)

    return arrive


def front_body(labels, tiles, r):
    w, sems, low = r.scratch
    rank = r.elow.shape[1]
    rows = r.trel.shape[0]
    channels = w.shape[2]
    width = channels // tiles
    arrive = fetch(r, sems.shape[0], labels, w, sems, slice(0, 4))
    r.begin("trel", "grel")
    r.need("mask", "xin", "elow", "emap", "mrel")
    r.middle[...] = jnp.zeros_like(r.middle)
    low[...] = jnp.zeros_like(low)

    def step(t, carry):
        arrive(t, width)
        col = pl.ds(pl.multiple_of(t * width, LANES), width)
        wide = lambda k: pl.ds(pl.multiple_of(k * channels + t * width, LANES), width)
        project = lambda k: dot(r.xin[...], w[k, :, col]) + dot(
            r.elow[...], r.emap[0:rank, wide(k)]
        )
        b = project(0)
        v = project(2)
        c = project(1)[HALO:]
        product = b * v
        r.gb[:, col] = b[HALO:].astype(BRAIN)
        r.va[:, col] = v[HALO:].astype(BRAIN)
        r.gc[:, col] = c.astype(BRAIN)
        taps = r.emap[rank : 2 * rank, col].astype(FLOAT)
        conv = (
            taps[0:1] * product[HALO:]
            + taps[1:2] * r.mask[0:rows, 0:1] * pltpu.roll(product, 1, 0)[HALO:]
            + taps[2:3] * r.mask[0:rows, 1:2] * pltpu.roll(product, 2, 0)[HALO:]
        )
        r.cv[:, col] = conv.astype(BRAIN)
        mix = (c * conv).astype(BRAIN)
        r.mixed[:, col] = mix
        for name in ("gb", "gc", "va", "cv", "mixed"):
            r.leave_tile(name, t, tiles)
        r.middle[...] += dot(mix, w[3, :, col], NT)
        low[...] += dot(mix, r.emap[0:rank, wide(3)], NT)
        return carry

    lax.fori_loop(0, tiles, step, 0)
    mlow = low[...].astype(BRAIN)
    r.mlow[...] = mlow
    r.need("trel", "grel")
    mid = r.middle[...] + r.trel[...].astype(FLOAT) + dot(mlow, r.mrel[3 * rank : 4 * rank])
    r.middle[...] = mid
    r.leave("middle")
    inv = lax.rsqrt(jnp.mean(mid * mid, axis=-1, keepdims=True) + EPSILON)
    x2 = (mid * inv * r.grel[1:2]).astype(BRAIN)
    r.second[...] = x2
    r.leave("second")
    r.glow[...] = dot(x2, r.mrel[rank : 3 * rank], NT).astype(BRAIN)


def feed_body(labels, tiles, sub, first, r):
    w, sems = r.scratch
    rank = r.ob.shape[1]
    width = w.shape[2] // tiles
    arrive = fetch(r, sems.shape[0], labels, w, sems, slice(0, 3))
    r.need("second", "crel", "glow", "ob", "emap")
    if first:
        r.out[...] = jnp.zeros_like(r.out)
        r.grad[...] = jnp.zeros_like(r.grad)
        r.small[...] = jnp.zeros_like(r.small)
    else:
        r.begin("small_in", "out_in", "grad_in")

    def step(t, carry):
        arrive(t, width)
        col = pl.ds(pl.multiple_of(t * width, LANES), width)
        eg, eu, ro = (r.emap[i * rank : (i + 1) * rank, col] for i in range(3))
        wg, wu, wo = (w[i, :, col] for i in range(3))
        x = r.second[...]
        lg, lu, ob = r.glow[:, 0:rank], r.glow[:, rank : 2 * rank], r.ob[...]
        g = dot(x, wg) + dot(lg, eg)
        u = dot(x, wu) + dot(lu, eu)
        h_grad = dot(r.crel[...], wo) + dot(ob, ro)
        sigma = 1.0 / (1.0 + jnp.exp(-g))
        act = g * sigma
        h = (act * u).astype(BRAIN)
        gg = (h_grad * u * (sigma * (1.0 + g * (1.0 - sigma)))).astype(BRAIN)
        ug = (h_grad * act).astype(BRAIN)
        if not first:
            pl.when(t == 0)(lambda: r.need("out_in", "grad_in", "small_in"))
        r.out[...] += dot(h, wo, NT)
        r.grad[...] += dot(gg, wg, NT) + dot(ug, wu, NT)
        r.small[:, 0:rank] += dot(gg, eg, NT)
        r.small[:, rank : 2 * rank] += dot(ug, eu, NT)
        r.small[:, 2 * rank : 3 * rank] += dot(h, ro, NT)
        changes = (dot(lg, gg, TN), dot(lu, ug, TN), dot(ob, h, TN))
        for j in range(0, width, LANES):
            at = t * width + j
            owner = at // sub
            for k in range(3):
                to = r.pos[owner] * (3 * sub) + k * sub + (at - owner * sub)
                to = pl.ds(pl.multiple_of(to, LANES), LANES)
                r.dmap[:, to] = changes[k][:, j : j + LANES].astype(r.dmap.dtype)
        return carry

    lax.fori_loop(0, tiles, step, 0)


def pulled(v, gain, grad):
    inv = lax.rsqrt(jnp.mean(v * v, axis=-1, keepdims=True) + EPSILON)
    scaled = grad * gain
    along = jnp.mean(v * scaled, axis=-1, keepdims=True)
    return inv * scaled - v * (inv * inv * inv * along)


def middle_body(labels, tiles, chan, parts, r):
    w, sems = r.scratch
    rank = r.mlow.shape[1]
    channels = w.shape[2]
    width = channels // tiles
    depth = w.shape[1]
    arrive = fetch(r, sems.shape[0], labels, w, sems, slice(3, 4))
    late = [f"part{q}" for q in range(parts)]
    r.begin("gc", "cv", "mixed", "out", "second", "mlow", *late)
    r.need("middle", "grad", "small", "crel", "mrel", "grel", "emap")
    gback = r.small[:, 0 : 2 * rank].astype(BRAIN)
    olow = r.small[:, 2 * rank : 3 * rank].astype(BRAIN)
    mid = r.middle[...]
    sgrad = r.grad[...] + dot(gback, r.mrel[rank : 3 * rank])
    mg = r.crel[...].astype(FLOAT) + pulled(mid, r.grel[1:2], sgrad)
    r.mgrad[...] = mg
    r.leave("mgrad")
    mlo = mg.astype(BRAIN)
    r.second_low[...] = mlo
    r.back[...] = dot(mlo, r.mrel[3 * rank : 4 * rank], NT).astype(BRAIN)
    r.need("gc", "cv", "mixed", *late)
    mix = 0
    for name in late:
        part = getattr(r, name)
        r.pack[:, mix : mix + part.shape[1]] = part[...]
        mix += part.shape[1]

    def step(t, carry):
        arrive(t, width)
        col = pl.ds(pl.multiple_of(t * width, LANES), width)
        own = pl.ds(pl.multiple_of(3 * channels + t * width, LANES), width)
        mx = dot(r.second_low[...], w[0, :, col]) + dot(r.back[...], r.emap[0:rank, own])
        r.gcg[:, col] = (mx * r.cv[:, col].astype(FLOAT)).astype(BRAIN)
        cg = mx * r.gc[:, col].astype(FLOAT)
        r.cgrad[:, col] = cg.astype(BRAIN)
        for name in ("gcg", "cgrad"):
            r.leave_tile(name, t, tiles)
        r.edge[:, col] = cg[:HALO].astype(BRAIN)
        change = dot(r.back[...], r.mixed[:, col], TN).astype(BRAIN)
        for j in range(0, width, LANES):
            at = t * width + j
            owner = at // chan
            to = mix + r.pos[owner] * chan + at - owner * chan
            r.pack[:, pl.ds(pl.multiple_of(to, LANES), LANES)] = change[:, j : j + LANES]
        return carry

    lax.fori_loop(0, tiles, step, 0)
    r.leave("edge")
    wide = mix + channels
    r.need("second", "mlow")
    dff = jnp.concatenate([dot(gback, r.second[...], TN), dot(olow, r.crel[...], TN)], axis=0)
    dff = jnp.concatenate([dff, dot(r.mlow[...], r.second_low[...], TN)], axis=0).astype(BRAIN)
    for b in range(depth // LANES):
        src = slice(b * LANES, (b + 1) * LANES)
        for k in range(4):
            to = pl.ds(pl.multiple_of(wide + k * depth + r.tab[b] * LANES, LANES), LANES)
            r.pack[:, to] = dff[k * rank : (k + 1) * rank, src]
    r.leave("pack")
    r.need("out")
    full = r.middle[...] + r.out[...] + dot(olow, r.mrel[4 * rank : 5 * rank])
    for b in range(depth // LANES):
        r.output[:, lanes(r.tab[b])] = full[:, b * LANES : (b + 1) * LANES].astype(BRAIN)


def back_body(labels, tiles, chan, r):
    w, sems, fgrad, back = r.scratch
    rank = r.elow.shape[1]
    rows = r.trel.shape[0]
    channels = w.shape[2]
    width = channels // tiles
    arrive = fetch(r, sems.shape[0], labels, w, sems, slice(0, 3))
    r.begin("mgrad", "trel", "grel", "xin")
    r.need("mask", "edge", "cgrad", "gcg", "gb", "va", "elow", "emap", "mrel")
    total = rows + HALO
    fgrad[...] = jnp.zeros_like(fgrad)
    back[...] = jnp.zeros_like(back)

    def step(t, carry):
        arrive(t, width)
        col = pl.ds(pl.multiple_of(t * width, LANES), width)
        taps = r.emap[rank : 2 * rank, col].astype(FLOAT)
        cg = jnp.concatenate([r.cgrad[:, col], r.edge[:, col]], axis=0).astype(FLOAT)
        pg = (
            taps[0:1] * cg
            + pltpu.roll(taps[1:2] * r.mask[:, 0:1] * cg, total - 1, 0)
            + pltpu.roll(taps[2:3] * r.mask[:, 1:2] * cg, total - 2, 0)
        )[:rows]
        parts = (
            (pg * r.va[:, col].astype(FLOAT)).astype(BRAIN),
            r.gcg[:, col],
            (pg * r.gb[:, col].astype(FLOAT)).astype(BRAIN),
        )
        for k in range(3):
            fgrad[...] += dot(parts[k], w[k, :, col], NT)
            wide = pl.ds(pl.multiple_of(k * channels + t * width, LANES), width)
            back[...] += dot(parts[k], r.emap[0:rank, wide], NT)
            change = dot(r.elow[HALO:, :], parts[k], TN).astype(BRAIN)
            for j in range(0, width, LANES):
                at = t * width + j
                owner = at // chan
                to = r.pos[owner] * 3 * chan + k * chan + at - owner * chan
                r.pack[:, pl.ds(pl.multiple_of(to, LANES), LANES)] = change[:, j : j + LANES]
        return carry

    lax.fori_loop(0, tiles, step, 0)
    low = back[...].astype(BRAIN)
    first = fgrad[...] + dot(low, r.mrel[0:rank])
    r.need("mgrad", "trel", "grel", "xin")
    dred = dot(low, r.xin[HALO:, :], TN).astype(BRAIN)
    for b in range(w.shape[1] // LANES):
        to = pl.ds(pl.multiple_of(3 * channels + r.tab[b] * LANES, LANES), LANES)
        r.pack[:, to] = dred[:, b * LANES : (b + 1) * LANES]
    r.leave("pack")
    full = r.mgrad[...] + pulled(r.trel[...].astype(FLOAT), r.grel[0:1], first)
    for b in range(w.shape[1] // LANES):
        r.igrad[:, lanes(r.tab[b])] = full[:, b * LANES : (b + 1) * LANES].astype(BRAIN)


def shifted(block, distance):
    size = lax.axis_size("tensor")
    return lax.ppermute(block, "tensor", [(i, (i + distance) % size) for i in range(size)])


def flipped(block, bit):
    return lax.ppermute(block, "dp", [(i, i ^ bit) for i in range(lax.axis_size("dp"))])


def swapped(block):
    return lax.ppermute(block, "ctx", [(0, 1), (1, 0)])


def turned(block, bits):
    route = [(2 * d + c, 2 * (d ^ bits[c]) + c) for d in range(lax.axis_size("dp")) for c in range(2)]
    return lax.ppermute(block, ("dp", "ctx"), route)


def passed_along(block, distance):
    axes = ("ctx", "tensor")
    size = lax.axis_size("ctx") * lax.axis_size("tensor")
    route = [(i, i + distance) for i in range(size) if 0 <= i + distance < size]
    return lax.ppermute(block, axes, route)


def after(value, *others):
    return lax.optimization_barrier((value, others))[0]


def shape_of(chip, core):
    near = jnp.where(core == 0, 1, 2)
    places = [(0, 0), (0, 1), (near, 0), (near, 1), (3 - near, 0), (3 - near, 1)]
    places += [(3, core), (3, 1 - core)]
    return jnp.stack([(chip ^ e) * 2 + h for e, h in places]).astype(jnp.int32)


class Line:
    def __init__(self):
        self.held = []
        self.values = {}

    def wait(self, *names):
        for name in names:
            self.held.append(self.values[name])
        self.held = self.held[-3:]

    def hold(self, *values):
        self.held = (self.held + list(values))[-3:]

    def ready(self, value):
        return after(value, *self.held) if self.held else value

    def start(self, name, move, value):
        self.values[name] = move(self.ready(value))

    def __getitem__(self, name):
        return self.values[name]


class Block:
    def __init__(self, line, name, unit, early):
        self.line, self.name, self.unit, self.early = line, name, unit, early

    def at(self, step):
        return self.line[self.name + step]

    def go(self, *steps):
        for step in steps:
            self.line.start(self.name + step, *self.plan(step))

    def wait(self, *steps):
        self.line.wait(*(self.name + step for step in steps))

    def plan(self, step):
        if step == "p":
            return (lambda v: turned(v, (1, 2))), self.unit
        if step == "z" and self.early:
            base = jnp.concatenate([self.unit, self.at("p")], axis=1)
            return (lambda v: lax.all_gather(v, "tensor", axis=0)), base
        if step == "z":
            return (lambda v: lax.all_gather(v, ("ctx", "tensor"), axis=0)), self.unit
        if step == "a":
            return (lambda v: turned(v, (2, 1))), self.at("z")
        if step == "c":
            return swapped, self.at("z")
        if step == "o":
            return (lambda v: turned(v, (1, 2))), self.at("z")
        if step == "d":
            came = self.at("o")
            shape = (came.shape[0] // 2,) + came.shape[1:]
            half = pl.pallas_call(
                half_kernel,
                out_shape=jax.ShapeDtypeStruct(shape, BRAIN),
                in_specs=[
                    pl.BlockSpec(memory_space=pltpu.SMEM),
                    pl.BlockSpec(memory_space=pltpu.HBM),
                ],
                out_specs=pl.BlockSpec(memory_space=pltpu.HBM),
                scratch_shapes=[
                    pltpu.VMEM(shape, BRAIN),
                    pltpu.SemaphoreType.DMA((2, shape[0])),
                ],
                cost_estimate=pl.CostEstimate(flops=1, bytes_accessed=1, transcendentals=0),
            )(self.line.ready(lax.axis_index("ctx")[None].astype(jnp.int32)), came)
            return (lambda v: turned(v, (2, 1))), half
        return swapped, self.at(step[1:])

    def pieces(self):
        if not self.early:
            return [self.at(n) for n in ("z", "o", "co", "d", "cd")], (0, 2, 4, 6, 7)
        labels = (
            (lambda c: c, lambda c: 2 + c),
            (lambda c: 4 + c, 6),
            (lambda c: 1 - c, lambda c: 5 - c),
            (lambda c: 3 - c, 7),
        )
        return [self.at(n) for n in ("z", "a", "c", "ca")], labels


def spread(update, adapter, slots, axis):
    onehot = (lax.broadcasted_iota(jnp.int32, (slots,), 0) == adapter).astype(FLOAT)
    layout = [1] * (update.ndim + 1)
    layout[axis] = slots
    return jnp.expand_dims(update, axis) * onehot.reshape(layout)


def rounded(value):
    return lax.reduce_precision(value, 8, 7).astype(BRAIN)


class Sum:
    def __init__(self, line, name, mine, widths):
        self.line, self.name, self.mine, self.widths = line, name, mine, widths
        self.count = lax.axis_size("tensor")

    def across(self):
        self.line.start(self.name + "across", swapped, self.mine)

    def down(self):
        pair = self.mine.astype(FLOAT) + self.line[self.name + "across"].astype(FLOAT)
        pair = rounded(pair)
        rest = pair[:, sum(self.widths) * self.count :]
        self.parts = []
        for s in range(self.count):
            first, part = 0, []
            for width in self.widths:
                part.append(pair[:, first + s * width : first + (s + 1) * width])
                first += width * self.count
            self.parts.append(jnp.concatenate(part + [rest], axis=1))
        for s in range(1, self.count):
            self.line.start(self.name + f"down{s}", lambda v, s=s: shifted(v, -s), self.parts[s])

    def out(self):
        terms = [self.parts[0]] + [self.line[self.name + f"down{s}"] for s in range(1, self.count)]
        stack = jnp.stack(terms)
        at = lax.axis_index("tensor")
        self.total = sum(
            lax.dynamic_index_in_dim(stack, (k - at) % self.count, 0, keepdims=False).astype(FLOAT)
            for k in range(self.count)
        )
        self.total = rounded(self.total)
        for e in range(1, lax.axis_size("dp")):
            self.line.start(self.name + f"out{e}", lambda v, e=e: flipped(v, e), self.total)

    def result(self):
        here = lax.axis_index("dp")
        rows = [(here, self.total)]
        for e in range(1, lax.axis_size("dp")):
            rows.append((here ^ e, self.line[self.name + f"out{e}"]))
        return [(s, row.astype(FLOAT)) for s, row in rows]


def plain_sum(mine, widths):
    count = lax.axis_size("tensor")
    at = lax.axis_index("tensor")
    mine = lax.psum(mine.astype(FLOAT), ("ctx", "tensor"))
    first, parts = 0, []
    for width in widths:
        parts.append(lax.dynamic_slice_in_dim(mine, first + at * width, width, 1))
        first += width * count
    rows = lax.all_gather(jnp.concatenate([*parts, mine[:, first:]], axis=1), "dp", axis=0)
    return [(s, rows[s]) for s in range(lax.axis_size("dp"))]


def chosen(table, adapter, axis):
    return lax.dynamic_index_in_dim(table, adapter, axis, keepdims=False)


def chunk_widths(units):
    if units == 1152:
        return (512, 384, 256)
    return (units // 3,) * 3


def per_device(
    tokens,
    segments,
    adapter_of,
    cotangent,
    first_gain,
    second_gain,
    conv_taps,
    entry_weight,
    mixer_weight,
    gates_weight,
    outlet_weight,
    entry_reduce,
    entry_expand,
    mixer_reduce,
    mixer_expand,
    gates_reduce,
    gates_expand,
    outlet_reduce,
    outlet_expand,
):
    slots, rank, depth = entry_reduce.shape
    seqs, cores, count = (lax.axis_size(a) for a in ("dp", "ctx", "tensor"))
    here, core, at = (lax.axis_index(a) for a in ("dp", "ctx", "tensor"))
    rows = tokens.shape[1]
    blocks = depth // LANES
    chan = mixer_weight.shape[0]
    units = outlet_weight.shape[0]
    channels = chan * count
    subs = chunk_widths(units)
    firsts = [sum(subs[:q]) for q in range(len(subs))]
    quick = (
        seqs == 4
        and cores == 2
        and count == 4
        and depth == seqs * cores * LANES
        and all(sub % LANES == 0 for sub in subs)
    )
    line = Line()

    adapter = adapter_of[here]
    pick = adapter[None].astype(jnp.int32)
    own = core[None].astype(jnp.int32)
    expand = chosen(entry_expand, adapter, 0).reshape(rank, 3 * chan)

    if quick:
        half = depth // seqs // cores
        [front_unit] = call(
            front_pack_body,
            dict(core=own),
            dict(entry=entry_weight, mixer=mixer_weight),
            {},
            dict(unit=((4, half, chan), BRAIN)),
            [],
        )
        line.start("halo", lambda v: passed_along(v, 1), tokens[0, rows - HALO :])
        halo = line["halo"]
        e = Block(line, "e", front_unit, False)
        e.go("z")
        span = 5 * chan + 3 * units
        span = (span + 2 * LANES - 1) // (2 * LANES) * LANES
        [local] = call(
            local_body,
            dict(pick=pick, core=after(own, front_unit)),
            dict(ee=expand, taps=conv_taps),
            dict(mr=mixer_reduce, ge=gates_expand, orr=outlet_reduce),
            dict(out=((rank, span), BRAIN)),
            [pltpu.VMEM((rank, 2 * span), BRAIN), pltpu.SemaphoreType.DMA((4,))],
        )
        feed_units = call(
            functools.partial(feed_pack_body, len(subs)),
            dict(core=after(own, front_unit)),
            dict(gates=gates_weight, outlet=outlet_weight),
            {},
            {f"unit{q}": ((3, half, sub), BRAIN) for q, sub in enumerate(subs)},
            [],
        )
        tab = shape_of(here, core)
        pos = ((at - jnp.arange(count)) % count).astype(jnp.int32)
    else:
        halo = passed_along(tokens[0, rows - HALO :], 1)
        local = jnp.concatenate(
            [
                expand,
                chosen(mixer_reduce, adapter, 0),
                jnp.pad(conv_taps, ((0, rank - 3), (0, 0))),
                chosen(gates_expand, adapter, 1)[0],
                chosen(gates_expand, adapter, 1)[1],
                chosen(outlet_reduce, adapter, 0),
            ],
            axis=1,
        )

        def full(block, rows_axis, cols_axis):
            block = lax.all_gather(block, "dp", axis=rows_axis, tiled=True)
            return lax.all_gather(block, "tensor", axis=cols_axis, tiled=True)

        front = [
            jnp.concatenate(
                [full(entry_weight, 1, 2), full(mixer_weight, 1, 0).T[None]], axis=0
            )
        ]
        front = [front[0][None]]
        front_at = (0,)
        pos = jnp.arange(count, dtype=jnp.int32)
        whole = jnp.concatenate(
            [full(gates_weight, 1, 2), full(outlet_weight, 1, 0).T[None]], axis=0
        ).reshape(3, depth, count, units)
        feed = [
            ([whole[:, :, :, first : first + sub].reshape(1, 3, depth, count * sub)], (0,))
            for first, sub in zip(firsts, subs)
        ]
        tab = jnp.arange(blocks, dtype=jnp.int32)
        side = list(lax.all_gather(local, "tensor", axis=0))

        def columns(first, size):
            return jnp.concatenate([part[:, first : first + size] for part in side], axis=1)

        low = jnp.concatenate([columns(k * chan, chan) for k in range(4)], axis=1)
        taps = jnp.pad(columns(4 * chan, chan), ((0, 0), (0, 3 * channels)))
        front_map = jnp.concatenate([low, taps], axis=0)
        feed_maps = [
            jnp.concatenate([columns(5 * chan + k * units + first, sub) for k in range(3)], axis=0)
            for first, sub in zip(firsts, subs)
        ]

    index = core * count + at
    seg = jnp.concatenate(
        [jnp.full((2,), -1, jnp.int32), segments[0], jnp.full((HALO,), -2, jnp.int32)]
    )
    seg = lax.dynamic_slice_in_dim(seg, index * rows, rows + HALO + 2)
    mask = jnp.stack([seg[1:-1] == seg[2:], seg[:-2] == seg[2:]], axis=1).astype(FLOAT)
    gains = jnp.stack([first_gain, second_gain]).astype(FLOAT)

    wide = lambda dtype: ((rows, depth), dtype)
    inner = lambda dtype: ((rows, channels), dtype)
    small = lambda n: ((rows, n), BRAIN)
    dma = pltpu.SemaphoreType.DMA((count if quick else 1, blocks))
    numbered = lambda pieces: {f"piece{p}": piece for p, piece in enumerate(pieces)}

    def run_prep():
        return call(
            prep_body,
            dict(pick=pick, tab=tab),
            dict(tok=tokens[0], halo=halo, cot=cotangent[0], gains=gains),
            dict(er=entry_reduce, gr=gates_reduce, me=mixer_expand, oe=outlet_expand),
            dict(
                trel=wide(BRAIN),
                xin=((rows + HALO, depth), BRAIN),
                crel=wide(BRAIN),
                mrel=((5 * rank, depth), BRAIN),
                grel=(gains.shape, FLOAT),
                elow=((rows + HALO, rank), BRAIN),
                ob=small(rank),
            ),
            [pltpu.VMEM((5, rank, depth), BRAIN), pltpu.SemaphoreType.DMA((5,))],
        )

    def run_front(pieces, labels, mask):
        return call(
            functools.partial(front_body, labels, 2),
            {},
            dict(
                mask=mask, xin=xin, elow=elow, emap=front_map, mrel=mrel, trel=trel, grel=grel
            ),
            numbered(pieces),
            dict(
                gb=inner(BRAIN),
                gc=inner(BRAIN),
                va=inner(BRAIN),
                cv=inner(BRAIN),
                mixed=inner(BRAIN),
                mlow=small(rank),
                middle=wide(FLOAT),
                second=wide(BRAIN),
                glow=small(2 * rank),
            ),
            [pltpu.VMEM((4, depth, channels), BRAIN), dma, pltpu.VMEM((rows, rank), FLOAT)],
            late=("trel", "grel"),
        )

    def run_feed(q, pieces, labels, state, feed_map):
        width = count * subs[q]
        ins = dict(second=second, crel=crel, glow=glow, ob=ob, emap=feed_map)
        if state:
            ins.update(out_in=state[0], grad_in=state[1], small_in=state[2])
            outs = dict(out="out_in", grad="grad_in", small="small_in")
        else:
            outs = dict(out=wide(FLOAT), grad=wide(FLOAT), small=((rows, 3 * rank), FLOAT))
        *state, change = call(
            functools.partial(
                feed_body, labels, max(1, width // 512), subs[q] if quick else width, not state
            ),
            dict(pos=pos, core=own),
            ins,
            numbered(pieces),
            dict(outs, dmap=((rank, 3 * width), BRAIN)),
            [pltpu.VMEM((3, depth, width), BRAIN), dma],
            late=("out_in", "grad_in", "small_in"),
        )
        return state, change

    state, changes = (), []
    if quick:
        f = [Block(line, f"f{q}", unit, q > 0) for q, unit in enumerate(feed_units)]
        f[1].go("p")
        f[2].go("p")
        trel, xin, crel, mrel, grel, elow, ob = run_prep()
        line.hold(local, ob)
        f[0].go("z")
        for k in range(1, count):
            line.start(f"local{k}", lambda v, k=k: shifted(v, k), local)
        f[1].wait("p")
        f[2].wait("p")
        e.wait("z")
        e.go("o")
        f[1].go("z")
        line.wait("local1", "local2", "local3")
        mine = jnp.concatenate([local] + [line[f"local{k}"] for k in range(1, count)], axis=0)
        line.start("locals", swapped, mine)
        line.wait("locals")
        front_map, *feed_maps = call(
            functools.partial(maps_body, chan, units, subs),
            dict(core=own, pos=pos),
            dict(mine=mine, theirs=line["locals"]),
            {},
            dict(
                {"front": ((2 * rank, 4 * channels), BRAIN)},
                **{f"feed{q}": ((3 * rank, count * sub), BRAIN) for q, sub in enumerate(subs)},
            ),
            [pltpu.VMEM((count * rank, 2 * span), BRAIN)],
        )
        line.hold(front_map)
        e.wait("o")
        e.go("d", "co")
        f[2].go("z")
        e.wait("d")
        e.go("cd")
        f[0].wait("z")
        f[0].go("o")
        e.wait("co", "cd")
        front, front_at = e.pieces()
        gb, gc, va, cv, mixed, mlow, middle, second, glow = run_front(
            front, front_at, line.ready(mask)
        )
        line.hold(glow)
        f[0].wait("o")
        f[0].go("d", "co")
        f[0].wait("d")
        f[0].go("cd")
        f[1].wait("z")
        f[1].go("a", "c")
        f[0].wait("cd", "co")
        state, change = run_feed(0, *f[0].pieces(), state, line.ready(feed_maps[0]))
        changes.append(change)
        line.hold(change)
        f[1].wait("a")
        f[1].go("ca")
        f[2].wait("z")
        f[2].go("a", "c")
        f[1].wait("c", "ca")
        state, change = run_feed(1, *f[1].pieces(), state, line.ready(feed_maps[1]))
        changes.append(change)
        line.hold(change)
        f[2].wait("a")
        f[2].go("ca")
        f[2].wait("c", "ca")
        state, change = run_feed(2, *f[2].pieces(), state, line.ready(feed_maps[2]))
        changes.append(change)
        line.hold(change)
    else:
        trel, xin, crel, mrel, grel, elow, ob = run_prep()
        gb, gc, va, cv, mixed, mlow, middle, second, glow = run_front(front, front_at, mask)
        for q, (pieces, labels) in enumerate(feed):
            state, change = run_feed(q, pieces, labels, state, feed_maps[q])
            change = change.reshape(rank, 3, count, subs[q]).swapaxes(1, 2)
            changes.append(change.reshape(rank, -1))

    names = [f"part{q}" for q in range(len(changes))]
    total = sum(change.shape[1] for change in changes) + channels + 4 * depth
    output, mgrad, cgrad, edge, gcg, pack, *_ = call(
        functools.partial(middle_body, front_at, 2, chan, len(changes)),
        dict(tab=tab, pos=pos),
        dict(
            middle=middle,
            grad=state[1],
            small=state[2],
            crel=crel,
            mrel=mrel,
            grel=grel,
            emap=front_map,
            gc=gc,
            cv=cv,
            mixed=mixed,
            out=state[0],
            second=second,
            mlow=mlow,
            **dict(zip(names, changes)),
        ),
        numbered(front),
        dict(
            output=wide(BRAIN),
            mgrad=wide(FLOAT),
            cgrad=inner(BRAIN),
            edge=((HALO, channels), BRAIN),
            gcg=inner(BRAIN),
            pack=((rank, total), BRAIN),
        ),
        [pltpu.VMEM((1, depth, channels), BRAIN), dma],
        late=("gc", "cv", "mixed", "out", "second", "mlow", *names),
        inner=dict(second_low=wide(BRAIN), back=small(rank)),
    )

    def run_back(mask, edge):
        return call(
            functools.partial(back_body, front_at, 2, chan),
            dict(tab=tab, pos=pos),
            dict(
                mask=mask,
                edge=edge,
                cgrad=cgrad,
                gcg=gcg,
                gb=gb,
                va=va,
                elow=elow,
                emap=front_map,
                mrel=mrel,
                mgrad=mgrad,
                trel=trel,
                grel=grel,
                xin=xin,
            ),
            numbered(front),
            dict(igrad=wide(BRAIN), pack=((rank, 3 * channels + depth), BRAIN)),
            [
                pltpu.VMEM((3, depth, channels), BRAIN),
                dma,
                pltpu.VMEM((rows, depth), FLOAT),
                pltpu.VMEM((rows, rank), FLOAT),
            ],
            late=("mgrad", "trel", "grel", "xin"),
        )

    most_widths = [3 * sub for sub in subs] + [chan]

    if quick:
        line.start("edge", lambda v: passed_along(v, -1), edge)
        most = Sum(line, "most", pack, most_widths)
        most.across()
        line.wait("edge", "mostacross")
        most.down()
        in_grad, pack = run_back(line.ready(mask), line["edge"])
        line.hold(pack)
        last = Sum(line, "last", pack, [3 * chan])
        last.across()
        line.wait("mostdown1", "mostdown2", "mostdown3")
        line.wait("lastacross")
        line.held = line.held[-1:] + [line["mostdown1"], line["mostdown2"], line["mostdown3"]]
        last.down()
        most.out()
        line.wait("lastdown1", "lastdown2", "lastdown3")
        last.out()
        most_rows, last_rows = most.result(), last.result()
    else:
        in_grad, last_pack = run_back(mask, passed_along(edge, -1))
        most_rows = plain_sum(pack, most_widths)
        last_rows = plain_sum(last_pack, [3 * chan])

    def placed(pick, found, axis):
        return sum(spread(pick(row), adapter_of[s], slots, axis) for s, row in found)

    def feed_part(row, k):
        return jnp.concatenate(
            [row[:, 3 * first + k * sub : 3 * first + (k + 1) * sub] for first, sub in zip(firsts, subs)],
            axis=1,
        )

    base = 3 * units + chan

    def wide_part(row, k):
        return row[:, base + k * depth : base + (k + 1) * depth]

    return (
        output[None],
        in_grad[None],
        placed(lambda row: row[:, 3 * chan :], last_rows, 0),
        placed(lambda row: row[:, : 3 * chan].reshape(rank, 3, chan), last_rows, 0),
        placed(lambda row: row[:, 3 * units : base], most_rows, 0),
        placed(lambda row: wide_part(row, 3), most_rows, 0),
        placed(lambda row: jnp.stack([wide_part(row, 0), wide_part(row, 1)]), most_rows, 1),
        placed(lambda row: jnp.stack([feed_part(row, 0), feed_part(row, 1)]), most_rows, 1),
        placed(lambda row: feed_part(row, 2), most_rows, 0),
        placed(lambda row: wide_part(row, 2), most_rows, 0),
    )


def solution(mesh):
    return jax.shard_map(
        per_device,
        mesh=mesh,
        in_specs=(
            P("dp", ("ctx", "tensor"), None),
            P("dp", None),
            P(),
            P("dp", ("ctx", "tensor"), None),
            P(),
            P(),
            P(None, "tensor"),
            P(None, "dp", "tensor"),
            P("tensor", "dp"),
            P(None, "dp", "tensor"),
            P("tensor", "dp"),
            P(),
            P(None, None, None, "tensor"),
            P(None, None, "tensor"),
            P(),
            P(),
            P(None, None, None, "tensor"),
            P(None, None, "tensor"),
            P(),
        ),
        out_specs=(
            P("dp", ("ctx", "tensor"), None),
            P("dp", ("ctx", "tensor"), None),
            P(),
            P(None, None, None, "tensor"),
            P(None, None, "tensor"),
            P(),
            P(),
            P(None, None, None, "tensor"),
            P(None, None, "tensor"),
            P(),
        ),
        check_vma=False,
    )
```

```python
import functools

import jax
import jax.numpy as jnp
from jax import lax
from jax.experimental import pallas as pl
from jax.experimental.pallas import tpu as pltpu
from jax.sharding import PartitionSpec as P

EPSILON = 1e-05
FLOAT = jnp.float32
BRAIN = jnp.bfloat16
HALO = 16
LANES = 128
ALONG = "tensor"
NN = ((1,), (0,))
NT = ((1,), (1,))
TN = ((0,), (0,))


def dot(a, b, dims=NN):
    return lax.dot_general(a, b, (dims, ((), ())), preferred_element_type=FLOAT)


def lanes(index):
    return pl.ds(pl.multiple_of(index * LANES, LANES), LANES)


class Held:
    def __init__(self):
        self.copies, self.gone = {}, []

    def begin(self, *names):
        for name in names:
            self.copies[name].start()

    def need(self, *names):
        for name in names:
            self.copies.pop(name).wait()

    def leave(self, name):
        copy = pltpu.make_async_copy(
            getattr(self, name), self.targets[name], self.out_sems.at[len(self.gone)]
        )
        copy.start()
        self.gone.append((name, copy.wait))

    def leave_tile(self, name, tile, tiles):
        ref, target, first = getattr(self, name), self.targets[name], len(self.gone)
        width = ref.shape[1] // tiles

        def copy(t):
            cols = pl.ds(t * width, width)
            if not isinstance(t, int):
                cols = pl.ds(pl.multiple_of(t * width, LANES), width)
            return pltpu.make_async_copy(
                ref.at[:, cols], target.at[:, cols], self.out_sems.at[first + t]
            )

        copy(tile).start()
        self.gone += [(name, lambda t=t: copy(t).wait()) for t in range(tiles)]


def call(body, scalars, ins, raw, outs, scratch, late=(), inner={}):
    forms = {n: o if isinstance(o, tuple) else (ins[o].shape, ins[o].dtype) for n, o in outs.items()}
    fresh = [n for n, o in outs.items() if isinstance(o, tuple)]
    raw_names = list(raw)

    def kernel(*refs):
        refs = list(refs)
        take = lambda count: [refs.pop(0) for _ in range(count)]
        r = Held()
        for name, ref in zip(scalars, take(len(scalars))):
            setattr(r, name, ref)
        sources = dict(zip(ins, take(len(ins))))
        for name, ref in zip(raw_names, take(len(raw_names))):
            setattr(r, name, ref)
        r.targets = dict(zip(outs, take(len(outs))))
        for name, ref in zip(ins, take(len(ins))):
            setattr(r, name, ref)
        for name, ref in zip(fresh + list(inner), take(len(fresh) + len(inner))):
            setattr(r, name, ref)
        for name, origin in outs.items():
            if not isinstance(origin, tuple):
                setattr(r, name, getattr(r, origin))
        in_sems, r.out_sems = take(2)
        r.scratch = refs
        for k, (name, source) in enumerate(sources.items()):
            r.copies[name] = pltpu.make_async_copy(source, getattr(r, name), in_sems.at[k])
            if name not in late:
                r.copies[name].start()
        body(r)
        for name in outs:
            if name not in [n for n, _ in r.gone]:
                r.leave(name)
        for _, wait in r.gone:
            wait()
        r.need(*list(r.copies))

    hbm = pl.BlockSpec(memory_space=pltpu.HBM)
    return pl.pallas_call(
        kernel,
        out_shape=[jax.ShapeDtypeStruct(*form) for form in forms.values()],
        in_specs=[pl.BlockSpec(memory_space=pltpu.SMEM)] * len(scalars)
        + [hbm] * (len(ins) + len(raw)),
        out_specs=[hbm] * len(outs),
        scratch_shapes=[pltpu.VMEM(v.shape, v.dtype) for v in ins.values()]
        + [pltpu.VMEM(*forms[n]) for n in fresh]
        + [pltpu.VMEM(*form) for form in inner.values()]
        + [pltpu.SemaphoreType.DMA((max(1, len(ins)),)), pltpu.SemaphoreType.DMA((32,))]
        + list(scratch),
        compiler_params=pltpu.CompilerParams(vmem_limit_bytes=54 << 20),
        cost_estimate=pl.CostEstimate(flops=1, bytes_accessed=1, transcendentals=0),
    )(*scalars.values(), *ins.values(), *raw.values())


def prep_body(r):
    rank = r.elow.shape[1]
    a = r.pick[0]
    maps, sems = r.scratch
    sources = (r.er.at[a], r.gr.at[0, a], r.gr.at[1, a], r.me.at[a], r.oe.at[a])
    copies = [
        pltpu.make_async_copy(source, maps.at[k], sems.at[k]) for k, source in enumerate(sources)
    ]
    for copy in copies:
        copy.start()
    r.need("tok", "halo")
    t32 = r.tok[...].astype(FLOAT)
    inv = lax.rsqrt(jnp.mean(t32 * t32, axis=-1, keepdims=True) + EPSILON)
    h32 = r.halo[...].astype(FLOAT)
    hinv = lax.rsqrt(jnp.mean(h32 * h32, axis=-1, keepdims=True) + EPSILON)
    r.need("cot", "gains")
    for copy in copies:
        copy.wait()
    for b in range(r.tok.shape[1] // LANES):
        src = lanes(r.tab[b])
        dst = slice(b * LANES, (b + 1) * LANES)
        part = r.tok[:, src]
        gain = r.gains[:, src]
        r.trel[:, dst] = part
        r.xin[HALO:, dst] = (part.astype(FLOAT) * inv * gain[0:1]).astype(BRAIN)
        r.xin[:HALO, dst] = (r.halo[:, src].astype(FLOAT) * hinv * gain[0:1]).astype(BRAIN)
        r.crel[:, dst] = r.cot[:, src]
        for k in range(5):
            r.mrel[k * rank : (k + 1) * rank, dst] = maps[k, :, src]
        r.grel[:, dst] = gain
    for name in ("trel", "xin", "crel"):
        r.leave(name)
    r.elow[...] = dot(r.xin[...], r.mrel[0:rank], NT).astype(BRAIN)
    r.ob[...] = dot(r.crel[...], r.mrel[4 * rank : 5 * rank], NT).astype(BRAIN)


def front_pack_body(r):
    half = r.unit.shape[1]
    rows = pl.ds(pl.multiple_of(r.core[0] * half, half), half)
    r.need("entry")
    for k in range(3):
        r.unit[k] = r.entry[k, rows, :]
    r.need("mixer")
    r.unit[3] = r.mixer[:, rows].astype(FLOAT).T.astype(BRAIN)


def feed_pack_body(count, r):
    units = [getattr(r, f"unit{q}") for q in range(count)]
    half = units[0].shape[1]
    rows = pl.ds(pl.multiple_of(r.core[0] * half, half), half)
    r.need("gates", "outlet")
    first = 0
    for q, unit in enumerate(units):
        cols = slice(first, first + unit.shape[2])
        for k in range(2):
            unit[k] = r.gates[k, rows, cols]
        unit[2] = r.outlet[cols, rows].astype(FLOAT).T.astype(BRAIN)
        r.leave(f"unit{q}")
        first += unit.shape[2]


def half_kernel(core, came, half, held, sems):
    count = half.shape[0]
    first = core[0] * count
    ins = [pltpu.make_async_copy(came.at[first + z], held.at[z], sems.at[0, z]) for z in range(count)]
    outs = [pltpu.make_async_copy(held.at[z], half.at[z], sems.at[1, z]) for z in range(count)]
    for copy in ins:
        copy.start()
    for z in range(count):
        ins[z].wait()
        outs[z].start()
    for copy in outs:
        copy.wait()


def local_body(r):
    whole, sems = r.scratch
    chan = r.taps.shape[1]
    units = r.orr.shape[2]
    a = r.pick[0]
    first = 5 * chan
    rank, half = r.out.shape
    copies = [
        pltpu.make_async_copy(source, whole.at[:, pl.ds(at, size)], sems.at[k])
        for k, (source, at, size) in enumerate(
            (
                (r.mr.at[a], 3 * chan, chan),
                (r.ge.at[0, a], first, units),
                (r.ge.at[1, a], first + units, units),
                (r.orr.at[a], first + 2 * units, units),
            )
        )
    ]
    for copy in copies:
        copy.start()
    r.need("ee", "taps")
    whole[:, : 3 * chan] = r.ee[...]
    whole[:, 4 * chan : 5 * chan] = jnp.zeros((rank, chan), BRAIN)
    whole[0:3, 4 * chan : 5 * chan] = r.taps[...]
    whole[:, first + 3 * units :] = jnp.zeros((rank, whole.shape[1] - first - 3 * units), BRAIN)
    for copy in copies:
        copy.wait()
    r.out[...] = whole[:, pl.ds(pl.multiple_of(r.core[0] * half, LANES), half)]


def maps_body(chan, units, subs, r):
    [side] = r.scratch
    front = r.front
    rank = front.shape[0] // 2
    half = r.mine.shape[1]
    count = r.mine.shape[0] // rank
    channels = chan * count
    r.need("mine", "theirs")
    side[:, pl.ds(pl.multiple_of(r.core[0] * half, LANES), half)] = r.mine[...]
    side[:, pl.ds(pl.multiple_of((1 - r.core[0]) * half, LANES), half)] = r.theirs[...]
    for s in range(count):
        own = slice(s * rank, (s + 1) * rank)
        z = r.pos[s]
        for k in range(4):
            at = pl.ds(pl.multiple_of(k * channels + z * chan, LANES), chan)
            front[0:rank, at] = side[own, k * chan : (k + 1) * chan]
        at = pl.ds(pl.multiple_of(z * chan, LANES), chan)
        front[rank : 2 * rank, at] = side[own, 4 * chan : 5 * chan]
        first = 5 * chan
        for q, sub in enumerate(subs):
            feed = getattr(r, f"feed{q}")
            for k in range(3):
                at = first + k * units
                to = pl.ds(pl.multiple_of(z * sub, LANES), sub)
                feed[k * rank : (k + 1) * rank, to] = side[own, at : at + sub]
            first += sub


def fetch(r, count, labels, w, sems, planes):
    pieces = [getattr(r, f"piece{p}") for p in range(len(labels))]
    width = pieces[0].shape[3]

    def copies(z):
        cols = pl.ds(pl.multiple_of(z * width, LANES), width)
        found = []
        for ref, label in zip(pieces, labels):
            for h in range(ref.shape[0] // count):
                size = ref.shape[2]
                place = label if isinstance(label, tuple) else (label + h * (size // LANES),)
                size //= len(place)
                for k, slot in enumerate(place):
                    if not isinstance(slot, int):
                        slot = slot(r.core[0])
                    source = ref.at[h * count + z, planes, pl.ds(k * size, size)]
                    target = pl.ds(pl.multiple_of(slot * LANES, LANES), size)
                    target = w.at[:, target, cols]
                    found.append(pltpu.make_async_copy(source, target, sems.at[z, len(found)]))
        return found

    for z in range(count):
        for copy in copies(z):
            copy.start()

    def wait(z):
        for copy in copies(z):
            copy.wait()

    def arrive(t, tile):
        need = lambda t: (t * tile + width - 1) // width
        lax.fori_loop(need(t), need(t + 1), lambda z, c: (wait(z), c)[1], 0)

    return arrive


def front_body(labels, tiles, r):
    w, sems, low = r.scratch
    rank = r.elow.shape[1]
    rows = r.trel.shape[0]
    channels = w.shape[2]
    width = channels // tiles
    arrive = fetch(r, sems.shape[0], labels, w, sems, slice(0, 4))
    r.begin("trel", "grel")
    r.need("mask", "xin", "elow", "emap", "mrel")
    r.middle[...] = jnp.zeros_like(r.middle)
    low[...] = jnp.zeros_like(low)

    def step(t, carry):
        arrive(t, width)
        col = pl.ds(pl.multiple_of(t * width, LANES), width)
        wide = lambda k: pl.ds(pl.multiple_of(k * channels + t * width, LANES), width)
        project = lambda k: dot(r.xin[...], w[k, :, col]) + dot(
            r.elow[...], r.emap[0:rank, wide(k)]
        )
        b = project(0)
        v = project(2)
        c = project(1)[HALO:]
        product = b * v
        r.gb[:, col] = b[HALO:].astype(BRAIN)
        r.va[:, col] = v[HALO:].astype(BRAIN)
        r.gc[:, col] = c.astype(BRAIN)
        taps = r.emap[rank : 2 * rank, col].astype(FLOAT)
        conv = (
            taps[0:1] * product[HALO:]
            + taps[1:2] * r.mask[0:rows, 0:1] * pltpu.roll(product, 1, 0)[HALO:]
            + taps[2:3] * r.mask[0:rows, 1:2] * pltpu.roll(product, 2, 0)[HALO:]
        )
        r.cv[:, col] = conv.astype(BRAIN)
        mix = (c * conv).astype(BRAIN)
        r.mixed[:, col] = mix
        for name in ("gb", "gc", "va", "cv", "mixed"):
            r.leave_tile(name, t, tiles)
        r.middle[...] += dot(mix, w[3, :, col], NT)
        low[...] += dot(mix, r.emap[0:rank, wide(3)], NT)
        return carry

    lax.fori_loop(0, tiles, step, 0)
    mlow = low[...].astype(BRAIN)
    r.mlow[...] = mlow
    r.need("trel", "grel")
    mid = r.middle[...] + r.trel[...].astype(FLOAT) + dot(mlow, r.mrel[3 * rank : 4 * rank])
    r.middle[...] = mid
    r.leave("middle")
    inv = lax.rsqrt(jnp.mean(mid * mid, axis=-1, keepdims=True) + EPSILON)
    x2 = (mid * inv * r.grel[1:2]).astype(BRAIN)
    r.second[...] = x2
    r.leave("second")
    r.glow[...] = dot(x2, r.mrel[rank : 3 * rank], NT).astype(BRAIN)


def feed_body(labels, tiles, sub, first, r):
    w, sems = r.scratch
    rank = r.ob.shape[1]
    width = w.shape[2] // tiles
    arrive = fetch(r, sems.shape[0], labels, w, sems, slice(0, 3))
    r.need("second", "crel", "glow", "ob", "emap")
    if first:
        r.out[...] = jnp.zeros_like(r.out)
        r.grad[...] = jnp.zeros_like(r.grad)
        r.small[...] = jnp.zeros_like(r.small)
    else:
        r.begin("small_in", "out_in", "grad_in")

    def step(t, carry):
        arrive(t, width)
        col = pl.ds(pl.multiple_of(t * width, LANES), width)
        eg, eu, ro = (r.emap[i * rank : (i + 1) * rank, col] for i in range(3))
        wg, wu, wo = (w[i, :, col] for i in range(3))
        x = r.second[...]
        lg, lu, ob = r.glow[:, 0:rank], r.glow[:, rank : 2 * rank], r.ob[...]
        g = dot(x, wg) + dot(lg, eg)
        u = dot(x, wu) + dot(lu, eu)
        h_grad = dot(r.crel[...], wo) + dot(ob, ro)
        sigma = 1.0 / (1.0 + jnp.exp(-g))
        act = g * sigma
        h = (act * u).astype(BRAIN)
        gg = (h_grad * u * (sigma * (1.0 + g * (1.0 - sigma)))).astype(BRAIN)
        ug = (h_grad * act).astype(BRAIN)
        if not first:
            pl.when(t == 0)(lambda: r.need("out_in", "grad_in", "small_in"))
        r.out[...] += dot(h, wo, NT)
        r.grad[...] += dot(gg, wg, NT) + dot(ug, wu, NT)
        r.small[:, 0:rank] += dot(gg, eg, NT)
        r.small[:, rank : 2 * rank] += dot(ug, eu, NT)
        r.small[:, 2 * rank : 3 * rank] += dot(h, ro, NT)
        changes = (dot(lg, gg, TN), dot(lu, ug, TN), dot(ob, h, TN))
        for j in range(0, width, LANES):
            at = t * width + j
            owner = at // sub
            for k in range(3):
                to = r.pos[owner] * (3 * sub) + k * sub + (at - owner * sub)
                to = pl.ds(pl.multiple_of(to, LANES), LANES)
                r.dmap[:, to] = changes[k][:, j : j + LANES].astype(r.dmap.dtype)
        return carry

    lax.fori_loop(0, tiles, step, 0)


def pulled(v, gain, grad):
    inv = lax.rsqrt(jnp.mean(v * v, axis=-1, keepdims=True) + EPSILON)
    scaled = grad * gain
    along = jnp.mean(v * scaled, axis=-1, keepdims=True)
    return inv * scaled - v * (inv * inv * inv * along)


def middle_body(labels, tiles, chan, parts, r):
    w, sems = r.scratch
    rank = r.mlow.shape[1]
    channels = w.shape[2]
    width = channels // tiles
    depth = w.shape[1]
    arrive = fetch(r, sems.shape[0], labels, w, sems, slice(3, 4))
    late = [f"part{q}" for q in range(parts)]
    r.begin("gc", "cv", "mixed", "out", "second", "mlow", *late)
    r.need("middle", "grad", "small", "crel", "mrel", "grel", "emap")
    gback = r.small[:, 0 : 2 * rank].astype(BRAIN)
    olow = r.small[:, 2 * rank : 3 * rank].astype(BRAIN)
    mid = r.middle[...]
    sgrad = r.grad[...] + dot(gback, r.mrel[rank : 3 * rank])
    mg = r.crel[...].astype(FLOAT) + pulled(mid, r.grel[1:2], sgrad)
    r.mgrad[...] = mg
    r.leave("mgrad")
    mlo = mg.astype(BRAIN)
    r.second_low[...] = mlo
    r.back[...] = dot(mlo, r.mrel[3 * rank : 4 * rank], NT).astype(BRAIN)
    r.need("gc", "cv", "mixed", *late)
    mix = 0
    for name in late:
        part = getattr(r, name)
        r.pack[:, mix : mix + part.shape[1]] = part[...]
        mix += part.shape[1]

    def step(t, carry):
        arrive(t, width)
        col = pl.ds(pl.multiple_of(t * width, LANES), width)
        own = pl.ds(pl.multiple_of(3 * channels + t * width, LANES), width)
        mx = dot(r.second_low[...], w[0, :, col]) + dot(r.back[...], r.emap[0:rank, own])
        r.gcg[:, col] = (mx * r.cv[:, col].astype(FLOAT)).astype(BRAIN)
        cg = mx * r.gc[:, col].astype(FLOAT)
        r.cgrad[:, col] = cg.astype(BRAIN)
        for name in ("gcg", "cgrad"):
            r.leave_tile(name, t, tiles)
        r.edge[:, col] = cg[:HALO].astype(BRAIN)
        change = dot(r.back[...], r.mixed[:, col], TN).astype(BRAIN)
        for j in range(0, width, LANES):
            at = t * width + j
            owner = at // chan
            to = mix + r.pos[owner] * chan + at - owner * chan
            r.pack[:, pl.ds(pl.multiple_of(to, LANES), LANES)] = change[:, j : j + LANES]
        return carry

    lax.fori_loop(0, tiles, step, 0)
    r.leave("edge")
    wide = mix + channels
    r.need("second", "mlow")
    dff = jnp.concatenate([dot(gback, r.second[...], TN), dot(olow, r.crel[...], TN)], axis=0)
    dff = jnp.concatenate([dff, dot(r.mlow[...], r.second_low[...], TN)], axis=0).astype(BRAIN)
    for b in range(depth // LANES):
        src = slice(b * LANES, (b + 1) * LANES)
        for k in range(4):
            to = pl.ds(pl.multiple_of(wide + k * depth + r.tab[b] * LANES, LANES), LANES)
            r.pack[:, to] = dff[k * rank : (k + 1) * rank, src]
    r.leave("pack")
    r.need("out")
    full = r.middle[...] + r.out[...] + dot(olow, r.mrel[4 * rank : 5 * rank])
    for b in range(depth // LANES):
        r.output[:, lanes(r.tab[b])] = full[:, b * LANES : (b + 1) * LANES].astype(BRAIN)


def back_body(labels, tiles, chan, r):
    w, sems, fgrad, back = r.scratch
    rank = r.elow.shape[1]
    rows = r.trel.shape[0]
    channels = w.shape[2]
    width = channels // tiles
    arrive = fetch(r, sems.shape[0], labels, w, sems, slice(0, 3))
    r.begin("mgrad", "trel", "grel", "xin")
    r.need("mask", "edge", "cgrad", "gcg", "gb", "va", "elow", "emap", "mrel")
    total = rows + HALO
    fgrad[...] = jnp.zeros_like(fgrad)
    back[...] = jnp.zeros_like(back)

    def step(t, carry):
        arrive(t, width)
        col = pl.ds(pl.multiple_of(t * width, LANES), width)
        taps = r.emap[rank : 2 * rank, col].astype(FLOAT)
        cg = jnp.concatenate([r.cgrad[:, col], r.edge[:, col]], axis=0).astype(FLOAT)
        pg = (
            taps[0:1] * cg
            + pltpu.roll(taps[1:2] * r.mask[:, 0:1] * cg, total - 1, 0)
            + pltpu.roll(taps[2:3] * r.mask[:, 1:2] * cg, total - 2, 0)
        )[:rows]
        parts = (
            (pg * r.va[:, col].astype(FLOAT)).astype(BRAIN),
            r.gcg[:, col],
            (pg * r.gb[:, col].astype(FLOAT)).astype(BRAIN),
        )
        for k in range(3):
            fgrad[...] += dot(parts[k], w[k, :, col], NT)
            wide = pl.ds(pl.multiple_of(k * channels + t * width, LANES), width)
            back[...] += dot(parts[k], r.emap[0:rank, wide], NT)
            change = dot(r.elow[HALO:, :], parts[k], TN).astype(BRAIN)
            for j in range(0, width, LANES):
                at = t * width + j
                owner = at // chan
                to = r.pos[owner] * 3 * chan + k * chan + at - owner * chan
                r.pack[:, pl.ds(pl.multiple_of(to, LANES), LANES)] = change[:, j : j + LANES]
        return carry

    lax.fori_loop(0, tiles, step, 0)
    low = back[...].astype(BRAIN)
    first = fgrad[...] + dot(low, r.mrel[0:rank])
    r.need("mgrad", "trel", "grel", "xin")
    dred = dot(low, r.xin[HALO:, :], TN).astype(BRAIN)
    for b in range(w.shape[1] // LANES):
        to = pl.ds(pl.multiple_of(3 * channels + r.tab[b] * LANES, LANES), LANES)
        r.pack[:, to] = dred[:, b * LANES : (b + 1) * LANES]
    r.leave("pack")
    full = r.mgrad[...] + pulled(r.trel[...].astype(FLOAT), r.grel[0:1], first)
    for b in range(w.shape[1] // LANES):
        r.igrad[:, lanes(r.tab[b])] = full[:, b * LANES : (b + 1) * LANES].astype(BRAIN)


def shifted(block, distance):
    size = lax.axis_size(ALONG)
    return lax.ppermute(block, ALONG, [(i, (i + distance) % size) for i in range(size)])


def flipped(block, bit):
    return lax.ppermute(block, "dp", [(i, i ^ bit) for i in range(lax.axis_size("dp"))])


def swapped(block):
    return lax.ppermute(block, "ctx", [(0, 1), (1, 0)])


def turned(block, bits):
    route = [(2 * d + c, 2 * (d ^ bits[c]) + c) for d in range(lax.axis_size("dp")) for c in range(2)]
    return lax.ppermute(block, ("dp", "ctx"), route)


def passed_along(block, distance):
    axes = ("ctx", ALONG)
    size = lax.axis_size("ctx") * lax.axis_size(ALONG)
    route = [(i, i + distance) for i in range(size) if 0 <= i + distance < size]
    return lax.ppermute(block, axes, route)


def after(value, *others):
    return lax.optimization_barrier((value, others))[0]


def shape_of(chip, core):
    near = jnp.where(core == 0, 1, 2)
    places = [(0, 0), (0, 1), (near, 0), (near, 1), (3 - near, 0), (3 - near, 1)]
    places += [(3, core), (3, 1 - core)]
    return jnp.stack([(chip ^ e) * 2 + h for e, h in places]).astype(jnp.int32)


class Line:
    def __init__(self):
        self.held = []
        self.values = {}

    def wait(self, *names):
        for name in names:
            self.held.append(self.values[name])
        self.held = self.held[-4:]

    def hold(self, *values):
        self.held = (self.held + list(values))[-3:]

    def ready(self, value):
        return after(value, *self.held) if self.held else value

    def start(self, name, move, value):
        self.values[name] = move(self.ready(value))

    def __getitem__(self, name):
        return self.values[name]


class Block:
    def __init__(self, line, name, unit, early):
        self.line, self.name, self.unit, self.early = line, name, unit, early

    def at(self, step):
        return self.line[self.name + step]

    def go(self, *steps):
        for step in steps:
            self.line.start(self.name + step, *self.plan(step))

    def wait(self, *steps):
        self.line.wait(*(self.name + step for step in steps))

    def plan(self, step):
        if step == "p":
            return (lambda v: turned(v, (1, 2))), self.unit
        if step == "z" and self.early:
            base = jnp.concatenate([self.unit, self.at("p")], axis=1)
            return (lambda v: lax.all_gather(v, ALONG, axis=0)), base
        if step == "z":
            return (lambda v: lax.all_gather(v, ("ctx", ALONG), axis=0)), self.unit
        if step == "a":
            return (lambda v: turned(v, (2, 1))), self.at("z")
        if step == "c":
            return swapped, self.at("z")
        if step == "o":
            return (lambda v: turned(v, (1, 2))), self.at("z")
        if step == "d":
            came = self.at("o")
            shape = (came.shape[0] // 2,) + came.shape[1:]
            half = pl.pallas_call(
                half_kernel,
                out_shape=jax.ShapeDtypeStruct(shape, BRAIN),
                in_specs=[
                    pl.BlockSpec(memory_space=pltpu.SMEM),
                    pl.BlockSpec(memory_space=pltpu.HBM),
                ],
                out_specs=pl.BlockSpec(memory_space=pltpu.HBM),
                scratch_shapes=[
                    pltpu.VMEM(shape, BRAIN),
                    pltpu.SemaphoreType.DMA((2, shape[0])),
                ],
                cost_estimate=pl.CostEstimate(flops=1, bytes_accessed=1, transcendentals=0),
            )(self.line.ready(lax.axis_index("ctx")[None].astype(jnp.int32)), came)
            return (lambda v: turned(v, (2, 1))), half
        return swapped, self.at(step[1:])

    def pieces(self):
        if not self.early:
            return [self.at(n) for n in ("z", "o", "co", "d", "cd")], (0, 2, 4, 6, 7)
        labels = (
            (lambda c: c, lambda c: 2 + c),
            (lambda c: 4 + c, 6),
            (lambda c: 1 - c, lambda c: 5 - c),
            (lambda c: 3 - c, 7),
        )
        return [self.at(n) for n in ("z", "a", "c", "ca")], labels


def spread(update, adapter, slots, axis):
    onehot = (lax.broadcasted_iota(jnp.int32, (slots,), 0) == adapter).astype(FLOAT)
    layout = [1] * (update.ndim + 1)
    layout[axis] = slots
    return jnp.expand_dims(update, axis) * onehot.reshape(layout)


def rounded(value):
    return lax.reduce_precision(value, 8, 7).astype(BRAIN)


class Sum:
    def __init__(self, line, name, mine, widths, halved):
        self.line, self.name, self.mine, self.widths = line, name, mine, widths
        self.count = lax.axis_size(ALONG)
        self.halved = halved

    def half(self, value):
        if not self.halved:
            return value
        size = value.shape[0] // 2
        return lax.dynamic_slice_in_dim(value, lax.axis_index("ctx") * size, size, 0)

    def wait_down(self):
        self.line.wait(*(self.name + f"down{s}" for s in range(1, self.count)))

    def across(self):
        self.line.start(self.name + "across", swapped, self.mine)

    def down(self):
        pair = self.half(self.mine).astype(FLOAT)
        pair = pair + self.half(self.line[self.name + "across"]).astype(FLOAT)
        pair = rounded(pair)
        rest = pair[:, sum(self.widths) * self.count :]
        self.parts = []
        for s in range(self.count):
            first, part = 0, []
            for width in self.widths:
                part.append(pair[:, first + s * width : first + (s + 1) * width])
                first += width * self.count
            self.parts.append(jnp.concatenate(part + [rest], axis=1))
        for s in range(1, self.count):
            self.line.start(self.name + f"down{s}", lambda v, s=s: shifted(v, -s), self.parts[s])

    def out(self):
        terms = [self.parts[0]] + [self.line[self.name + f"down{s}"] for s in range(1, self.count)]
        stack = jnp.stack(terms)
        at = lax.axis_index(ALONG)
        self.total = sum(
            lax.dynamic_index_in_dim(stack, (k - at) % self.count, 0, keepdims=False).astype(FLOAT)
            for k in range(self.count)
        )
        self.total = rounded(self.total)
        for e in range(1, lax.axis_size("dp")):
            self.line.start(self.name + f"out{e}", lambda v, e=e: flipped(v, e), self.total)

    def result(self):
        here = lax.axis_index("dp")
        rows = [(here, self.total)]
        for e in range(1, lax.axis_size("dp")):
            rows.append((here ^ e, self.line[self.name + f"out{e}"]))
        if self.halved:
            size = self.total.shape[0]
            mine = jnp.concatenate([row for _, row in rows], axis=0)
            other = swapped(mine)
            low = lax.axis_index("ctx") == 0
            both = [
                jnp.concatenate([jnp.where(low, mine, other)[at], jnp.where(low, other, mine)[at]])
                for at in (slice(k * size, (k + 1) * size) for k in range(len(rows)))
            ]
            rows = [(s, row) for (s, _), row in zip(rows, both)]
        return [(s, row.astype(FLOAT)) for s, row in rows]


def plain_sum(mine, widths):
    count = lax.axis_size(ALONG)
    at = lax.axis_index(ALONG)
    mine = lax.psum(mine.astype(FLOAT), ("ctx", ALONG))
    first, parts = 0, []
    for width in widths:
        parts.append(lax.dynamic_slice_in_dim(mine, first + at * width, width, 1))
        first += width * count
    rows = lax.all_gather(jnp.concatenate([*parts, mine[:, first:]], axis=1), "dp", axis=0)
    return [(s, rows[s]) for s in range(lax.axis_size("dp"))]


def chosen(table, adapter, axis):
    return lax.dynamic_index_in_dim(table, adapter, axis, keepdims=False)


def chunk_widths(units):
    if units == 1152:
        return (512, 384, 256)
    return (units // 3,) * 3


def per_device(
    tokens,
    segments,
    adapter_of,
    cotangent,
    first_gain,
    second_gain,
    conv_taps,
    entry_weight,
    mixer_weight,
    gates_weight,
    outlet_weight,
    entry_reduce,
    entry_expand,
    mixer_reduce,
    mixer_expand,
    gates_reduce,
    gates_expand,
    outlet_reduce,
    outlet_expand,
):
    slots, rank, depth = entry_reduce.shape
    seqs, cores, count = (lax.axis_size(a) for a in ("dp", "ctx", ALONG))
    here, core, at = (lax.axis_index(a) for a in ("dp", "ctx", ALONG))
    rows = tokens.shape[1]
    blocks = depth // LANES
    chan = mixer_weight.shape[0]
    units = outlet_weight.shape[0]
    channels = chan * count
    subs = chunk_widths(units)
    firsts = [sum(subs[:q]) for q in range(len(subs))]
    quick = (
        seqs == 4
        and cores == 2
        and count == 4
        and depth == seqs * cores * LANES
        and all(sub % LANES == 0 for sub in subs)
    )
    line = Line()

    adapter = adapter_of[here]
    pick = adapter[None].astype(jnp.int32)
    own = core[None].astype(jnp.int32)
    expand = chosen(entry_expand, adapter, 0).reshape(rank, 3 * chan)

    if quick:
        half = depth // seqs // cores
        [front_unit] = call(
            front_pack_body,
            dict(core=own),
            dict(entry=entry_weight, mixer=mixer_weight),
            {},
            dict(unit=((4, half, chan), BRAIN)),
            [],
        )
        line.start("halo", lambda v: passed_along(v, 1), tokens[0, rows - HALO :])
        halo = line["halo"]
        e = Block(line, "e", front_unit, False)
        e.go("z")
        span = 5 * chan + 3 * units
        span = (span + 2 * LANES - 1) // (2 * LANES) * LANES
        [local] = call(
            local_body,
            dict(pick=pick, core=after(own, front_unit)),
            dict(ee=expand, taps=conv_taps),
            dict(mr=mixer_reduce, ge=gates_expand, orr=outlet_reduce),
            dict(out=((rank, span), BRAIN)),
            [pltpu.VMEM((rank, 2 * span), BRAIN), pltpu.SemaphoreType.DMA((4,))],
        )
        feed_units = call(
            functools.partial(feed_pack_body, len(subs)),
            dict(core=after(own, front_unit)),
            dict(gates=gates_weight, outlet=outlet_weight),
            {},
            {f"unit{q}": ((3, half, sub), BRAIN) for q, sub in enumerate(subs)},
            [],
        )
        tab = shape_of(here, core)
        pos = ((at - jnp.arange(count)) % count).astype(jnp.int32)
    else:
        halo = passed_along(tokens[0, rows - HALO :], 1)
        local = jnp.concatenate(
            [
                expand,
                chosen(mixer_reduce, adapter, 0),
                jnp.pad(conv_taps, ((0, rank - 3), (0, 0))),
                chosen(gates_expand, adapter, 1)[0],
                chosen(gates_expand, adapter, 1)[1],
                chosen(outlet_reduce, adapter, 0),
            ],
            axis=1,
        )

        def full(block, rows_axis, cols_axis):
            block = lax.all_gather(block, "dp", axis=rows_axis, tiled=True)
            return lax.all_gather(block, ALONG, axis=cols_axis, tiled=True)

        front = [
            jnp.concatenate(
                [full(entry_weight, 1, 2), full(mixer_weight, 1, 0).T[None]], axis=0
            )
        ]
        front = [front[0][None]]
        front_at = (0,)
        pos = jnp.arange(count, dtype=jnp.int32)
        whole = jnp.concatenate(
            [full(gates_weight, 1, 2), full(outlet_weight, 1, 0).T[None]], axis=0
        ).reshape(3, depth, count, units)
        feed = [
            ([whole[:, :, :, first : first + sub].reshape(1, 3, depth, count * sub)], (0,))
            for first, sub in zip(firsts, subs)
        ]
        tab = jnp.arange(blocks, dtype=jnp.int32)
        side = list(lax.all_gather(local, ALONG, axis=0))

        def columns(first, size):
            return jnp.concatenate([part[:, first : first + size] for part in side], axis=1)

        low = jnp.concatenate([columns(k * chan, chan) for k in range(4)], axis=1)
        taps = jnp.pad(columns(4 * chan, chan), ((0, 0), (0, 3 * channels)))
        front_map = jnp.concatenate([low, taps], axis=0)
        feed_maps = [
            jnp.concatenate([columns(5 * chan + k * units + first, sub) for k in range(3)], axis=0)
            for first, sub in zip(firsts, subs)
        ]

    index = core * count + at
    seg = jnp.concatenate(
        [jnp.full((2,), -1, jnp.int32), segments[0], jnp.full((HALO,), -2, jnp.int32)]
    )
    seg = lax.dynamic_slice_in_dim(seg, index * rows, rows + HALO + 2)
    mask = jnp.stack([seg[1:-1] == seg[2:], seg[:-2] == seg[2:]], axis=1).astype(FLOAT)
    gains = jnp.stack([first_gain, second_gain]).astype(FLOAT)

    wide = lambda dtype: ((rows, depth), dtype)
    inner = lambda dtype: ((rows, channels), dtype)
    small = lambda n: ((rows, n), BRAIN)
    dma = pltpu.SemaphoreType.DMA((count if quick else 1, blocks))
    numbered = lambda pieces: {f"piece{p}": piece for p, piece in enumerate(pieces)}

    def run_prep():
        return call(
            prep_body,
            dict(pick=pick, tab=tab),
            dict(tok=tokens[0], halo=halo, cot=cotangent[0], gains=gains),
            dict(er=entry_reduce, gr=gates_reduce, me=mixer_expand, oe=outlet_expand),
            dict(
                trel=wide(BRAIN),
                xin=((rows + HALO, depth), BRAIN),
                crel=wide(BRAIN),
                mrel=((5 * rank, depth), BRAIN),
                grel=(gains.shape, FLOAT),
                elow=((rows + HALO, rank), BRAIN),
                ob=small(rank),
            ),
            [pltpu.VMEM((5, rank, depth), BRAIN), pltpu.SemaphoreType.DMA((5,))],
        )

    def run_front(pieces, labels, mask):
        return call(
            functools.partial(front_body, labels, 2),
            {},
            dict(
                mask=mask, xin=xin, elow=elow, emap=front_map, mrel=mrel, trel=trel, grel=grel
            ),
            numbered(pieces),
            dict(
                gb=inner(BRAIN),
                gc=inner(BRAIN),
                va=inner(BRAIN),
                cv=inner(BRAIN),
                mixed=inner(BRAIN),
                mlow=small(rank),
                middle=wide(FLOAT),
                second=wide(BRAIN),
                glow=small(2 * rank),
            ),
            [pltpu.VMEM((4, depth, channels), BRAIN), dma, pltpu.VMEM((rows, rank), FLOAT)],
            late=("trel", "grel"),
        )

    def run_feed(q, pieces, labels, state, feed_map):
        width = count * subs[q]
        ins = dict(second=second, crel=crel, glow=glow, ob=ob, emap=feed_map)
        if state:
            ins.update(out_in=state[0], grad_in=state[1], small_in=state[2])
            outs = dict(out="out_in", grad="grad_in", small="small_in")
        else:
            outs = dict(out=wide(FLOAT), grad=wide(FLOAT), small=((rows, 3 * rank), FLOAT))
        *state, change = call(
            functools.partial(
                feed_body, labels, max(1, width // 512), subs[q] if quick else width, not state
            ),
            dict(pos=pos, core=own),
            ins,
            numbered(pieces),
            dict(outs, dmap=((rank, 3 * width), BRAIN)),
            [pltpu.VMEM((3, depth, width), BRAIN), dma],
            late=("out_in", "grad_in", "small_in"),
        )
        return state, change

    state, changes = (), []
    if quick:
        f = [Block(line, f"f{q}", unit, q > 0) for q, unit in enumerate(feed_units)]
        f[1].go("p")
        f[2].go("p")
        trel, xin, crel, mrel, grel, elow, ob = run_prep()
        line.hold(local, ob)
        f[0].go("z")
        for k in range(1, count):
            line.start(f"local{k}", lambda v, k=k: shifted(v, k), local)
        f[1].wait("p")
        f[2].wait("p")
        e.wait("z")
        e.go("o")
        f[1].go("z")
        line.wait("local1", "local2", "local3")
        mine = jnp.concatenate([local] + [line[f"local{k}"] for k in range(1, count)], axis=0)
        line.start("locals", swapped, mine)
        line.wait("locals")
        front_map, *feed_maps = call(
            functools.partial(maps_body, chan, units, subs),
            dict(core=own, pos=pos),
            dict(mine=mine, theirs=line["locals"]),
            {},
            dict(
                {"front": ((2 * rank, 4 * channels), BRAIN)},
                **{f"feed{q}": ((3 * rank, count * sub), BRAIN) for q, sub in enumerate(subs)},
            ),
            [pltpu.VMEM((count * rank, 2 * span), BRAIN)],
        )
        line.hold(front_map)
        e.wait("o")
        e.go("d", "co")
        f[2].go("z")
        e.wait("d")
        e.go("cd")
        f[0].wait("z")
        f[0].go("o")
        e.wait("co", "cd")
        front, front_at = e.pieces()
        gb, gc, va, cv, mixed, mlow, middle, second, glow = run_front(
            front, front_at, line.ready(mask)
        )
        line.hold(glow)
        f[0].wait("o")
        f[0].go("d", "co")
        f[0].wait("d")
        f[0].go("cd")
        f[1].wait("z")
        f[1].go("a", "c")
        f[0].wait("cd", "co")
        state, change = run_feed(0, *f[0].pieces(), state, line.ready(feed_maps[0]))
        changes.append(change)
        line.hold(change)
        f[1].wait("a")
        f[1].go("ca")
        f[2].wait("z")
        f[2].go("a", "c")
        f[1].wait("c", "ca")
        state, change = run_feed(1, *f[1].pieces(), state, line.ready(feed_maps[1]))
        changes.append(change)
        line.hold(change)
        f[2].wait("a")
        f[2].go("ca")
        f[2].wait("c", "ca")
        state, change = run_feed(2, *f[2].pieces(), state, line.ready(feed_maps[2]))
        changes.append(change)
        line.hold(change)
    else:
        trel, xin, crel, mrel, grel, elow, ob = run_prep()
        gb, gc, va, cv, mixed, mlow, middle, second, glow = run_front(front, front_at, mask)
        for q, (pieces, labels) in enumerate(feed):
            state, change = run_feed(q, pieces, labels, state, feed_maps[q])
            change = change.reshape(rank, 3, count, subs[q]).swapaxes(1, 2)
            changes.append(change.reshape(rank, -1))

    names = [f"part{q}" for q in range(len(changes))]
    total = sum(change.shape[1] for change in changes) + channels + 4 * depth
    output, mgrad, cgrad, edge, gcg, pack, *_ = call(
        functools.partial(middle_body, front_at, 2, chan, len(changes)),
        dict(tab=tab, pos=pos),
        dict(
            middle=middle,
            grad=state[1],
            small=state[2],
            crel=crel,
            mrel=mrel,
            grel=grel,
            emap=front_map,
            gc=gc,
            cv=cv,
            mixed=mixed,
            out=state[0],
            second=second,
            mlow=mlow,
            **dict(zip(names, changes)),
        ),
        numbered(front),
        dict(
            output=wide(BRAIN),
            mgrad=wide(FLOAT),
            cgrad=inner(BRAIN),
            edge=((HALO, channels), BRAIN),
            gcg=inner(BRAIN),
            pack=((rank, total), BRAIN),
        ),
        [pltpu.VMEM((1, depth, channels), BRAIN), dma],
        late=("gc", "cv", "mixed", "out", "second", "mlow", *names),
        inner=dict(second_low=wide(BRAIN), back=small(rank)),
    )

    def run_back(mask, edge):
        return call(
            functools.partial(back_body, front_at, 2, chan),
            dict(tab=tab, pos=pos),
            dict(
                mask=mask,
                edge=edge,
                cgrad=cgrad,
                gcg=gcg,
                gb=gb,
                va=va,
                elow=elow,
                emap=front_map,
                mrel=mrel,
                mgrad=mgrad,
                trel=trel,
                grel=grel,
                xin=xin,
            ),
            numbered(front),
            dict(igrad=wide(BRAIN), pack=((rank, 3 * channels + depth), BRAIN)),
            [
                pltpu.VMEM((3, depth, channels), BRAIN),
                dma,
                pltpu.VMEM((rows, depth), FLOAT),
                pltpu.VMEM((rows, rank), FLOAT),
            ],
            late=("mgrad", "trel", "grel", "xin"),
        )

    most_widths = [3 * sub for sub in subs] + [chan]

    if quick:
        line.start("edge", lambda v: passed_along(v, -1), edge)
        most = Sum(line, "most", pack, most_widths, True)
        most.across()
        line.wait("edge", "mostacross")
        most.down()
        in_grad, pack = run_back(line.ready(mask), line["edge"])
        line.hold(pack)
        last = Sum(line, "last", pack, [3 * chan], False)
        last.across()
        line.wait("lastacross")
        most.wait_down()
        last.down()
        most.out()
        last.wait_down()
        last.out()
        most_rows, last_rows = most.result(), last.result()
    else:
        in_grad, last_pack = run_back(mask, passed_along(edge, -1))
        most_rows = plain_sum(pack, most_widths)
        last_rows = plain_sum(last_pack, [3 * chan])

    def placed(pick, found, axis):
        return sum(spread(pick(row), adapter_of[s], slots, axis) for s, row in found)

    def feed_part(row, k):
        return jnp.concatenate(
            [row[:, 3 * first + k * sub : 3 * first + (k + 1) * sub] for first, sub in zip(firsts, subs)],
            axis=1,
        )

    base = 3 * units + chan

    def wide_part(row, k):
        return row[:, base + k * depth : base + (k + 1) * depth]

    return (
        output[None],
        in_grad[None],
        placed(lambda row: row[:, 3 * chan :], last_rows, 0),
        placed(lambda row: row[:, : 3 * chan].reshape(rank, 3, chan), last_rows, 0),
        placed(lambda row: row[:, 3 * units : base], most_rows, 0),
        placed(lambda row: wide_part(row, 3), most_rows, 0),
        placed(lambda row: jnp.stack([wide_part(row, 0), wide_part(row, 1)]), most_rows, 1),
        placed(lambda row: jnp.stack([feed_part(row, 0), feed_part(row, 1)]), most_rows, 1),
        placed(lambda row: feed_part(row, 2), most_rows, 0),
        placed(lambda row: wide_part(row, 2), most_rows, 0),
    )


def solution(mesh):
    return jax.shard_map(
        per_device,
        mesh=mesh,
        in_specs=(
            P("dp", ("ctx", ALONG), None),
            P("dp", None),
            P(),
            P("dp", ("ctx", ALONG), None),
            P(),
            P(),
            P(None, ALONG),
            P(None, "dp", ALONG),
            P(ALONG, "dp"),
            P(None, "dp", ALONG),
            P(ALONG, "dp"),
            P(),
            P(None, None, None, ALONG),
            P(None, None, ALONG),
            P(),
            P(),
            P(None, None, None, ALONG),
            P(None, None, ALONG),
            P(),
        ),
        out_specs=(
            P("dp", ("ctx", ALONG), None),
            P("dp", ("ctx", ALONG), None),
            P(),
            P(None, None, None, ALONG),
            P(None, None, ALONG),
            P(),
            P(),
            P(None, None, None, ALONG),
            P(None, None, ALONG),
            P(),
        ),
        check_vma=False,
    )
```

```python
import functools

import jax
import jax.numpy as jnp
from jax import lax
from jax.experimental import pallas as pl
from jax.experimental.pallas import tpu as pltpu
from jax.sharding import PartitionSpec as P

EPSILON = 1e-05
FLOAT = jnp.float32
BRAIN = jnp.bfloat16
HALO = 16
LANES = 128
ALONG = "tensor"
NN = ((1,), (0,))
NT = ((1,), (1,))
TN = ((0,), (0,))


def dot(a, b, dims=NN):
    return lax.dot_general(a, b, (dims, ((), ())), preferred_element_type=FLOAT)


def lanes(index):
    return pl.ds(pl.multiple_of(index * LANES, LANES), LANES)


class Held:
    def __init__(self):
        self.copies, self.begun, self.gone, self.extra = {}, set(), [], ()

    def put(self, name, ref):
        self.__dict__[name] = ref

    def begin(self, *names):
        for name in names:
            if name in self.copies and name not in self.begun:
                self.copies[name].start()
                self.begun.add(name)

    def need(self, *names):
        for name in names:
            if name in self.copies:
                self.copies.pop(name).wait()

    def leave(self, name):
        copy = pltpu.make_async_copy(
            getattr(self, name), self.targets[name], self.out_sems.at[len(self.gone)]
        )
        copy.start()
        self.gone.append((name, copy.wait))

    def leave_tile(self, name, tile, tiles):
        ref, target, first = getattr(self, name), self.targets[name], len(self.gone)
        width = ref.shape[1] // tiles

        def copy(t):
            cols = pl.ds(t * width, width)
            if not isinstance(t, int):
                cols = pl.ds(pl.multiple_of(t * width, LANES), width)
            return pltpu.make_async_copy(
                ref.at[:, cols], target.at[:, cols], self.out_sems.at[first + t]
            )

        copy(tile).start()
        self.gone += [(name, lambda t=t: copy(t).wait()) for t in range(tiles)]


def call(body, scalars, ins, raw, outs, scratch, late=(), inner={}):
    forms = {n: o if isinstance(o, tuple) else (ins[o].shape, ins[o].dtype) for n, o in outs.items()}
    fresh = [n for n, o in outs.items() if isinstance(o, tuple)]
    raw_names = list(raw)

    def kernel(*refs):
        refs = list(refs)
        take = lambda count: [refs.pop(0) for _ in range(count)]
        r = Held()
        for name, ref in zip(scalars, take(len(scalars))):
            setattr(r, name, ref)
        sources = dict(zip(ins, take(len(ins))))
        for name, ref in zip(raw_names, take(len(raw_names))):
            setattr(r, name, ref)
        r.targets = dict(zip(outs, take(len(outs))))
        for name, ref in zip(ins, take(len(ins))):
            setattr(r, name, ref)
        for name, ref in zip(fresh + list(inner), take(len(fresh) + len(inner))):
            setattr(r, name, ref)
        for name, origin in outs.items():
            if not isinstance(origin, tuple):
                setattr(r, name, getattr(r, origin))
        in_sems, r.out_sems = take(2)
        r.scratch = refs
        for k, (name, source) in enumerate(sources.items()):
            r.copies[name] = pltpu.make_async_copy(source, getattr(r, name), in_sems.at[k])
            if name not in late:
                r.begin(name)
        body(r)
        for name in outs:
            if name not in [n for n, _ in r.gone]:
                r.leave(name)
        for _, wait in r.gone:
            wait()
        r.need(*list(r.copies))

    hbm = pl.BlockSpec(memory_space=pltpu.HBM)
    return pl.pallas_call(
        kernel,
        out_shape=[jax.ShapeDtypeStruct(*form) for form in forms.values()],
        in_specs=[pl.BlockSpec(memory_space=pltpu.SMEM)] * len(scalars)
        + [hbm] * (len(ins) + len(raw)),
        out_specs=[hbm] * len(outs),
        scratch_shapes=[pltpu.VMEM(v.shape, v.dtype) for v in ins.values()]
        + [pltpu.VMEM(*forms[n]) for n in fresh]
        + [pltpu.VMEM(*form) for form in inner.values()]
        + [pltpu.SemaphoreType.DMA((max(1, len(ins)),)), pltpu.SemaphoreType.DMA((32,))]
        + list(scratch),
        compiler_params=pltpu.CompilerParams(vmem_limit_bytes=54 << 20),
        cost_estimate=pl.CostEstimate(flops=1, bytes_accessed=1, transcendentals=0),
    )(*scalars.values(), *ins.values(), *raw.values())


def prep_body(r):
    rank = r.elow.shape[1]
    a = r.pick[0]
    maps, sems = r.scratch
    sources = (r.er.at[a], r.gr.at[0, a], r.gr.at[1, a], r.me.at[a], r.oe.at[a])
    copies = [
        pltpu.make_async_copy(source, maps.at[k], sems.at[k]) for k, source in enumerate(sources)
    ]
    for copy in copies:
        copy.start()
    r.need("tok", "halo")
    t32 = r.tok[...].astype(FLOAT)
    inv = lax.rsqrt(jnp.mean(t32 * t32, axis=-1, keepdims=True) + EPSILON)
    h32 = r.halo[...].astype(FLOAT)
    hinv = lax.rsqrt(jnp.mean(h32 * h32, axis=-1, keepdims=True) + EPSILON)
    r.need("cot", "gains")
    for copy in copies:
        copy.wait()
    for b in range(r.tok.shape[1] // LANES):
        src = lanes(r.tab[b])
        dst = slice(b * LANES, (b + 1) * LANES)
        part = r.tok[:, src]
        gain = r.gains[:, src]
        r.trel[:, dst] = part
        r.xin[HALO:, dst] = (part.astype(FLOAT) * inv * gain[0:1]).astype(BRAIN)
        r.xin[:HALO, dst] = (r.halo[:, src].astype(FLOAT) * hinv * gain[0:1]).astype(BRAIN)
        r.crel[:, dst] = r.cot[:, src]
        for k in range(5):
            r.mrel[k * rank : (k + 1) * rank, dst] = maps[k, :, src]
        r.grel[:, dst] = gain
    for name in ("trel", "xin", "crel"):
        r.leave(name)
    r.elow[...] = dot(r.xin[...], r.mrel[0:rank], NT).astype(BRAIN)
    r.ob[...] = dot(r.crel[...], r.mrel[4 * rank : 5 * rank], NT).astype(BRAIN)


def front_pack_body(r):
    half = r.unit.shape[1]
    rows = pl.ds(pl.multiple_of(r.core[0] * half, half), half)
    r.need("entry")
    for k in range(3):
        r.unit[k] = r.entry[k, rows, :]
    r.need("mixer")
    r.unit[3] = r.mixer[:, rows].astype(FLOAT).T.astype(BRAIN)


def feed_pack_body(count, r):
    units = [getattr(r, f"unit{q}") for q in range(count)]
    half = units[0].shape[1]
    rows = pl.ds(pl.multiple_of(r.core[0] * half, half), half)
    r.need("gates", "outlet")
    first = 0
    for q, unit in enumerate(units):
        cols = slice(first, first + unit.shape[2])
        for k in range(2):
            unit[k] = r.gates[k, rows, cols]
        unit[2] = r.outlet[cols, rows].astype(FLOAT).T.astype(BRAIN)
        r.leave(f"unit{q}")
        first += unit.shape[2]


def half_kernel(core, came, half, held, sems):
    count = half.shape[0]
    first = core[0] * count
    ins = [pltpu.make_async_copy(came.at[first + z], held.at[z], sems.at[0, z]) for z in range(count)]
    outs = [pltpu.make_async_copy(held.at[z], half.at[z], sems.at[1, z]) for z in range(count)]
    for copy in ins:
        copy.start()
    for z in range(count):
        ins[z].wait()
        outs[z].start()
    for copy in outs:
        copy.wait()


def local_body(r):
    whole, sems = r.scratch
    chan = r.taps.shape[1]
    units = r.orr.shape[2]
    a = r.pick[0]
    first = 5 * chan
    rank, half = r.out.shape
    copies = [
        pltpu.make_async_copy(source, whole.at[:, pl.ds(at, size)], sems.at[k])
        for k, (source, at, size) in enumerate(
            (
                (r.mr.at[a], 3 * chan, chan),
                (r.ge.at[0, a], first, units),
                (r.ge.at[1, a], first + units, units),
                (r.orr.at[a], first + 2 * units, units),
            )
        )
    ]
    for copy in copies:
        copy.start()
    r.need("ee", "taps")
    whole[:, : 3 * chan] = r.ee[...]
    whole[:, 4 * chan : 5 * chan] = jnp.zeros((rank, chan), BRAIN)
    whole[0:3, 4 * chan : 5 * chan] = r.taps[...]
    whole[:, first + 3 * units :] = jnp.zeros((rank, whole.shape[1] - first - 3 * units), BRAIN)
    for copy in copies:
        copy.wait()
    r.out[...] = whole[:, pl.ds(pl.multiple_of(r.core[0] * half, LANES), half)]


def maps_body(chan, units, subs, r):
    [side] = r.scratch
    front = r.front
    rank = front.shape[0] // 2
    half = r.mine.shape[1]
    count = r.mine.shape[0] // rank
    channels = chan * count
    r.need("mine", "theirs")
    side[:, pl.ds(pl.multiple_of(r.core[0] * half, LANES), half)] = r.mine[...]
    side[:, pl.ds(pl.multiple_of((1 - r.core[0]) * half, LANES), half)] = r.theirs[...]
    for s in range(count):
        own = slice(s * rank, (s + 1) * rank)
        z = r.pos[s]
        for k in range(4):
            at = pl.ds(pl.multiple_of(k * channels + z * chan, LANES), chan)
            front[0:rank, at] = side[own, k * chan : (k + 1) * chan]
        at = pl.ds(pl.multiple_of(z * chan, LANES), chan)
        front[rank : 2 * rank, at] = side[own, 4 * chan : 5 * chan]
        first = 5 * chan
        for q, sub in enumerate(subs):
            feed = getattr(r, f"feed{q}")
            for k in range(3):
                at = first + k * units
                to = pl.ds(pl.multiple_of(z * sub, LANES), sub)
                feed[k * rank : (k + 1) * rank, to] = side[own, at : at + sub]
            first += sub


def piece_names(count, front):
    return [f"front{p}" if front else f"feed{p}" for p in range(count)]


def fetch(r, count, labels, w, sems, planes, front=True):
    pieces = [getattr(r, name) for name in piece_names(len(labels), front)]
    width = pieces[0].shape[3]

    def copies(z):
        cols = pl.ds(pl.multiple_of(z * width, LANES), width)
        found = []
        for ref, label in zip(pieces, labels):
            for h in range(ref.shape[0] // count):
                size = ref.shape[2]
                place = label if isinstance(label, tuple) else (label + h * (size // LANES),)
                size //= len(place)
                for k, slot in enumerate(place):
                    if not isinstance(slot, int):
                        slot = slot(r.core[0])
                    source = ref.at[h * count + z, planes, pl.ds(k * size, size)]
                    target = pl.ds(pl.multiple_of(slot * LANES, LANES), size)
                    target = w.at[:, target, cols]
                    found.append(pltpu.make_async_copy(source, target, sems.at[z, len(found)]))
        return found

    for z in range(count):
        for copy in copies(z):
            copy.start()

    def wait(z):
        for copy in copies(z):
            copy.wait()

    def arrive(t, tile):
        need = lambda t: (t * tile + width - 1) // width
        lax.fori_loop(need(t), need(t + 1), lambda z, c: (wait(z), c)[1], 0)

    return arrive


def front_body(labels, tiles, r):
    w, sems, low = r.scratch
    rank = r.elow.shape[1]
    rows = r.trel.shape[0]
    channels = w.shape[2]
    width = channels // tiles
    arrive = fetch(r, sems.shape[0], labels, w, sems, slice(0, 4))
    r.begin("trel", "grel")
    r.need("mask", "xin", "elow", "emap", "mrel")
    r.middle[...] = jnp.zeros_like(r.middle)
    low[...] = jnp.zeros_like(low)

    def step(t, carry):
        arrive(t, width)
        col = pl.ds(pl.multiple_of(t * width, LANES), width)
        wide = lambda k: pl.ds(pl.multiple_of(k * channels + t * width, LANES), width)
        project = lambda k: dot(r.xin[...], w[k, :, col]) + dot(
            r.elow[...], r.emap[0:rank, wide(k)]
        )
        b = project(0)
        v = project(2)
        c = project(1)[HALO:]
        product = b * v
        r.gb[:, col] = b[HALO:].astype(BRAIN)
        r.va[:, col] = v[HALO:].astype(BRAIN)
        r.gc[:, col] = c.astype(BRAIN)
        taps = r.emap[rank : 2 * rank, col].astype(FLOAT)
        conv = (
            taps[0:1] * product[HALO:]
            + taps[1:2] * r.mask[0:rows, 0:1] * pltpu.roll(product, 1, 0)[HALO:]
            + taps[2:3] * r.mask[0:rows, 1:2] * pltpu.roll(product, 2, 0)[HALO:]
        )
        r.cv[:, col] = conv.astype(BRAIN)
        mix = (c * conv).astype(BRAIN)
        r.mixed[:, col] = mix
        for name in ("gb", "gc", "va", "cv", "mixed"):
            r.leave_tile(name, t, tiles)
        r.middle[...] += dot(mix, w[3, :, col], NT)
        low[...] += dot(mix, r.emap[0:rank, wide(3)], NT)
        return carry

    lax.fori_loop(0, tiles, step, 0)
    mlow = low[...].astype(BRAIN)
    r.mlow[...] = mlow
    r.need("trel", "grel")
    mid = r.middle[...] + r.trel[...].astype(FLOAT) + dot(mlow, r.mrel[3 * rank : 4 * rank])
    r.middle[...] = mid
    r.leave("middle")
    inv = lax.rsqrt(jnp.mean(mid * mid, axis=-1, keepdims=True) + EPSILON)
    x2 = (mid * inv * r.grel[1:2]).astype(BRAIN)
    r.second[...] = x2
    r.leave("second")
    r.glow[...] = dot(x2, r.mrel[rank : 3 * rank], NT).astype(BRAIN)


def feed_body(labels, tiles, sub, first, r):
    w, sems = r.scratch
    rank = r.ob.shape[1]
    width = w.shape[2] // tiles
    arrive = fetch(r, sems.shape[0], labels, w, sems, slice(0, 3), False)
    r.need("second", "crel", "glow", "ob", "emap")
    if first:
        r.out[...] = jnp.zeros_like(r.out)
        r.grad[...] = jnp.zeros_like(r.grad)
        r.small[...] = jnp.zeros_like(r.small)
    else:
        r.begin("small_in", "out_in", "grad_in", *r.extra)

    def step(t, carry):
        arrive(t, width)
        col = pl.ds(pl.multiple_of(t * width, LANES), width)
        eg, eu, ro = (r.emap[i * rank : (i + 1) * rank, col] for i in range(3))
        wg, wu, wo = (w[i, :, col] for i in range(3))
        x = r.second[...]
        lg, lu, ob = r.glow[:, 0:rank], r.glow[:, rank : 2 * rank], r.ob[...]
        g = dot(x, wg) + dot(lg, eg)
        u = dot(x, wu) + dot(lu, eu)
        h_grad = dot(r.crel[...], wo) + dot(ob, ro)
        sigma = 1.0 / (1.0 + jnp.exp(-g))
        act = g * sigma
        h = (act * u).astype(BRAIN)
        gg = (h_grad * u * (sigma * (1.0 + g * (1.0 - sigma)))).astype(BRAIN)
        ug = (h_grad * act).astype(BRAIN)
        if not first:
            pl.when(t == 0)(lambda: r.need("out_in", "grad_in", "small_in"))
        r.out[...] += dot(h, wo, NT)
        r.grad[...] += dot(gg, wg, NT) + dot(ug, wu, NT)
        r.small[:, 0:rank] += dot(gg, eg, NT)
        r.small[:, rank : 2 * rank] += dot(ug, eu, NT)
        r.small[:, 2 * rank : 3 * rank] += dot(h, ro, NT)
        changes = (dot(lg, gg, TN), dot(lu, ug, TN), dot(ob, h, TN))
        for j in range(0, width, LANES):
            at = t * width + j
            owner = at // sub
            for k in range(3):
                to = r.pos[owner] * (3 * sub) + k * sub + (at - owner * sub)
                to = pl.ds(pl.multiple_of(to, LANES), LANES)
                r.dmap[:, to] = changes[k][:, j : j + LANES].astype(r.dmap.dtype)
        return carry

    lax.fori_loop(0, tiles, step, 0)


def pulled(v, gain, grad):
    inv = lax.rsqrt(jnp.mean(v * v, axis=-1, keepdims=True) + EPSILON)
    scaled = grad * gain
    along = jnp.mean(v * scaled, axis=-1, keepdims=True)
    return inv * scaled - v * (inv * inv * inv * along)


def middle_body(labels, tiles, chan, parts, r):
    w, sems = r.scratch
    rank = r.mlow.shape[1]
    channels = w.shape[2]
    width = channels // tiles
    depth = w.shape[1]
    arrive = fetch(r, sems.shape[0], labels, w, sems, slice(3, 4))
    late = [f"part{q}" for q in range(parts)]
    r.begin("gc", "cv", "mixed", "out", "second", "mlow", *late)
    r.need("middle", "grad", "small", "crel", "mrel", "grel", "fmap")
    gback = r.small[:, 0 : 2 * rank].astype(BRAIN)
    olow = r.small[:, 2 * rank : 3 * rank].astype(BRAIN)
    mid = r.middle[...]
    sgrad = r.grad[...] + dot(gback, r.mrel[rank : 3 * rank])
    mg = r.crel[...].astype(FLOAT) + pulled(mid, r.grel[1:2], sgrad)
    r.mgrad[...] = mg
    r.leave("mgrad")
    mlo = mg.astype(BRAIN)
    r.second_low[...] = mlo
    r.back[...] = dot(mlo, r.mrel[3 * rank : 4 * rank], NT).astype(BRAIN)
    r.need("gc", "cv", "mixed", *late)
    mix = 0
    for name in late:
        part = getattr(r, name)
        r.pack[:, mix : mix + part.shape[1]] = part[...]
        mix += part.shape[1]

    def step(t, carry):
        arrive(t, width)
        col = pl.ds(pl.multiple_of(t * width, LANES), width)
        own = pl.ds(pl.multiple_of(3 * channels + t * width, LANES), width)
        mx = dot(r.second_low[...], w[0, :, col]) + dot(r.back[...], r.fmap[0:rank, own])
        r.gcg[:, col] = (mx * r.cv[:, col].astype(FLOAT)).astype(BRAIN)
        cg = mx * r.gc[:, col].astype(FLOAT)
        r.cgrad[:, col] = cg.astype(BRAIN)
        for name in ("gcg", "cgrad"):
            r.leave_tile(name, t, tiles)
        r.edge[:, col] = cg[:HALO].astype(BRAIN)
        change = dot(r.back[...], r.mixed[:, col], TN).astype(BRAIN)
        for j in range(0, width, LANES):
            at = t * width + j
            owner = at // chan
            to = mix + r.pos[owner] * chan + at - owner * chan
            r.pack[:, pl.ds(pl.multiple_of(to, LANES), LANES)] = change[:, j : j + LANES]
        return carry

    lax.fori_loop(0, tiles, step, 0)
    r.leave("edge")
    wide = mix + channels
    r.need("second", "mlow")
    dff = jnp.concatenate([dot(gback, r.second[...], TN), dot(olow, r.crel[...], TN)], axis=0)
    dff = jnp.concatenate([dff, dot(r.mlow[...], r.second_low[...], TN)], axis=0).astype(BRAIN)
    for b in range(depth // LANES):
        src = slice(b * LANES, (b + 1) * LANES)
        for k in range(4):
            to = pl.ds(pl.multiple_of(wide + k * depth + r.tab[b] * LANES, LANES), LANES)
            r.pack[:, to] = dff[k * rank : (k + 1) * rank, src]
    r.leave("pack")
    r.need("out")
    full = r.middle[...] + r.out[...] + dot(olow, r.mrel[4 * rank : 5 * rank])
    for b in range(depth // LANES):
        r.output[:, lanes(r.tab[b])] = full[:, b * LANES : (b + 1) * LANES].astype(BRAIN)


def last_body(feed, middle, parts, r):
    scratch = r.scratch
    r.out, r.grad, r.small = r.out_in, r.grad_in, r.small_in
    r.put(f"part{parts}", r.dmap)
    r.extra = [name for name in r.copies if name not in r.begun]
    r.scratch = scratch[:2]
    feed_body(*feed, r)
    r.scratch = scratch[2:]
    middle_body(*middle, r)


def back_body(labels, tiles, chan, r):
    w, sems, fgrad, back = r.scratch
    rank = r.elow.shape[1]
    rows = r.trel.shape[0]
    channels = w.shape[2]
    width = channels // tiles
    arrive = fetch(r, sems.shape[0], labels, w, sems, slice(0, 3))
    r.begin("mgrad", "trel", "grel", "xin")
    r.need("mask", "edge", "cgrad", "gcg", "gb", "va", "elow", "emap", "mrel")
    total = rows + HALO
    fgrad[...] = jnp.zeros_like(fgrad)
    back[...] = jnp.zeros_like(back)

    def step(t, carry):
        arrive(t, width)
        col = pl.ds(pl.multiple_of(t * width, LANES), width)
        taps = r.emap[rank : 2 * rank, col].astype(FLOAT)
        cg = jnp.concatenate([r.cgrad[:, col], r.edge[:, col]], axis=0).astype(FLOAT)
        pg = (
            taps[0:1] * cg
            + pltpu.roll(taps[1:2] * r.mask[:, 0:1] * cg, total - 1, 0)
            + pltpu.roll(taps[2:3] * r.mask[:, 1:2] * cg, total - 2, 0)
        )[:rows]
        parts = (
            (pg * r.va[:, col].astype(FLOAT)).astype(BRAIN),
            r.gcg[:, col],
            (pg * r.gb[:, col].astype(FLOAT)).astype(BRAIN),
        )
        for k in range(3):
            fgrad[...] += dot(parts[k], w[k, :, col], NT)
            wide = pl.ds(pl.multiple_of(k * channels + t * width, LANES), width)
            back[...] += dot(parts[k], r.emap[0:rank, wide], NT)
            change = dot(r.elow[HALO:, :], parts[k], TN).astype(BRAIN)
            for j in range(0, width, LANES):
                at = t * width + j
                owner = at // chan
                to = r.pos[owner] * 3 * chan + k * chan + at - owner * chan
                r.pack[:, pl.ds(pl.multiple_of(to, LANES), LANES)] = change[:, j : j + LANES]
        return carry

    lax.fori_loop(0, tiles, step, 0)
    low = back[...].astype(BRAIN)
    first = fgrad[...] + dot(low, r.mrel[0:rank])
    r.need("mgrad", "trel", "grel", "xin")
    dred = dot(low, r.xin[HALO:, :], TN).astype(BRAIN)
    for b in range(w.shape[1] // LANES):
        to = pl.ds(pl.multiple_of(3 * channels + r.tab[b] * LANES, LANES), LANES)
        r.pack[:, to] = dred[:, b * LANES : (b + 1) * LANES]
    r.leave("pack")
    full = r.mgrad[...] + pulled(r.trel[...].astype(FLOAT), r.grel[0:1], first)
    for b in range(w.shape[1] // LANES):
        r.igrad[:, lanes(r.tab[b])] = full[:, b * LANES : (b + 1) * LANES].astype(BRAIN)


def shifted(block, distance):
    size = lax.axis_size(ALONG)
    return lax.ppermute(block, ALONG, [(i, (i + distance) % size) for i in range(size)])


def flipped(block, bit):
    return lax.ppermute(block, "dp", [(i, i ^ bit) for i in range(lax.axis_size("dp"))])


def swapped(block):
    return lax.ppermute(block, "ctx", [(0, 1), (1, 0)])


def turned(block, bits):
    route = [(2 * d + c, 2 * (d ^ bits[c]) + c) for d in range(lax.axis_size("dp")) for c in range(2)]
    return lax.ppermute(block, ("dp", "ctx"), route)


def passed_along(block, distance):
    axes = ("ctx", ALONG)
    size = lax.axis_size("ctx") * lax.axis_size(ALONG)
    route = [(i, i + distance) for i in range(size) if 0 <= i + distance < size]
    return lax.ppermute(block, axes, route)


def after(value, *others):
    return lax.optimization_barrier((value, others))[0]


def shape_of(chip, core):
    near = jnp.where(core == 0, 1, 2)
    places = [(0, 0), (0, 1), (near, 0), (near, 1), (3 - near, 0), (3 - near, 1)]
    places += [(3, core), (3, 1 - core)]
    return jnp.stack([(chip ^ e) * 2 + h for e, h in places]).astype(jnp.int32)


class Line:
    def __init__(self):
        self.held = []
        self.values = {}

    def wait(self, *names):
        for name in names:
            self.held.append(self.values[name])
        self.held = self.held[-4:]

    def hold(self, *values):
        self.held = (self.held + list(values))[-3:]

    def ready(self, value):
        return after(value, *self.held) if self.held else value

    def start(self, name, move, value):
        self.values[name] = move(self.ready(value))

    def __getitem__(self, name):
        return self.values[name]


class Block:
    def __init__(self, line, name, unit, early):
        self.line, self.name, self.unit, self.early = line, name, unit, early

    def at(self, step):
        return self.line[self.name + step]

    def go(self, *steps):
        for step in steps:
            self.line.start(self.name + step, *self.plan(step))

    def wait(self, *steps):
        self.line.wait(*(self.name + step for step in steps))

    def plan(self, step):
        if step == "p":
            return (lambda v: turned(v, (1, 2))), self.unit
        if step == "z" and self.early:
            base = jnp.concatenate([self.unit, self.at("p")], axis=1)
            return (lambda v: lax.all_gather(v, ALONG, axis=0)), base
        if step == "z":
            return (lambda v: lax.all_gather(v, ("ctx", ALONG), axis=0)), self.unit
        if step == "a":
            return (lambda v: turned(v, (2, 1))), self.at("z")
        if step == "c":
            return swapped, self.at("z")
        if step == "o":
            return (lambda v: turned(v, (1, 2))), self.at("z")
        if step == "d":
            came = self.at("o")
            shape = (came.shape[0] // 2,) + came.shape[1:]
            half = pl.pallas_call(
                half_kernel,
                out_shape=jax.ShapeDtypeStruct(shape, BRAIN),
                in_specs=[
                    pl.BlockSpec(memory_space=pltpu.SMEM),
                    pl.BlockSpec(memory_space=pltpu.HBM),
                ],
                out_specs=pl.BlockSpec(memory_space=pltpu.HBM),
                scratch_shapes=[
                    pltpu.VMEM(shape, BRAIN),
                    pltpu.SemaphoreType.DMA((2, shape[0])),
                ],
                cost_estimate=pl.CostEstimate(flops=1, bytes_accessed=1, transcendentals=0),
            )(self.line.ready(lax.axis_index("ctx")[None].astype(jnp.int32)), came)
            return (lambda v: turned(v, (2, 1))), half
        return swapped, self.at(step[1:])

    def pieces(self):
        if not self.early:
            return [self.at(n) for n in ("z", "o", "co", "d", "cd")], (0, 2, 4, 6, 7)
        labels = (
            (lambda c: c, lambda c: 2 + c),
            (lambda c: 4 + c, 6),
            (lambda c: 1 - c, lambda c: 5 - c),
            (lambda c: 3 - c, 7),
        )
        return [self.at(n) for n in ("z", "a", "c", "ca")], labels


def spread(update, adapter, slots, axis):
    layout = list(update.shape)
    layout.insert(axis, slots)
    slot = lax.broadcasted_iota(jnp.int32, layout, axis)
    return jnp.where(slot == adapter, jnp.expand_dims(update, axis), 0.0)


def rounded(value):
    return lax.reduce_precision(value, 8, 7).astype(BRAIN)


class Sum:
    def __init__(self, line, name, mine, widths, halved):
        self.line, self.name, self.mine, self.widths = line, name, mine, widths
        self.count = lax.axis_size(ALONG)
        self.halved = halved

    def half(self, value):
        if not self.halved:
            return value
        size = value.shape[0] // 2
        return lax.dynamic_slice_in_dim(value, lax.axis_index("ctx") * size, size, 0)

    def wait_down(self):
        self.line.wait(*(self.name + f"down{s}" for s in range(1, self.count)))

    def across(self):
        self.line.start(self.name + "across", swapped, self.mine)

    def down(self):
        pair = self.half(self.mine).astype(FLOAT)
        pair = pair + self.half(self.line[self.name + "across"]).astype(FLOAT)
        pair = rounded(pair)
        rest = pair[:, sum(self.widths) * self.count :]
        self.parts = []
        for s in range(self.count):
            first, part = 0, []
            for width in self.widths:
                part.append(pair[:, first + s * width : first + (s + 1) * width])
                first += width * self.count
            self.parts.append(jnp.concatenate(part + [rest], axis=1))
        for s in range(1, self.count):
            self.line.start(self.name + f"down{s}", lambda v, s=s: shifted(v, -s), self.parts[s])

    def out(self):
        terms = [self.parts[0]] + [self.line[self.name + f"down{s}"] for s in range(1, self.count)]
        stack = jnp.stack(terms)
        at = lax.axis_index(ALONG)
        self.total = sum(
            lax.dynamic_index_in_dim(stack, (k - at) % self.count, 0, keepdims=False).astype(FLOAT)
            for k in range(self.count)
        )
        self.total = rounded(self.total)
        for e in range(1, lax.axis_size("dp")):
            self.line.start(self.name + f"out{e}", lambda v, e=e: flipped(v, e), self.total)

    def result(self):
        here = lax.axis_index("dp")
        rows = [(here, self.total)]
        for e in range(1, lax.axis_size("dp")):
            rows.append((here ^ e, self.line[self.name + f"out{e}"]))
        if self.halved:
            size = self.total.shape[0]
            mine = jnp.concatenate([row for _, row in rows], axis=0)
            other = swapped(mine)
            low = lax.axis_index("ctx") == 0
            both = [
                jnp.concatenate([jnp.where(low, mine, other)[at], jnp.where(low, other, mine)[at]])
                for at in (slice(k * size, (k + 1) * size) for k in range(len(rows)))
            ]
            rows = [(s, row) for (s, _), row in zip(rows, both)]
        return [(s, row.astype(FLOAT)) for s, row in rows]


def plain_sum(mine, widths):
    count = lax.axis_size(ALONG)
    at = lax.axis_index(ALONG)
    mine = lax.psum(mine.astype(FLOAT), ("ctx", ALONG))
    first, parts = 0, []
    for width in widths:
        parts.append(lax.dynamic_slice_in_dim(mine, first + at * width, width, 1))
        first += width * count
    rows = lax.all_gather(jnp.concatenate([*parts, mine[:, first:]], axis=1), "dp", axis=0)
    return [(s, rows[s]) for s in range(lax.axis_size("dp"))]


def chosen(table, adapter, axis):
    return lax.dynamic_index_in_dim(table, adapter, axis, keepdims=False)


def chunk_widths(units):
    if units == 1152:
        return (512, 384, 256)
    return (units // 3,) * 3


def per_device(
    tokens,
    segments,
    adapter_of,
    cotangent,
    first_gain,
    second_gain,
    conv_taps,
    entry_weight,
    mixer_weight,
    gates_weight,
    outlet_weight,
    entry_reduce,
    entry_expand,
    mixer_reduce,
    mixer_expand,
    gates_reduce,
    gates_expand,
    outlet_reduce,
    outlet_expand,
):
    slots, rank, depth = entry_reduce.shape
    seqs, cores, count = (lax.axis_size(a) for a in ("dp", "ctx", ALONG))
    here, core, at = (lax.axis_index(a) for a in ("dp", "ctx", ALONG))
    rows = tokens.shape[1]
    blocks = depth // LANES
    chan = mixer_weight.shape[0]
    units = outlet_weight.shape[0]
    channels = chan * count
    subs = chunk_widths(units)
    firsts = [sum(subs[:q]) for q in range(len(subs))]
    quick = (
        seqs == 4
        and cores == 2
        and count == 4
        and depth == seqs * cores * LANES
        and all(sub % LANES == 0 for sub in subs)
    )
    line = Line()

    adapter = adapter_of[here]
    pick = adapter[None].astype(jnp.int32)
    own = core[None].astype(jnp.int32)
    expand = chosen(entry_expand, adapter, 0).reshape(rank, 3 * chan)

    if quick:
        half = depth // seqs // cores
        [front_unit] = call(
            front_pack_body,
            dict(core=own),
            dict(entry=entry_weight, mixer=mixer_weight),
            {},
            dict(unit=((4, half, chan), BRAIN)),
            [],
        )
        line.start("halo", lambda v: passed_along(v, 1), tokens[0, rows - HALO :])
        halo = line["halo"]
        e = Block(line, "e", front_unit, False)
        e.go("z")
        span = 5 * chan + 3 * units
        span = (span + 2 * LANES - 1) // (2 * LANES) * LANES
        [local] = call(
            local_body,
            dict(pick=pick, core=after(own, front_unit)),
            dict(ee=expand, taps=conv_taps),
            dict(mr=mixer_reduce, ge=gates_expand, orr=outlet_reduce),
            dict(out=((rank, span), BRAIN)),
            [pltpu.VMEM((rank, 2 * span), BRAIN), pltpu.SemaphoreType.DMA((4,))],
        )
        feed_units = call(
            functools.partial(feed_pack_body, len(subs)),
            dict(core=after(own, front_unit)),
            dict(gates=gates_weight, outlet=outlet_weight),
            {},
            {f"unit{q}": ((3, half, sub), BRAIN) for q, sub in enumerate(subs)},
            [],
        )
        tab = shape_of(here, core)
        pos = ((at - jnp.arange(count)) % count).astype(jnp.int32)
    else:
        halo = passed_along(tokens[0, rows - HALO :], 1)
        local = jnp.concatenate(
            [
                expand,
                chosen(mixer_reduce, adapter, 0),
                jnp.pad(conv_taps, ((0, rank - 3), (0, 0))),
                chosen(gates_expand, adapter, 1)[0],
                chosen(gates_expand, adapter, 1)[1],
                chosen(outlet_reduce, adapter, 0),
            ],
            axis=1,
        )

        def full(block, rows_axis, cols_axis):
            block = lax.all_gather(block, "dp", axis=rows_axis, tiled=True)
            return lax.all_gather(block, ALONG, axis=cols_axis, tiled=True)

        front = [
            jnp.concatenate(
                [full(entry_weight, 1, 2), full(mixer_weight, 1, 0).T[None]], axis=0
            )
        ]
        front = [front[0][None]]
        front_at = (0,)
        pos = jnp.arange(count, dtype=jnp.int32)
        whole = jnp.concatenate(
            [full(gates_weight, 1, 2), full(outlet_weight, 1, 0).T[None]], axis=0
        ).reshape(3, depth, count, units)
        feed = [
            ([whole[:, :, :, first : first + sub].reshape(1, 3, depth, count * sub)], (0,))
            for first, sub in zip(firsts, subs)
        ]
        tab = jnp.arange(blocks, dtype=jnp.int32)
        side = list(lax.all_gather(local, ALONG, axis=0))

        def columns(first, size):
            return jnp.concatenate([part[:, first : first + size] for part in side], axis=1)

        low = jnp.concatenate([columns(k * chan, chan) for k in range(4)], axis=1)
        taps = jnp.pad(columns(4 * chan, chan), ((0, 0), (0, 3 * channels)))
        front_map = jnp.concatenate([low, taps], axis=0)
        feed_maps = [
            jnp.concatenate([columns(5 * chan + k * units + first, sub) for k in range(3)], axis=0)
            for first, sub in zip(firsts, subs)
        ]

    index = core * count + at
    seg = jnp.concatenate(
        [jnp.full((2,), -1, jnp.int32), segments[0], jnp.full((HALO,), -2, jnp.int32)]
    )
    seg = lax.dynamic_slice_in_dim(seg, index * rows, rows + HALO + 2)
    mask = jnp.stack([seg[1:-1] == seg[2:], seg[:-2] == seg[2:]], axis=1).astype(FLOAT)
    gains = jnp.stack([first_gain, second_gain]).astype(FLOAT)

    wide = lambda dtype: ((rows, depth), dtype)
    inner = lambda dtype: ((rows, channels), dtype)
    small = lambda n: ((rows, n), BRAIN)
    dma = pltpu.SemaphoreType.DMA((count if quick else 1, blocks))
    numbered = lambda pieces, front=True: dict(zip(piece_names(len(pieces), front), pieces))

    def run_prep():
        return call(
            prep_body,
            dict(pick=pick, tab=tab),
            dict(tok=tokens[0], halo=halo, cot=cotangent[0], gains=gains),
            dict(er=entry_reduce, gr=gates_reduce, me=mixer_expand, oe=outlet_expand),
            dict(
                trel=wide(BRAIN),
                xin=((rows + HALO, depth), BRAIN),
                crel=wide(BRAIN),
                mrel=((5 * rank, depth), BRAIN),
                grel=(gains.shape, FLOAT),
                elow=((rows + HALO, rank), BRAIN),
                ob=small(rank),
            ),
            [pltpu.VMEM((5, rank, depth), BRAIN), pltpu.SemaphoreType.DMA((5,))],
        )

    def run_front(pieces, labels, mask):
        return call(
            functools.partial(front_body, labels, 2),
            {},
            dict(
                mask=mask, xin=xin, elow=elow, emap=front_map, mrel=mrel, trel=trel, grel=grel
            ),
            numbered(pieces),
            dict(
                gb=inner(BRAIN),
                gc=inner(BRAIN),
                va=inner(BRAIN),
                cv=inner(BRAIN),
                mixed=inner(BRAIN),
                mlow=small(rank),
                middle=wide(FLOAT),
                second=wide(BRAIN),
                glow=small(2 * rank),
            ),
            [pltpu.VMEM((4, depth, channels), BRAIN), dma, pltpu.VMEM((rows, rank), FLOAT)],
            late=("trel", "grel"),
        )

    def run_feed(q, pieces, labels, state, feed_map):
        width = count * subs[q]
        ins = dict(second=second, crel=crel, glow=glow, ob=ob, emap=feed_map)
        if state:
            ins.update(out_in=state[0], grad_in=state[1], small_in=state[2])
            outs = dict(out="out_in", grad="grad_in", small="small_in")
        else:
            outs = dict(out=wide(FLOAT), grad=wide(FLOAT), small=((rows, 3 * rank), FLOAT))
        *state, change = call(
            functools.partial(
                feed_body, labels, max(1, width // 512), subs[q] if quick else width, not state
            ),
            dict(pos=pos, core=own),
            ins,
            numbered(pieces, False),
            dict(outs, dmap=((rank, 3 * width), BRAIN)),
            [pltpu.VMEM((3, depth, width), BRAIN), dma],
            late=("out_in", "grad_in", "small_in"),
        )
        return state, change

    def run_middle(chunk=None):
        names = [f"part{q}" for q in range(len(changes))]
        total = 3 * units * count + channels + 4 * depth
        mids = dict(
            middle=middle,
            crel=crel,
            mrel=mrel,
            grel=grel,
            fmap=front_map,
            gc=gc,
            cv=cv,
            mixed=mixed,
            second=second,
            mlow=mlow,
            **dict(zip(names, changes)),
        )
        outs = dict(
            output=wide(BRAIN),
            mgrad=wide(FLOAT),
            cgrad=inner(BRAIN),
            edge=((HALO, channels), BRAIN),
            gcg=inner(BRAIN),
            pack=((rank, total), BRAIN),
        )
        held = dict(second_low=wide(BRAIN), back=small(rank))
        room = [pltpu.VMEM((1, depth, channels), BRAIN), dma]
        late = ("gc", "cv", "mixed", "out", "second", "mlow", *names)
        if chunk is None:
            body = functools.partial(middle_body, front_at, 2, chan, len(changes))
            ins = dict(mids, grad=state[1], small=state[2], out=state[0])
            raw = numbered(front)
        else:
            pieces, labels, feed_map = chunk
            width = count * subs[-1]
            body = functools.partial(
                last_body,
                (labels, max(1, width // 512), subs[-1], False),
                (front_at, 2, chan, len(subs)),
                len(subs) - 1,
            )
            ins = dict(second=second, crel=crel, glow=glow, ob=ob, emap=feed_map)
            late = [name for name in mids if name not in ins]
            ins |= dict(out_in=state[0], grad_in=state[1], small_in=state[2])
            late += [name for name in ins if name not in mids][-3:]
            ins |= mids
            raw = numbered(pieces, False) | numbered(front)
            held |= dict(dmap=((rank, 3 * width), BRAIN))
            room = [pltpu.VMEM((3, depth, width), BRAIN), dma, *room]
        return call(body, dict(tab=tab, pos=pos, core=own), ins, raw, outs, room, late, held)

    state, changes = (), []
    if quick:
        f = [Block(line, f"f{q}", unit, q > 0) for q, unit in enumerate(feed_units)]
        f[1].go("p")
        f[2].go("p")
        trel, xin, crel, mrel, grel, elow, ob = run_prep()
        line.hold(local, ob)
        f[0].go("z")
        for k in range(1, count):
            line.start(f"local{k}", lambda v, k=k: shifted(v, k), local)
        f[1].wait("p")
        f[2].wait("p")
        e.wait("z")
        e.go("o")
        f[1].go("z")
        line.wait("local1", "local2", "local3")
        mine = jnp.concatenate([local] + [line[f"local{k}"] for k in range(1, count)], axis=0)
        line.start("locals", swapped, mine)
        line.wait("locals")
        front_map, *feed_maps = call(
            functools.partial(maps_body, chan, units, subs),
            dict(core=own, pos=pos),
            dict(mine=mine, theirs=line["locals"]),
            {},
            dict(
                {"front": ((2 * rank, 4 * channels), BRAIN)},
                **{f"feed{q}": ((3 * rank, count * sub), BRAIN) for q, sub in enumerate(subs)},
            ),
            [pltpu.VMEM((count * rank, 2 * span), BRAIN)],
        )
        line.hold(front_map)
        e.wait("o")
        e.go("d", "co")
        f[2].go("z")
        e.wait("d")
        e.go("cd")
        f[0].wait("z")
        f[0].go("o")
        e.wait("co", "cd")
        front, front_at = e.pieces()
        gb, gc, va, cv, mixed, mlow, middle, second, glow = run_front(
            front, front_at, line.ready(mask)
        )
        line.hold(glow)
        f[0].wait("o")
        f[0].go("d", "co")
        f[0].wait("d")
        f[0].go("cd")
        f[1].wait("z")
        f[1].go("a", "c")
        f[0].wait("cd", "co")
        state, change = run_feed(0, *f[0].pieces(), state, line.ready(feed_maps[0]))
        changes.append(change)
        line.hold(change)
        f[1].wait("a")
        f[1].go("ca")
        f[2].wait("z")
        f[2].go("a", "c")
        f[1].wait("c", "ca")
        state, change = run_feed(1, *f[1].pieces(), state, line.ready(feed_maps[1]))
        changes.append(change)
        line.hold(change)
        f[2].wait("a")
        f[2].go("ca")
        f[2].wait("c", "ca")
        output, mgrad, cgrad, edge, gcg, pack = run_middle(
            (*f[2].pieces(), line.ready(feed_maps[2]))
        )
        line.hold(gcg)
    else:
        trel, xin, crel, mrel, grel, elow, ob = run_prep()
        gb, gc, va, cv, mixed, mlow, middle, second, glow = run_front(front, front_at, mask)
        for q, (pieces, labels) in enumerate(feed):
            state, change = run_feed(q, pieces, labels, state, feed_maps[q])
            change = change.reshape(rank, 3, count, subs[q]).swapaxes(1, 2)
            changes.append(change.reshape(rank, -1))

    if not quick:
        output, mgrad, cgrad, edge, gcg, pack = run_middle()

    def run_back(mask, edge):
        return call(
            functools.partial(back_body, front_at, 2, chan),
            dict(tab=tab, pos=pos),
            dict(
                mask=mask,
                edge=edge,
                cgrad=cgrad,
                gcg=gcg,
                gb=gb,
                va=va,
                elow=elow,
                emap=front_map,
                mrel=mrel,
                mgrad=mgrad,
                trel=trel,
                grel=grel,
                xin=xin,
            ),
            numbered(front),
            dict(igrad=wide(BRAIN), pack=((rank, 3 * channels + depth), BRAIN)),
            [
                pltpu.VMEM((3, depth, channels), BRAIN),
                dma,
                pltpu.VMEM((rows, depth), FLOAT),
                pltpu.VMEM((rows, rank), FLOAT),
            ],
            late=("mgrad", "trel", "grel", "xin"),
        )

    most_widths = [3 * sub for sub in subs] + [chan]

    if quick:
        line.start("edge", lambda v: passed_along(v, -1), edge)
        most = Sum(line, "most", pack, most_widths, True)
        most.across()
        line.wait("edge", "mostacross")
        most.down()
        in_grad, pack = run_back(line.ready(mask), line["edge"])
        line.hold(pack)
        last = Sum(line, "last", pack, [3 * chan], False)
        last.across()
        line.wait("lastacross")
        most.wait_down()
        last.down()
        most.out()
        last.wait_down()
        last.out()
        most_rows, last_rows = most.result(), last.result()
    else:
        in_grad, last_pack = run_back(mask, passed_along(edge, -1))
        most_rows = plain_sum(pack, most_widths)
        last_rows = plain_sum(last_pack, [3 * chan])

    def placed(pick, found, axis):
        return sum(spread(pick(row), adapter_of[s], slots, axis) for s, row in found)

    def feed_part(row, k):
        return jnp.concatenate(
            [row[:, 3 * first + k * sub : 3 * first + (k + 1) * sub] for first, sub in zip(firsts, subs)],
            axis=1,
        )

    base = 3 * units + chan

    def wide_part(row, k):
        return row[:, base + k * depth : base + (k + 1) * depth]

    return (
        output[None],
        in_grad[None],
        placed(lambda row: row[:, 3 * chan :], last_rows, 0),
        placed(lambda row: row[:, : 3 * chan].reshape(rank, 3, chan), last_rows, 0),
        placed(lambda row: row[:, 3 * units : base], most_rows, 0),
        placed(lambda row: wide_part(row, 3), most_rows, 0),
        placed(lambda row: jnp.stack([wide_part(row, 0), wide_part(row, 1)]), most_rows, 1),
        placed(lambda row: jnp.stack([feed_part(row, 0), feed_part(row, 1)]), most_rows, 1),
        placed(lambda row: feed_part(row, 2), most_rows, 0),
        placed(lambda row: wide_part(row, 2), most_rows, 0),
    )


def solution(mesh):
    return jax.shard_map(
        per_device,
        mesh=mesh,
        in_specs=(
            P("dp", ("ctx", ALONG), None),
            P("dp", None),
            P(),
            P("dp", ("ctx", ALONG), None),
            P(),
            P(),
            P(None, ALONG),
            P(None, "dp", ALONG),
            P(ALONG, "dp"),
            P(None, "dp", ALONG),
            P(ALONG, "dp"),
            P(),
            P(None, None, None, ALONG),
            P(None, None, ALONG),
            P(),
            P(),
            P(None, None, None, ALONG),
            P(None, None, ALONG),
            P(),
        ),
        out_specs=(
            P("dp", ("ctx", ALONG), None),
            P("dp", ("ctx", ALONG), None),
            P(),
            P(None, None, None, ALONG),
            P(None, None, ALONG),
            P(),
            P(),
            P(None, None, None, ALONG),
            P(None, None, ALONG),
            P(),
        ),
        check_vma=False,
    )
```

```python
import functools

import jax
import jax.numpy as jnp
from jax import lax
from jax.experimental import pallas as pl
from jax.experimental.pallas import tpu as pltpu
from jax.sharding import PartitionSpec as P

EPSILON = 1e-05
FLOAT = jnp.float32
BRAIN = jnp.bfloat16
HALO = 16
LANES = 128
ALONG = "tensor"
NN = ((1,), (0,))
NT = ((1,), (1,))
TN = ((0,), (0,))


def dot(a, b, dims=NN):
    return lax.dot_general(a, b, (dims, ((), ())), preferred_element_type=FLOAT)


def lanes(index):
    return pl.ds(pl.multiple_of(index * LANES, LANES), LANES)


class Held:
    def __init__(self):
        self.copies, self.begun, self.gone, self.extra = {}, set(), [], ()

    def put(self, name, ref):
        self.__dict__[name] = ref

    def begin(self, *names):
        for name in names:
            if name in self.copies and name not in self.begun:
                self.copies[name].start()
                self.begun.add(name)

    def need(self, *names):
        for name in names:
            if name in self.copies:
                self.copies.pop(name).wait()

    def leave(self, name):
        copy = pltpu.make_async_copy(
            getattr(self, name), self.targets[name], self.out_sems.at[len(self.gone)]
        )
        copy.start()
        self.gone.append((name, copy.wait))

    def leave_tile(self, name, tile, tiles):
        ref, target, first = getattr(self, name), self.targets[name], len(self.gone)
        width = ref.shape[1] // tiles

        def copy(t):
            cols = pl.ds(t * width, width)
            if not isinstance(t, int):
                cols = pl.ds(pl.multiple_of(t * width, LANES), width)
            return pltpu.make_async_copy(
                ref.at[:, cols], target.at[:, cols], self.out_sems.at[first + t]
            )

        copy(tile).start()
        self.gone += [(name, lambda t=t: copy(t).wait()) for t in range(tiles)]


def call(body, scalars, ins, raw, outs, scratch, late=(), inner={}):
    forms = {n: o if isinstance(o, tuple) else (ins[o].shape, ins[o].dtype) for n, o in outs.items()}
    fresh = [n for n, o in outs.items() if isinstance(o, tuple)]
    raw_names = list(raw)

    def kernel(*refs):
        refs = list(refs)
        take = lambda count: [refs.pop(0) for _ in range(count)]
        r = Held()
        for name, ref in zip(scalars, take(len(scalars))):
            setattr(r, name, ref)
        sources = dict(zip(ins, take(len(ins))))
        for name, ref in zip(raw_names, take(len(raw_names))):
            setattr(r, name, ref)
        r.targets = dict(zip(outs, take(len(outs))))
        for name, ref in zip(ins, take(len(ins))):
            setattr(r, name, ref)
        for name, ref in zip(fresh + list(inner), take(len(fresh) + len(inner))):
            setattr(r, name, ref)
        for name, origin in outs.items():
            if not isinstance(origin, tuple):
                setattr(r, name, getattr(r, origin))
        in_sems, r.out_sems = take(2)
        r.scratch = refs
        for k, (name, source) in enumerate(sources.items()):
            r.copies[name] = pltpu.make_async_copy(source, getattr(r, name), in_sems.at[k])
            if name not in late:
                r.begin(name)
        body(r)
        for name in outs:
            if name not in [n for n, _ in r.gone]:
                r.leave(name)
        for _, wait in r.gone:
            wait()
        r.need(*list(r.copies))

    hbm = pl.BlockSpec(memory_space=pltpu.HBM)
    return pl.pallas_call(
        kernel,
        out_shape=[jax.ShapeDtypeStruct(*form) for form in forms.values()],
        in_specs=[pl.BlockSpec(memory_space=pltpu.SMEM)] * len(scalars)
        + [hbm] * (len(ins) + len(raw)),
        out_specs=[hbm] * len(outs),
        scratch_shapes=[pltpu.VMEM(v.shape, v.dtype) for v in ins.values()]
        + [pltpu.VMEM(*forms[n]) for n in fresh]
        + [pltpu.VMEM(*form) for form in inner.values()]
        + [pltpu.SemaphoreType.DMA((max(1, len(ins)),)), pltpu.SemaphoreType.DMA((32,))]
        + list(scratch),
        compiler_params=pltpu.CompilerParams(vmem_limit_bytes=54 << 20),
        cost_estimate=pl.CostEstimate(flops=1, bytes_accessed=1, transcendentals=0),
    )(*scalars.values(), *ins.values(), *raw.values())


def prep_body(r):
    rank = r.elow.shape[1]
    a = r.pick[0]
    maps, sems = r.scratch
    sources = (r.er.at[a], r.gr.at[0, a], r.gr.at[1, a], r.me.at[a], r.oe.at[a])
    copies = [
        pltpu.make_async_copy(source, maps.at[k], sems.at[k]) for k, source in enumerate(sources)
    ]
    for copy in copies:
        copy.start()
    r.need("tok", "halo")
    t32 = r.tok[...].astype(FLOAT)
    inv = lax.rsqrt(jnp.mean(t32 * t32, axis=-1, keepdims=True) + EPSILON)
    h32 = r.halo[...].astype(FLOAT)
    hinv = lax.rsqrt(jnp.mean(h32 * h32, axis=-1, keepdims=True) + EPSILON)
    r.need("cot", "gains")
    for copy in copies:
        copy.wait()
    for b in range(r.tok.shape[1] // LANES):
        src = lanes(r.tab[b])
        dst = slice(b * LANES, (b + 1) * LANES)
        part = r.tok[:, src]
        gain = r.gains[:, src]
        r.trel[:, dst] = part
        r.xin[HALO:, dst] = (part.astype(FLOAT) * inv * gain[0:1]).astype(BRAIN)
        r.xin[:HALO, dst] = (r.halo[:, src].astype(FLOAT) * hinv * gain[0:1]).astype(BRAIN)
        r.crel[:, dst] = r.cot[:, src]
        for k in range(5):
            r.mrel[k * rank : (k + 1) * rank, dst] = maps[k, :, src]
        r.grel[:, dst] = gain
    for name in ("trel", "xin", "crel"):
        r.leave(name)
    r.elow[...] = dot(r.xin[...], r.mrel[0:rank], NT).astype(BRAIN)
    r.ob[...] = dot(r.crel[...], r.mrel[4 * rank : 5 * rank], NT).astype(BRAIN)


def front_pack_body(r):
    half = r.unit.shape[1]
    rows = pl.ds(pl.multiple_of(r.core[0] * half, half), half)
    r.need("entry")
    for k in range(3):
        r.unit[k] = r.entry[k, rows, :]
    r.need("mixer")
    r.unit[3] = r.mixer[:, rows].astype(FLOAT).T.astype(BRAIN)


def feed_pack_body(count, r):
    units = [getattr(r, f"unit{q}") for q in range(count)]
    half = units[0].shape[1]
    rows = pl.ds(pl.multiple_of(r.core[0] * half, half), half)
    r.need("gates", "outlet")
    first = 0
    for q, unit in enumerate(units):
        cols = slice(first, first + unit.shape[2])
        for k in range(2):
            unit[k] = r.gates[k, rows, cols]
        unit[2] = r.outlet[cols, rows].astype(FLOAT).T.astype(BRAIN)
        r.leave(f"unit{q}")
        first += unit.shape[2]


def half_kernel(core, came, half, held, sems):
    count = half.shape[0]
    first = core[0] * count
    ins = [pltpu.make_async_copy(came.at[first + z], held.at[z], sems.at[0, z]) for z in range(count)]
    outs = [pltpu.make_async_copy(held.at[z], half.at[z], sems.at[1, z]) for z in range(count)]
    for copy in ins:
        copy.start()
    for z in range(count):
        ins[z].wait()
        outs[z].start()
    for copy in outs:
        copy.wait()


def local_body(r):
    whole, sems = r.scratch
    chan = r.taps.shape[1]
    units = r.orr.shape[2]
    a = r.pick[0]
    first = 5 * chan
    rank, half = r.out.shape
    copies = [
        pltpu.make_async_copy(source, whole.at[:, pl.ds(at, size)], sems.at[k])
        for k, (source, at, size) in enumerate(
            (
                (r.mr.at[a], 3 * chan, chan),
                (r.ge.at[0, a], first, units),
                (r.ge.at[1, a], first + units, units),
                (r.orr.at[a], first + 2 * units, units),
            )
        )
    ]
    for copy in copies:
        copy.start()
    r.need("ee", "taps")
    whole[:, : 3 * chan] = r.ee[...]
    whole[:, 4 * chan : 5 * chan] = jnp.zeros((rank, chan), BRAIN)
    whole[0:3, 4 * chan : 5 * chan] = r.taps[...]
    whole[:, first + 3 * units :] = jnp.zeros((rank, whole.shape[1] - first - 3 * units), BRAIN)
    for copy in copies:
        copy.wait()
    r.out[...] = whole[:, pl.ds(pl.multiple_of(r.core[0] * half, LANES), half)]


def maps_body(chan, units, subs, r):
    [side] = r.scratch
    front = r.front
    rank = front.shape[0] // 2
    half = r.mine.shape[1]
    count = r.mine.shape[0] // rank
    channels = chan * count
    r.need("mine", "theirs")
    side[:, pl.ds(pl.multiple_of(r.core[0] * half, LANES), half)] = r.mine[...]
    side[:, pl.ds(pl.multiple_of((1 - r.core[0]) * half, LANES), half)] = r.theirs[...]
    for s in range(count):
        own = slice(s * rank, (s + 1) * rank)
        z = r.pos[s]
        for k in range(4):
            at = pl.ds(pl.multiple_of(k * channels + z * chan, LANES), chan)
            front[0:rank, at] = side[own, k * chan : (k + 1) * chan]
        at = pl.ds(pl.multiple_of(z * chan, LANES), chan)
        front[rank : 2 * rank, at] = side[own, 4 * chan : 5 * chan]
        first = 5 * chan
        for q, sub in enumerate(subs):
            feed = getattr(r, f"feed{q}")
            for k in range(3):
                at = first + k * units
                to = pl.ds(pl.multiple_of(z * sub, LANES), sub)
                feed[k * rank : (k + 1) * rank, to] = side[own, at : at + sub]
            first += sub


def piece_names(count, front):
    return [f"front{p}" if front else f"feed{p}" for p in range(count)]


def fetch(r, count, labels, w, sems, planes, front=True):
    pieces = [getattr(r, name) for name in piece_names(len(labels), front)]
    width = pieces[0].shape[3]

    def copies(z):
        cols = pl.ds(pl.multiple_of(z * width, LANES), width)
        found = []
        for ref, label in zip(pieces, labels):
            for h in range(ref.shape[0] // count):
                size = ref.shape[2]
                place = label if isinstance(label, tuple) else (label + h * (size // LANES),)
                size //= len(place)
                for k, slot in enumerate(place):
                    if not isinstance(slot, int):
                        slot = slot(r.core[0])
                    source = ref.at[h * count + z, planes, pl.ds(k * size, size)]
                    target = pl.ds(pl.multiple_of(slot * LANES, LANES), size)
                    target = w.at[:, target, cols]
                    found.append(pltpu.make_async_copy(source, target, sems.at[z, len(found)]))
        return found

    for z in range(count):
        for copy in copies(z):
            copy.start()

    def wait(z):
        for copy in copies(z):
            copy.wait()

    def arrive(t, tile):
        need = lambda t: (t * tile + width - 1) // width
        lax.fori_loop(need(t), need(t + 1), lambda z, c: (wait(z), c)[1], 0)

    return arrive


def front_body(labels, tiles, r):
    w, sems, low = r.scratch
    rank = r.elow.shape[1]
    rows = r.trel.shape[0]
    channels = w.shape[2]
    width = channels // tiles
    arrive = fetch(r, sems.shape[0], labels, w, sems, slice(0, 4))
    r.begin("trel", "grel")
    r.need("mask", "xin", "elow", "emap", "mrel")
    r.middle[...] = jnp.zeros_like(r.middle)
    low[...] = jnp.zeros_like(low)

    def step(t, carry):
        arrive(t, width)
        col = pl.ds(pl.multiple_of(t * width, LANES), width)
        wide = lambda k: pl.ds(pl.multiple_of(k * channels + t * width, LANES), width)
        project = lambda k: dot(r.xin[...], w[k, :, col]) + dot(
            r.elow[...], r.emap[0:rank, wide(k)]
        )
        b = project(0)
        v = project(2)
        c = project(1)[HALO:]
        product = b * v
        r.gb[:, col] = b[HALO:].astype(BRAIN)
        r.va[:, col] = v[HALO:].astype(BRAIN)
        r.gc[:, col] = c.astype(BRAIN)
        taps = r.emap[rank : 2 * rank, col].astype(FLOAT)
        conv = (
            taps[0:1] * product[HALO:]
            + taps[1:2] * r.mask[0:rows, 0:1] * pltpu.roll(product, 1, 0)[HALO:]
            + taps[2:3] * r.mask[0:rows, 1:2] * pltpu.roll(product, 2, 0)[HALO:]
        )
        r.cv[:, col] = conv.astype(BRAIN)
        mix = (c * conv).astype(BRAIN)
        r.mixed[:, col] = mix
        for name in ("gb", "gc", "va", "cv", "mixed"):
            r.leave_tile(name, t, tiles)
        r.middle[...] += dot(mix, w[3, :, col], NT)
        low[...] += dot(mix, r.emap[0:rank, wide(3)], NT)
        return carry

    lax.fori_loop(0, tiles, step, 0)
    mlow = low[...].astype(BRAIN)
    r.mlow[...] = mlow
    r.need("trel", "grel")
    mid = r.middle[...] + r.trel[...].astype(FLOAT) + dot(mlow, r.mrel[3 * rank : 4 * rank])
    r.middle[...] = mid
    r.leave("middle")
    inv = lax.rsqrt(jnp.mean(mid * mid, axis=-1, keepdims=True) + EPSILON)
    x2 = (mid * inv * r.grel[1:2]).astype(BRAIN)
    r.second[...] = x2
    r.leave("second")
    r.glow[...] = dot(x2, r.mrel[rank : 3 * rank], NT).astype(BRAIN)


def feed_body(labels, tiles, sub, first, r):
    w, sems = r.scratch
    rank = r.ob.shape[1]
    width = w.shape[2] // tiles
    arrive = fetch(r, sems.shape[0], labels, w, sems, slice(0, 3), False)
    r.need("second", "crel", "glow", "ob", "emap")
    if first:
        r.out[...] = jnp.zeros_like(r.out)
        r.grad[...] = jnp.zeros_like(r.grad)
        r.small[...] = jnp.zeros_like(r.small)
    else:
        r.begin("small_in", "out_in", "grad_in", *r.extra)

    def step(t, carry):
        arrive(t, width)
        col = pl.ds(pl.multiple_of(t * width, LANES), width)
        eg, eu, ro = (r.emap[i * rank : (i + 1) * rank, col] for i in range(3))
        wg, wu, wo = (w[i, :, col] for i in range(3))
        x = r.second[...]
        lg, lu, ob = r.glow[:, 0:rank], r.glow[:, rank : 2 * rank], r.ob[...]
        g = dot(x, wg) + dot(lg, eg)
        u = dot(x, wu) + dot(lu, eu)
        h_grad = dot(r.crel[...], wo) + dot(ob, ro)
        sigma = 1.0 / (1.0 + jnp.exp(-g))
        act = g * sigma
        h = (act * u).astype(BRAIN)
        gg = (h_grad * u * (sigma * (1.0 + g * (1.0 - sigma)))).astype(BRAIN)
        ug = (h_grad * act).astype(BRAIN)
        if not first:
            pl.when(t == 0)(lambda: r.need("out_in", "grad_in", "small_in"))
        r.out[...] += dot(h, wo, NT)
        r.grad[...] += dot(gg, wg, NT) + dot(ug, wu, NT)
        r.small[:, 0:rank] += dot(gg, eg, NT)
        r.small[:, rank : 2 * rank] += dot(ug, eu, NT)
        r.small[:, 2 * rank : 3 * rank] += dot(h, ro, NT)
        changes = (dot(lg, gg, TN), dot(lu, ug, TN), dot(ob, h, TN))
        for j in range(0, width, LANES):
            at = t * width + j
            owner = at // sub
            for k in range(3):
                to = r.pos[owner] * (3 * sub) + k * sub + (at - owner * sub)
                to = pl.ds(pl.multiple_of(to, LANES), LANES)
                r.dmap[:, to] = changes[k][:, j : j + LANES].astype(r.dmap.dtype)
        return carry

    lax.fori_loop(0, tiles, step, 0)


def pulled(v, gain, grad):
    inv = lax.rsqrt(jnp.mean(v * v, axis=-1, keepdims=True) + EPSILON)
    scaled = grad * gain
    along = jnp.mean(v * scaled, axis=-1, keepdims=True)
    return inv * scaled - v * (inv * inv * inv * along)


def middle_body(labels, tiles, chan, parts, r):
    w, sems = r.scratch
    rank = r.mlow.shape[1]
    channels = w.shape[2]
    width = channels // tiles
    depth = w.shape[1]
    arrive = fetch(r, sems.shape[0], labels, w, sems, slice(3, 4))
    late = [f"part{q}" for q in range(parts)]
    r.begin("gc", "cv", "mixed", "out", "second", "mlow", *late)
    r.need("middle", "grad", "small", "crel", "mrel", "grel", "fmap")
    gback = r.small[:, 0 : 2 * rank].astype(BRAIN)
    olow = r.small[:, 2 * rank : 3 * rank].astype(BRAIN)
    mid = r.middle[...]
    sgrad = r.grad[...] + dot(gback, r.mrel[rank : 3 * rank])
    mg = r.crel[...].astype(FLOAT) + pulled(mid, r.grel[1:2], sgrad)
    r.mgrad[...] = mg
    r.leave("mgrad")
    mlo = mg.astype(BRAIN)
    r.second_low[...] = mlo
    r.back[...] = dot(mlo, r.mrel[3 * rank : 4 * rank], NT).astype(BRAIN)
    r.need("gc", "cv", "mixed", *late)
    mix = 0
    for name in late:
        part = getattr(r, name)
        r.pack[:, mix : mix + part.shape[1]] = part[...]
        mix += part.shape[1]

    def step(t, carry):
        arrive(t, width)
        col = pl.ds(pl.multiple_of(t * width, LANES), width)
        own = pl.ds(pl.multiple_of(3 * channels + t * width, LANES), width)
        mx = dot(r.second_low[...], w[0, :, col]) + dot(r.back[...], r.fmap[0:rank, own])
        r.gcg[:, col] = (mx * r.cv[:, col].astype(FLOAT)).astype(BRAIN)
        cg = mx * r.gc[:, col].astype(FLOAT)
        r.cgrad[:, col] = cg.astype(BRAIN)
        for name in ("gcg", "cgrad"):
            r.leave_tile(name, t, tiles)
        r.edge[:, col] = cg[:HALO].astype(BRAIN)
        change = dot(r.back[...], r.mixed[:, col], TN).astype(BRAIN)
        for j in range(0, width, LANES):
            at = t * width + j
            owner = at // chan
            to = mix + r.pos[owner] * chan + at - owner * chan
            r.pack[:, pl.ds(pl.multiple_of(to, LANES), LANES)] = change[:, j : j + LANES]
        return carry

    lax.fori_loop(0, tiles, step, 0)
    r.leave("edge")
    wide = mix + channels
    r.need("second", "mlow")
    dff = jnp.concatenate([dot(gback, r.second[...], TN), dot(olow, r.crel[...], TN)], axis=0)
    dff = jnp.concatenate([dff, dot(r.mlow[...], r.second_low[...], TN)], axis=0).astype(BRAIN)
    for b in range(depth // LANES):
        src = slice(b * LANES, (b + 1) * LANES)
        for k in range(4):
            to = pl.ds(pl.multiple_of(wide + k * depth + r.tab[b] * LANES, LANES), LANES)
            r.pack[:, to] = dff[k * rank : (k + 1) * rank, src]
    r.leave("pack")
    r.need("out")
    full = r.middle[...] + r.out[...] + dot(olow, r.mrel[4 * rank : 5 * rank])
    for b in range(depth // LANES):
        r.output[:, lanes(r.tab[b])] = full[:, b * LANES : (b + 1) * LANES].astype(BRAIN)


def last_body(feed, middle, parts, r):
    scratch = r.scratch
    r.out, r.grad, r.small = r.out_in, r.grad_in, r.small_in
    r.put(f"part{parts}", r.dmap)
    r.extra = [name for name in r.copies if name not in r.begun]
    r.scratch = scratch[:2]
    feed_body(*feed, r)
    r.scratch = scratch[2:]
    middle_body(*middle, r)


def back_body(labels, tiles, chan, r):
    w, sems, fgrad, back = r.scratch
    rank = r.elow.shape[1]
    rows = r.trel.shape[0]
    channels = w.shape[2]
    width = channels // tiles
    arrive = fetch(r, sems.shape[0], labels, w, sems, slice(0, 3))
    r.begin("mgrad", "trel", "grel", "xin")
    r.need("mask", "edge", "cgrad", "gcg", "gb", "va", "elow", "emap", "mrel")
    total = rows + HALO
    fgrad[...] = jnp.zeros_like(fgrad)
    back[...] = jnp.zeros_like(back)

    def step(t, carry):
        arrive(t, width)
        col = pl.ds(pl.multiple_of(t * width, LANES), width)
        taps = r.emap[rank : 2 * rank, col].astype(FLOAT)
        cg = jnp.concatenate([r.cgrad[:, col], r.edge[:, col]], axis=0).astype(FLOAT)
        pg = (
            taps[0:1] * cg
            + pltpu.roll(taps[1:2] * r.mask[:, 0:1] * cg, total - 1, 0)
            + pltpu.roll(taps[2:3] * r.mask[:, 1:2] * cg, total - 2, 0)
        )[:rows]
        parts = (
            (pg * r.va[:, col].astype(FLOAT)).astype(BRAIN),
            r.gcg[:, col],
            (pg * r.gb[:, col].astype(FLOAT)).astype(BRAIN),
        )
        for k in range(3):
            fgrad[...] += dot(parts[k], w[k, :, col], NT)
            wide = pl.ds(pl.multiple_of(k * channels + t * width, LANES), width)
            back[...] += dot(parts[k], r.emap[0:rank, wide], NT)
            change = dot(r.elow[HALO:, :], parts[k], TN).astype(BRAIN)
            for j in range(0, width, LANES):
                at = t * width + j
                owner = at // chan
                to = r.pos[owner] * 3 * chan + k * chan + at - owner * chan
                r.pack[:, pl.ds(pl.multiple_of(to, LANES), LANES)] = change[:, j : j + LANES]
        return carry

    lax.fori_loop(0, tiles, step, 0)
    low = back[...].astype(BRAIN)
    first = fgrad[...] + dot(low, r.mrel[0:rank])
    r.need("mgrad", "trel", "grel", "xin")
    dred = dot(low, r.xin[HALO:, :], TN).astype(BRAIN)
    for b in range(w.shape[1] // LANES):
        to = pl.ds(pl.multiple_of(3 * channels + r.tab[b] * LANES, LANES), LANES)
        r.pack[:, to] = dred[:, b * LANES : (b + 1) * LANES]
    r.leave("pack")
    full = r.mgrad[...] + pulled(r.trel[...].astype(FLOAT), r.grel[0:1], first)
    for b in range(w.shape[1] // LANES):
        r.igrad[:, lanes(r.tab[b])] = full[:, b * LANES : (b + 1) * LANES].astype(BRAIN)


def shifted(block, distance):
    size = lax.axis_size(ALONG)
    return lax.ppermute(block, ALONG, [(i, (i + distance) % size) for i in range(size)])


def flipped(block, bit):
    return lax.ppermute(block, "dp", [(i, i ^ bit) for i in range(lax.axis_size("dp"))])


def swapped(block):
    return lax.ppermute(block, "ctx", [(0, 1), (1, 0)])


def turned(block, bits):
    route = [(2 * d + c, 2 * (d ^ bits[c]) + c) for d in range(lax.axis_size("dp")) for c in range(2)]
    return lax.ppermute(block, ("dp", "ctx"), route)


def passed_along(block, distance):
    axes = ("ctx", ALONG)
    size = lax.axis_size("ctx") * lax.axis_size(ALONG)
    route = [(i, i + distance) for i in range(size) if 0 <= i + distance < size]
    return lax.ppermute(block, axes, route)


def after(value, *others):
    return lax.optimization_barrier((value, others))[0]


def shape_of(chip, core):
    near = jnp.where(core == 0, 1, 2)
    places = [(0, 0), (0, 1), (near, 0), (near, 1), (3 - near, 0), (3 - near, 1)]
    places += [(3, core), (3, 1 - core)]
    return jnp.stack([(chip ^ e) * 2 + h for e, h in places]).astype(jnp.int32)


class Line:
    def __init__(self):
        self.held = []
        self.values = {}

    def wait(self, *names):
        for name in names:
            self.held.append(self.values[name])
        self.held = self.held[-4:]

    def hold(self, *values):
        self.held = (self.held + list(values))[-3:]

    def ready(self, value):
        return after(value, *self.held) if self.held else value

    def start(self, name, move, value):
        self.values[name] = move(self.ready(value))

    def __getitem__(self, name):
        return self.values[name]


class Block:
    def __init__(self, line, name, unit, early):
        self.line, self.name, self.unit, self.early = line, name, unit, early

    def at(self, step):
        return self.line[self.name + step]

    def go(self, *steps):
        for step in steps:
            self.line.start(self.name + step, *self.plan(step))

    def wait(self, *steps):
        self.line.wait(*(self.name + step for step in steps))

    def plan(self, step):
        if step == "p":
            return (lambda v: turned(v, (1, 2))), self.unit
        if step == "z" and self.early:
            base = jnp.concatenate([self.unit, self.at("p")], axis=1)
            return (lambda v: lax.all_gather(v, ALONG, axis=0)), base
        if step == "z":
            return (lambda v: lax.all_gather(v, ("ctx", ALONG), axis=0)), self.unit
        if step == "a":
            return (lambda v: turned(v, (2, 1))), self.at("z")
        if step == "c":
            return swapped, self.at("z")
        if step == "o":
            return (lambda v: turned(v, (1, 2))), self.at("z")
        if step == "d":
            came = self.at("o")
            shape = (came.shape[0] // 2,) + came.shape[1:]
            half = pl.pallas_call(
                half_kernel,
                out_shape=jax.ShapeDtypeStruct(shape, BRAIN),
                in_specs=[
                    pl.BlockSpec(memory_space=pltpu.SMEM),
                    pl.BlockSpec(memory_space=pltpu.HBM),
                ],
                out_specs=pl.BlockSpec(memory_space=pltpu.HBM),
                scratch_shapes=[
                    pltpu.VMEM(shape, BRAIN),
                    pltpu.SemaphoreType.DMA((2, shape[0])),
                ],
                cost_estimate=pl.CostEstimate(flops=1, bytes_accessed=1, transcendentals=0),
            )(self.line.ready(lax.axis_index("ctx")[None].astype(jnp.int32)), came)
            return (lambda v: turned(v, (2, 1))), half
        return swapped, self.at(step[1:])

    def pieces(self):
        if not self.early:
            return [self.at(n) for n in ("z", "o", "co", "d", "cd")], (0, 2, 4, 6, 7)
        labels = (
            (lambda c: c, lambda c: 2 + c),
            (lambda c: 4 + c, 6),
            (lambda c: 1 - c, lambda c: 5 - c),
            (lambda c: 3 - c, 7),
        )
        return [self.at(n) for n in ("z", "a", "c", "ca")], labels


def spread(update, adapter, slots, axis):
    layout = list(update.shape)
    layout.insert(axis, slots)
    slot = lax.broadcasted_iota(jnp.int32, layout, axis)
    return jnp.where(slot == adapter, jnp.expand_dims(update, axis), 0.0)


def rounded(value):
    return lax.reduce_precision(value, 8, 7).astype(BRAIN)


class Sum:
    def __init__(self, line, name, mine, widths, halved):
        self.line, self.name, self.mine, self.widths = line, name, mine, widths
        self.count = lax.axis_size(ALONG)
        self.halved = halved

    def half(self, value):
        if not self.halved:
            return value
        size = value.shape[0] // 2
        return lax.dynamic_slice_in_dim(value, lax.axis_index("ctx") * size, size, 0)

    def wait_down(self):
        self.line.wait(*(self.name + f"down{s}" for s in range(1, self.count)))

    def across(self):
        self.line.start(self.name + "across", swapped, self.mine)

    def down(self):
        pair = self.half(self.mine).astype(FLOAT)
        pair = pair + self.half(self.line[self.name + "across"]).astype(FLOAT)
        pair = rounded(pair)
        rest = pair[:, sum(self.widths) * self.count :]
        self.parts = []
        for s in range(self.count):
            first, part = 0, []
            for width in self.widths:
                part.append(pair[:, first + s * width : first + (s + 1) * width])
                first += width * self.count
            self.parts.append(jnp.concatenate(part + [rest], axis=1))
        for s in range(1, self.count):
            self.line.start(self.name + f"down{s}", lambda v, s=s: shifted(v, -s), self.parts[s])

    def out(self):
        terms = [self.parts[0]] + [self.line[self.name + f"down{s}"] for s in range(1, self.count)]
        stack = jnp.stack(terms)
        at = lax.axis_index(ALONG)
        self.total = sum(
            lax.dynamic_index_in_dim(stack, (k - at) % self.count, 0, keepdims=False).astype(FLOAT)
            for k in range(self.count)
        )
        self.total = rounded(self.total)
        for e in range(1, lax.axis_size("dp")):
            self.line.start(self.name + f"out{e}", lambda v, e=e: flipped(v, e), self.total)

    def result(self):
        here = lax.axis_index("dp")
        rows = [(here, self.total)]
        for e in range(1, lax.axis_size("dp")):
            rows.append((here ^ e, self.line[self.name + f"out{e}"]))
        if self.halved:
            size = self.total.shape[0]
            mine = jnp.concatenate([row for _, row in rows], axis=0)
            other = swapped(mine)
            low = lax.axis_index("ctx") == 0
            both = [
                jnp.concatenate([jnp.where(low, mine, other)[at], jnp.where(low, other, mine)[at]])
                for at in (slice(k * size, (k + 1) * size) for k in range(len(rows)))
            ]
            rows = [(s, row) for (s, _), row in zip(rows, both)]
        return [(s, row.astype(FLOAT)) for s, row in rows]


def plain_sum(mine, widths):
    count = lax.axis_size(ALONG)
    at = lax.axis_index(ALONG)
    mine = lax.psum(mine.astype(FLOAT), ("ctx", ALONG))
    first, parts = 0, []
    for width in widths:
        parts.append(lax.dynamic_slice_in_dim(mine, first + at * width, width, 1))
        first += width * count
    rows = lax.all_gather(jnp.concatenate([*parts, mine[:, first:]], axis=1), "dp", axis=0)
    return [(s, rows[s]) for s in range(lax.axis_size("dp"))]


def chosen(table, adapter, axis):
    return lax.dynamic_index_in_dim(table, adapter, axis, keepdims=False)


def chunk_widths(units):
    if units == 1152:
        return (640, 256, 256)
    return (units // 3,) * 3


def per_device(
    tokens,
    segments,
    adapter_of,
    cotangent,
    first_gain,
    second_gain,
    conv_taps,
    entry_weight,
    mixer_weight,
    gates_weight,
    outlet_weight,
    entry_reduce,
    entry_expand,
    mixer_reduce,
    mixer_expand,
    gates_reduce,
    gates_expand,
    outlet_reduce,
    outlet_expand,
):
    slots, rank, depth = entry_reduce.shape
    seqs, cores, count = (lax.axis_size(a) for a in ("dp", "ctx", ALONG))
    here, core, at = (lax.axis_index(a) for a in ("dp", "ctx", ALONG))
    rows = tokens.shape[1]
    blocks = depth // LANES
    chan = mixer_weight.shape[0]
    units = outlet_weight.shape[0]
    channels = chan * count
    subs = chunk_widths(units)
    firsts = [sum(subs[:q]) for q in range(len(subs))]
    quick = (
        seqs == 4
        and cores == 2
        and count == 4
        and depth == seqs * cores * LANES
        and all(sub % LANES == 0 for sub in subs)
    )
    line = Line()

    adapter = adapter_of[here]
    pick = adapter[None].astype(jnp.int32)
    own = core[None].astype(jnp.int32)
    expand = chosen(entry_expand, adapter, 0).reshape(rank, 3 * chan)

    if quick:
        half = depth // seqs // cores
        [front_unit] = call(
            front_pack_body,
            dict(core=own),
            dict(entry=entry_weight, mixer=mixer_weight),
            {},
            dict(unit=((4, half, chan), BRAIN)),
            [],
        )
        line.start("halo", lambda v: passed_along(v, 1), tokens[0, rows - HALO :])
        halo = line["halo"]
        e = Block(line, "e", front_unit, False)
        e.go("z")
        span = 5 * chan + 3 * units
        span = (span + 2 * LANES - 1) // (2 * LANES) * LANES
        [local] = call(
            local_body,
            dict(pick=pick, core=after(own, front_unit)),
            dict(ee=expand, taps=conv_taps),
            dict(mr=mixer_reduce, ge=gates_expand, orr=outlet_reduce),
            dict(out=((rank, span), BRAIN)),
            [pltpu.VMEM((rank, 2 * span), BRAIN), pltpu.SemaphoreType.DMA((4,))],
        )
        feed_units = call(
            functools.partial(feed_pack_body, len(subs)),
            dict(core=after(own, front_unit)),
            dict(gates=gates_weight, outlet=outlet_weight),
            {},
            {f"unit{q}": ((3, half, sub), BRAIN) for q, sub in enumerate(subs)},
            [],
        )
        tab = shape_of(here, core)
        pos = ((at - jnp.arange(count)) % count).astype(jnp.int32)
    else:
        halo = passed_along(tokens[0, rows - HALO :], 1)
        local = jnp.concatenate(
            [
                expand,
                chosen(mixer_reduce, adapter, 0),
                jnp.pad(conv_taps, ((0, rank - 3), (0, 0))),
                chosen(gates_expand, adapter, 1)[0],
                chosen(gates_expand, adapter, 1)[1],
                chosen(outlet_reduce, adapter, 0),
            ],
            axis=1,
        )

        def full(block, rows_axis, cols_axis):
            block = lax.all_gather(block, "dp", axis=rows_axis, tiled=True)
            return lax.all_gather(block, ALONG, axis=cols_axis, tiled=True)

        front = [
            jnp.concatenate(
                [full(entry_weight, 1, 2), full(mixer_weight, 1, 0).T[None]], axis=0
            )
        ]
        front = [front[0][None]]
        front_at = (0,)
        pos = jnp.arange(count, dtype=jnp.int32)
        whole = jnp.concatenate(
            [full(gates_weight, 1, 2), full(outlet_weight, 1, 0).T[None]], axis=0
        ).reshape(3, depth, count, units)
        feed = [
            ([whole[:, :, :, first : first + sub].reshape(1, 3, depth, count * sub)], (0,))
            for first, sub in zip(firsts, subs)
        ]
        tab = jnp.arange(blocks, dtype=jnp.int32)
        side = list(lax.all_gather(local, ALONG, axis=0))

        def columns(first, size):
            return jnp.concatenate([part[:, first : first + size] for part in side], axis=1)

        low = jnp.concatenate([columns(k * chan, chan) for k in range(4)], axis=1)
        taps = jnp.pad(columns(4 * chan, chan), ((0, 0), (0, 3 * channels)))
        front_map = jnp.concatenate([low, taps], axis=0)
        feed_maps = [
            jnp.concatenate([columns(5 * chan + k * units + first, sub) for k in range(3)], axis=0)
            for first, sub in zip(firsts, subs)
        ]

    index = core * count + at
    seg = jnp.concatenate(
        [jnp.full((2,), -1, jnp.int32), segments[0], jnp.full((HALO,), -2, jnp.int32)]
    )
    seg = lax.dynamic_slice_in_dim(seg, index * rows, rows + HALO + 2)
    mask = jnp.stack([seg[1:-1] == seg[2:], seg[:-2] == seg[2:]], axis=1).astype(FLOAT)
    gains = jnp.stack([first_gain, second_gain]).astype(FLOAT)

    wide = lambda dtype: ((rows, depth), dtype)
    inner = lambda dtype: ((rows, channels), dtype)
    small = lambda n: ((rows, n), BRAIN)
    dma = pltpu.SemaphoreType.DMA((count if quick else 1, blocks))
    numbered = lambda pieces, front=True: dict(zip(piece_names(len(pieces), front), pieces))

    def run_prep():
        return call(
            prep_body,
            dict(pick=pick, tab=tab),
            dict(tok=tokens[0], halo=halo, cot=cotangent[0], gains=gains),
            dict(er=entry_reduce, gr=gates_reduce, me=mixer_expand, oe=outlet_expand),
            dict(
                trel=wide(BRAIN),
                xin=((rows + HALO, depth), BRAIN),
                crel=wide(BRAIN),
                mrel=((5 * rank, depth), BRAIN),
                grel=(gains.shape, FLOAT),
                elow=((rows + HALO, rank), BRAIN),
                ob=small(rank),
            ),
            [pltpu.VMEM((5, rank, depth), BRAIN), pltpu.SemaphoreType.DMA((5,))],
        )

    def run_front(pieces, labels, mask):
        return call(
            functools.partial(front_body, labels, 2),
            {},
            dict(
                mask=mask, xin=xin, elow=elow, emap=front_map, mrel=mrel, trel=trel, grel=grel
            ),
            numbered(pieces),
            dict(
                gb=inner(BRAIN),
                gc=inner(BRAIN),
                va=inner(BRAIN),
                cv=inner(BRAIN),
                mixed=inner(BRAIN),
                mlow=small(rank),
                middle=wide(FLOAT),
                second=wide(BRAIN),
                glow=small(2 * rank),
            ),
            [pltpu.VMEM((4, depth, channels), BRAIN), dma, pltpu.VMEM((rows, rank), FLOAT)],
            late=("trel", "grel"),
        )

    def run_feed(q, pieces, labels, state, feed_map):
        width = count * subs[q]
        ins = dict(second=second, crel=crel, glow=glow, ob=ob, emap=feed_map)
        if state:
            ins.update(out_in=state[0], grad_in=state[1], small_in=state[2])
            outs = dict(out="out_in", grad="grad_in", small="small_in")
        else:
            outs = dict(out=wide(FLOAT), grad=wide(FLOAT), small=((rows, 3 * rank), FLOAT))
        *state, change = call(
            functools.partial(
                feed_body, labels, max(1, width // 512), subs[q] if quick else width, not state
            ),
            dict(pos=pos, core=own),
            ins,
            numbered(pieces, False),
            dict(outs, dmap=((rank, 3 * width), BRAIN)),
            [pltpu.VMEM((3, depth, width), BRAIN), dma],
            late=("out_in", "grad_in", "small_in"),
        )
        return state, change

    def run_middle(chunk=None):
        names = [f"part{q}" for q in range(len(changes))]
        total = 3 * units * count + channels + 4 * depth
        mids = dict(
            middle=middle,
            crel=crel,
            mrel=mrel,
            grel=grel,
            fmap=front_map,
            gc=gc,
            cv=cv,
            mixed=mixed,
            second=second,
            mlow=mlow,
            **dict(zip(names, changes)),
        )
        outs = dict(
            output=wide(BRAIN),
            mgrad=wide(FLOAT),
            cgrad=inner(BRAIN),
            edge=((HALO, channels), BRAIN),
            gcg=inner(BRAIN),
            pack=((rank, total), BRAIN),
        )
        held = dict(second_low=wide(BRAIN), back=small(rank))
        room = [pltpu.VMEM((1, depth, channels), BRAIN), dma]
        late = ("gc", "cv", "mixed", "out", "second", "mlow", *names)
        if chunk is None:
            body = functools.partial(middle_body, front_at, 2, chan, len(changes))
            ins = dict(mids, grad=state[1], small=state[2], out=state[0])
            raw = numbered(front)
        else:
            pieces, labels, feed_map = chunk
            width = count * subs[-1]
            body = functools.partial(
                last_body,
                (labels, max(1, width // 512), subs[-1], False),
                (front_at, 2, chan, len(subs)),
                len(subs) - 1,
            )
            ins = dict(second=second, crel=crel, glow=glow, ob=ob, emap=feed_map)
            late = [name for name in mids if name not in ins]
            ins |= dict(out_in=state[0], grad_in=state[1], small_in=state[2])
            late += [name for name in ins if name not in mids][-3:]
            ins |= mids
            raw = numbered(pieces, False) | numbered(front)
            held |= dict(dmap=((rank, 3 * width), BRAIN))
            room = [pltpu.VMEM((3, depth, width), BRAIN), dma, *room]
        return call(body, dict(tab=tab, pos=pos, core=own), ins, raw, outs, room, late, held)

    state, changes = (), []
    if quick:
        f = [Block(line, f"f{q}", unit, q > 0) for q, unit in enumerate(feed_units)]
        f[1].go("p")
        f[2].go("p")
        trel, xin, crel, mrel, grel, elow, ob = run_prep()
        line.hold(local, ob)
        f[0].go("z")
        for k in range(1, count):
            line.start(f"local{k}", lambda v, k=k: shifted(v, k), local)
        f[1].wait("p")
        f[2].wait("p")
        e.wait("z")
        e.go("o")
        f[1].go("z")
        line.wait("local1", "local2", "local3")
        mine = jnp.concatenate([local] + [line[f"local{k}"] for k in range(1, count)], axis=0)
        line.start("locals", swapped, mine)
        line.wait("locals")
        front_map, *feed_maps = call(
            functools.partial(maps_body, chan, units, subs),
            dict(core=own, pos=pos),
            dict(mine=mine, theirs=line["locals"]),
            {},
            dict(
                {"front": ((2 * rank, 4 * channels), BRAIN)},
                **{f"feed{q}": ((3 * rank, count * sub), BRAIN) for q, sub in enumerate(subs)},
            ),
            [pltpu.VMEM((count * rank, 2 * span), BRAIN)],
        )
        line.hold(front_map)
        e.wait("o")
        e.go("d", "co")
        f[2].go("z")
        e.wait("d")
        e.go("cd")
        f[0].wait("z")
        f[0].go("o")
        e.wait("co", "cd")
        front, front_at = e.pieces()
        gb, gc, va, cv, mixed, mlow, middle, second, glow = run_front(
            front, front_at, line.ready(mask)
        )
        line.hold(glow)
        f[0].wait("o")
        f[0].go("d", "co")
        f[0].wait("d")
        f[0].go("cd")
        f[1].wait("z")
        f[1].go("a", "c")
        f[0].wait("cd", "co")
        state, change = run_feed(0, *f[0].pieces(), state, line.ready(feed_maps[0]))
        changes.append(change)
        line.hold(change)
        f[1].wait("a")
        f[1].go("ca")
        f[2].wait("z")
        f[2].go("a", "c")
        f[1].wait("c", "ca")
        state, change = run_feed(1, *f[1].pieces(), state, line.ready(feed_maps[1]))
        changes.append(change)
        line.hold(change)
        f[2].wait("a")
        f[2].go("ca")
        f[2].wait("c", "ca")
        output, mgrad, cgrad, edge, gcg, pack = run_middle(
            (*f[2].pieces(), line.ready(feed_maps[2]))
        )
        line.hold(gcg)
    else:
        trel, xin, crel, mrel, grel, elow, ob = run_prep()
        gb, gc, va, cv, mixed, mlow, middle, second, glow = run_front(front, front_at, mask)
        for q, (pieces, labels) in enumerate(feed):
            state, change = run_feed(q, pieces, labels, state, feed_maps[q])
            change = change.reshape(rank, 3, count, subs[q]).swapaxes(1, 2)
            changes.append(change.reshape(rank, -1))

    if not quick:
        output, mgrad, cgrad, edge, gcg, pack = run_middle()

    def run_back(mask, edge):
        return call(
            functools.partial(back_body, front_at, 2, chan),
            dict(tab=tab, pos=pos),
            dict(
                mask=mask,
                edge=edge,
                cgrad=cgrad,
                gcg=gcg,
                gb=gb,
                va=va,
                elow=elow,
                emap=front_map,
                mrel=mrel,
                mgrad=mgrad,
                trel=trel,
                grel=grel,
                xin=xin,
            ),
            numbered(front),
            dict(igrad=wide(BRAIN), pack=((rank, 3 * channels + depth), BRAIN)),
            [
                pltpu.VMEM((3, depth, channels), BRAIN),
                dma,
                pltpu.VMEM((rows, depth), FLOAT),
                pltpu.VMEM((rows, rank), FLOAT),
            ],
            late=("mgrad", "trel", "grel", "xin"),
        )

    most_widths = [3 * sub for sub in subs] + [chan]

    if quick:
        line.start("edge", lambda v: passed_along(v, -1), edge)
        most = Sum(line, "most", pack, most_widths, True)
        most.across()
        line.wait("edge", "mostacross")
        most.down()
        in_grad, pack = run_back(line.ready(mask), line["edge"])
        line.hold(pack)
        last = Sum(line, "last", pack, [3 * chan], False)
        last.across()
        line.wait("lastacross")
        most.wait_down()
        last.down()
        most.out()
        last.wait_down()
        last.out()
        most_rows, last_rows = most.result(), last.result()
    else:
        in_grad, last_pack = run_back(mask, passed_along(edge, -1))
        most_rows = plain_sum(pack, most_widths)
        last_rows = plain_sum(last_pack, [3 * chan])

    def placed(pick, found, axis):
        return sum(spread(pick(row), adapter_of[s], slots, axis) for s, row in found)

    def feed_part(row, k):
        return jnp.concatenate(
            [row[:, 3 * first + k * sub : 3 * first + (k + 1) * sub] for first, sub in zip(firsts, subs)],
            axis=1,
        )

    base = 3 * units + chan

    def wide_part(row, k):
        return row[:, base + k * depth : base + (k + 1) * depth]

    return (
        output[None],
        in_grad[None],
        placed(lambda row: row[:, 3 * chan :], last_rows, 0),
        placed(lambda row: row[:, : 3 * chan].reshape(rank, 3, chan), last_rows, 0),
        placed(lambda row: row[:, 3 * units : base], most_rows, 0),
        placed(lambda row: wide_part(row, 3), most_rows, 0),
        placed(lambda row: jnp.stack([wide_part(row, 0), wide_part(row, 1)]), most_rows, 1),
        placed(lambda row: jnp.stack([feed_part(row, 0), feed_part(row, 1)]), most_rows, 1),
        placed(lambda row: feed_part(row, 2), most_rows, 0),
        placed(lambda row: wide_part(row, 2), most_rows, 0),
    )


def solution(mesh):
    return jax.shard_map(
        per_device,
        mesh=mesh,
        in_specs=(
            P("dp", ("ctx", ALONG), None),
            P("dp", None),
            P(),
            P("dp", ("ctx", ALONG), None),
            P(),
            P(),
            P(None, ALONG),
            P(None, "dp", ALONG),
            P(ALONG, "dp"),
            P(None, "dp", ALONG),
            P(ALONG, "dp"),
            P(),
            P(None, None, None, ALONG),
            P(None, None, ALONG),
            P(),
            P(),
            P(None, None, None, ALONG),
            P(None, None, ALONG),
            P(),
        ),
        out_specs=(
            P("dp", ("ctx", ALONG), None),
            P("dp", ("ctx", ALONG), None),
            P(),
            P(None, None, None, ALONG),
            P(None, None, ALONG),
            P(),
            P(),
            P(None, None, None, ALONG),
            P(None, None, ALONG),
            P(),
        ),
        check_vma=False,
    )
```
